256 devices in a mesh: grp: 4 (over x), gx: 16 (over y_hi, z), gy: 4 (over y_lo, core).
Axes of the slice: x: 4, y: 4 (y_hi: 2, y_lo: 2; y = y_hi * 2 + y_lo), z: 8, core: 2. Of those that a mesh axis runs over, the one named last changes fastest.
Arguments:
- coarse_modes: float32 [4, 2, 8, 64, 4096], P('grp', None, None, 'gy', 'gx'), may hold values from -6 to 6
- salinity: float32 [32, 256, 16384], P('grp', 'gy', 'gx'), may hold values from -6 to 6
- viscosity: float32 [4], P('grp'), may hold values from 0.1 to 1
- forcing_gain: float32 [4], P('grp'), may hold values from 0.5 to 2
- diffusivity: float32 [32], P('grp'), may hold values from 0.3 to 1.5
Outputs:
- salinity_next: float32 [32, 256, 16384], P('grp', 'gy', 'gx')
- coarse_next: float32 [4, 2, 8, 64, 4096], P('grp', None, None, 'gy', 'gx')
The draws below stay inside these ranges and needn't reach their ends.
All inputs are finite; a program needn't handle non-finite values.
Results may differ from the reference program's by a relative error of at most 0.0003.
Values sent between devices are 32-bit elements; how exact they have to be, the bound alone decides.
No kernel may reach another device: no remote copies, remote signals or barrier semaphores. Data moves between devices by JAX's collectives and lax.ppermute only.
A program may use at most 128 MiB of HBM per device.

```python
import math
import jax
import jax.numpy as jnp
from jax import lax

FIELDS = 4
NV = 4096
RATIO = 4
LV = 8
NYC = 64
NZF = 32
NYF = 256
NXF = 16384


def shard_levels(own_key, dims, split, low, high):
    def one(dim, parts):
        draws = jax.random.uniform(jax.random.fold_in(jax.random.fold_in(own_key, 6), dim), (parts,), jnp.float32, low / len(split), high / len(split))
        return jnp.repeat(jnp.exp(draws), dims[dim] // parts).reshape((-1,) + (1,) * (len(dims) - dim - 1))

    gain = one(*split[0])
    for cut in split[1:]:
        gain = gain * one(*cut)
    return gain


def noise(stream_key, shape, scale, reach, shards=(), kind=jnp.bfloat16):
    entries = jax.random.normal(stream_key, shape, jnp.float32) * scale
    if len(shards) > 0:
        entries = shard_levels(stream_key, shape, shards, -0.22, 0.18) * entries
    return jnp.clip(entries, min=-reach, max=reach).astype(kind)


def setup_inputs(seed: int = 0) -> dict:
    splits = jax.random.split(jax.random.key(seed), 6)
    return {
        "coarse_modes": noise(splits[0], (FIELDS, 2, LV, NYC, NV), 1.0, 6.0, ((0, 4), (3, 4), (4, 16)), jnp.float32),
        "salinity": noise(splits[1], (NZF, NYF, NXF), 1.0, 6.0, ((0, 4), (1, 4), (2, 16)), jnp.float32),
        "viscosity": jnp.clip(jnp.exp(math.log(1.0) - 2.3025851 * jax.random.uniform(splits[2], (FIELDS,), jnp.float32) ** shard_levels(splits[2], (FIELDS,), ((0, 4),), -0.2, 0.2)), 0.1, 1.0),
        "forcing_gain": jnp.clip(0.5 + 1.5 * jax.random.uniform(splits[3], (FIELDS,), jnp.float32) ** shard_levels(splits[3], (FIELDS,), ((0, 4),), -0.2, 0.2), 0.5, 2.0),
        "diffusivity": jnp.clip(jnp.exp(math.log(1.5) - 1.60943787 * jax.random.uniform(splits[4], (NZF,), jnp.float32) ** shard_levels(splits[4], (NZF,), ((0, 4),), -0.2, 0.2)), 0.3, 1.5),
    }


fine_step = 0.1


def refine(coarse, dimension):
    extent = coarse.shape[dimension]
    pieces = []
    for sub_cell in range(RATIO):
        offset = (sub_cell + 0.5) / RATIO - 0.5
        beside = jnp.roll(coarse, -1 if offset > 0 else 1, axis=dimension)
        pieces.append((1.0 - abs(offset)) * coarse + abs(offset) * beside)
    stacked = jnp.stack(pieces, axis=dimension + 1)
    target = list(coarse.shape)
    target[dimension] = extent * RATIO
    return stacked.reshape(target)


def reference(coarse_modes, salinity, viscosity, forcing_gain, diffusivity):
    spectral = lax.complex(coarse_modes[:, 0], coarse_modes[:, 1])
    physical = jnp.real(jnp.fft.ifft(spectral, axis=-1, norm="ortho"))

    def update(fine_level):
        coarse_plane = lax.dynamic_index_in_dim(physical, fine_level // RATIO, 1, keepdims=False)
        velocity = refine(refine(coarse_plane, 1), 2)
        centre = lax.dynamic_index_in_dim(salinity, fine_level, 0, keepdims=False)
        upper_cells = lax.dynamic_index_in_dim(salinity, (fine_level + 1) % NZF, 0, keepdims=False)
        lower_cells = lax.dynamic_index_in_dim(salinity, (fine_level + NZF - 1) % NZF, 0, keepdims=False)
        east_cells = jnp.roll(centre, -1, axis=1)
        west_cells = jnp.roll(centre, 1, axis=1)
        north_cells = jnp.roll(centre, -1, axis=0)
        south_cells = jnp.roll(centre, 1, axis=0)
        diffuse_rate = lax.dynamic_index_in_dim(diffusivity, fine_level, 0, keepdims=False)
        spread = diffuse_rate * (east_cells + west_cells + north_cells + south_cells + upper_cells + lower_cells - 6.0 * centre)
        advection = velocity[0] * (east_cells - west_cells) * 0.5 + velocity[1] * (north_cells - south_cells) * 0.5 + velocity[2] * (upper_cells - lower_cells) * 0.5
        updated = centre + fine_step * (spread - advection)
        buoyancy = velocity[3] - updated
        restricted = buoyancy.reshape(NYC, RATIO, NV, RATIO).mean(axis=(1, 3))
        return updated, restricted

    salinity_next, restricted = lax.map(update, jnp.arange(NZF, dtype=jnp.int32))
    buoyancy = restricted.reshape(LV, RATIO, NYC, NV).mean(axis=1)
    spectrum = jnp.fft.fft(buoyancy, axis=-1, norm="ortho")
    spectral_parts = jnp.stack([jnp.real(spectrum), jnp.imag(spectrum)])
    mode_index = jnp.arange(NV, dtype=jnp.int32)
    wavenumber = jnp.where(mode_index < NV // 2, mode_index, mode_index - NV)
    scaled_wave = (2.0 * math.pi / NV) * wavenumber.astype(jnp.float32)
    damping = jnp.exp(-viscosity[:, None] * scaled_wave[None, :] * scaled_wave[None, :])
    coarse_next = damping[:, None, None, None, :] * coarse_modes + forcing_gain[:, None, None, None, None] * spectral_parts[None]
    return salinity_next, coarse_next
```

```python
import functools
import math

import jax
import jax.numpy as jnp
import numpy as np
from jax import lax
from jax.experimental import pallas as pl
from jax.experimental.pallas import tpu as pltpu
from jax.sharding import Mesh
from jax.sharding import PartitionSpec as P

GX = ("gx_0", "gx_1")
GRP_GX = ("grp", "gx_0", "gx_1")
F32 = jnp.float32
BF16 = jnp.bfloat16
G = 16
NV = 4096
W = 256
FINE = 1024
VMEM_LIMIT = 48 << 20


def split_table(table):
    table = np.asarray(table, np.float64)
    high = table.astype(np.float32).astype(jnp.bfloat16)
    low = (table - high.astype(np.float64)).astype(np.float32).astype(jnp.bfloat16)
    return high, low


@functools.cache
def tables():
    out = {}
    k = np.arange(W)
    angle = 2 * np.pi * (np.outer(k, k) % W) / W
    norm = NV ** -0.5
    out["inv"] = split_table(np.concatenate([np.cos(angle), -np.sin(angle)], 0) * norm)
    r = np.arange(G)
    angle = 2 * np.pi * np.outer(r, k) / NV
    twc = np.zeros((G, 8, 128), np.float32)
    tws = np.zeros((G, 8, 128), np.float32)
    twc[:, :2] = np.cos(angle).reshape(G, 2, 128)
    tws[:, :2] = np.sin(angle).reshape(G, 2, 128)
    out["tw"] = (twc, tws)
    lanes = 16 * (k % 16) + k // 16
    order = np.argsort(lanes)
    assert np.array_equal(order, 16 * (k % 16) + k // 16)
    full = np.zeros((W + 2, FINE))
    for n in range(FINE):
        c, s = divmod(n, 4)
        o = (s + 0.5) / 4 - 0.5
        full[c + 1, n] += 1 - abs(o)
        full[c + 1 + (1 if o > 0 else -1), n] += abs(o)
    out["ref"] = full[1:-1][order].astype(jnp.bfloat16)
    edge = np.zeros((2, 128, 256))
    filt = np.zeros((W + 2, W))
    for b in range(W):
        filt[b : b + 3, b] = (0.125, 0.75, 0.125)
    out["filt"] = filt[1:-1][order].astype(jnp.bfloat16)
    fedge = np.zeros((2, 128, 256))
    for q in range(2):
        edge[q, 2 * q, :128] = full[0, :128]
        edge[q, 2 * q + 1, 128:] = full[-1, -128:]
        fedge[q, 2 * q] = filt[0]
        fedge[q, 2 * q + 1] = filt[-1]
    out["edge"] = edge.astype(jnp.bfloat16)
    out["fedge"] = fedge.astype(jnp.bfloat16)
    ym = np.zeros((64, 32))
    yt = np.zeros((16, 32))
    place = lambda c: 16 if c < 0 else 17 if c > 15 else c
    for n in range(64):
        c, s = divmod(n, 4)
        o = (s + 0.5) / 4 - 0.5
        ym[n, c] += 1 - abs(o)
        ym[n, place(c + (1 if o > 0 else -1))] += abs(o)
    for c in range(16):
        yt[c, c] += 0.75
        yt[c, place(c - 1)] += 0.125
        yt[c, place(c + 1)] += 0.125
    out["ym"] = np.concatenate([ym, ym], 1).astype(jnp.bfloat16)
    out["yt"] = np.concatenate([yt, yt], 1).astype(jnp.bfloat16)
    cm = np.zeros((FINE, W))
    cm[np.arange(FINE), np.arange(FINE) // 4] = 1.0 / 4
    out["cm"] = cm.astype(jnp.bfloat16)
    rm = np.zeros((32, 128))
    rm[np.arange(128) // 4, np.arange(128)] = 1.0 / 16
    out["rm"] = np.concatenate([rm, rm], 1).astype(jnp.bfloat16)
    g = np.arange(G)
    angle = 2 * np.pi * np.outer(k, k) / NV
    out["fwd"] = (np.concatenate([np.cos(angle), -np.sin(angle)], 1) * norm).astype(np.float32)
    angle = 2 * np.pi * (np.outer(g, k) % G) / G
    out["comb"] = (np.cos(angle).astype(np.float32), np.sin(angle).astype(np.float32))
    return out


def halves(x):
    high = x.astype(BF16)
    low = (x - high.astype(F32)).astype(BF16)
    return high, low


def mm(a, b):
    return jnp.dot(a, b, preferred_element_type=F32)


def call(kernel, out_shape, **kw):
    return pl.pallas_call(
        kernel,
        out_shape=out_shape,
        compiler_params=pltpu.CompilerParams(vmem_limit_bytes=VMEM_LIMIT),
        **kw,
    )


def sds(*shape, dtype=F32):
    return jax.ShapeDtypeStruct(shape, dtype)


def iota(shape, dim):
    return lax.broadcasted_iota(jnp.int32, shape, dim)


def roll(x, shift, axis):
    return pltpu.roll(x, shift % x.shape[axis], axis)


def edges_kernel(me, modes_a, modes_b, south, north, west, east, low, high, chunk, up, down, zlow, zhigh):
    zlow[...] = low[0]
    zhigh[...] = high[0]
    for dst, rows, row, line in ((up, north, 7, 15), (down, south, 0, 0)):
        dst[0:16, :128] = modes_a[pl.ds(line, 16, stride=16), :]
        dst[0:16, 128:] = modes_b[pl.ds(line, 16, stride=16), :]
        face = rows[:, row, :]
        for j in range(4):
            dst[16 + 8 * j : 24 + 8 * j, :] = face[:, 256 * j : 256 * j + 256]
    zero = jnp.zeros((8, 128), F32)
    for r in range(G):
        chunk[r, 0:16, :] = modes_a[pl.ds(r, 16, stride=16), :]
        chunk[r, 16:32, :] = modes_b[pl.ds(r, 16, stride=16), :]
        chunk[r, 32:40, :] = zero
    row_id = iota((8, 128), 0)

    def column(block, lane):
        tile = zero
        for i in range(4):
            both = jnp.concatenate([block[2 * i], block[2 * i + 1]], 0).T
            line = jnp.broadcast_to(both[lane : lane + 1, :], (8, 128))
            tile = jnp.where(row_id == 4 + i, line, tile)
        return tile

    chunk[(me[0] + 1) % G, 32:40, :] = column(east, 127)
    chunk[(me[0] + G - 1) % G, 32:40, :] = column(west, 0)


def edges(me, modes, salinity):
    block = lambda shape, *index: pl.BlockSpec(shape, lambda i, m, index=index: index)
    return call(
        edges_kernel,
        (sds(G, 40, 128), sds(48, 256), sds(48, 256), sds(64, FINE), sds(64, FINE)),
        grid_spec=pltpu.PrefetchScalarGridSpec(
            num_scalar_prefetch=1,
            grid=(1,),
            in_specs=[
                block((256, 128), 0, 0),
                block((256, 128), 0, 1),
                block((8, 8, FINE), 0, 0, 0),
                block((8, 8, FINE), 0, 7, 0),
                block((8, 64, 128), 0, 0, 0),
                block((8, 64, 128), 0, 0, 7),
                block((1, 64, FINE), 0, 0, 0),
                block((1, 64, FINE), 7, 0, 0),
            ],
            out_specs=[
                block((G, 40, 128), 0, 0, 0),
                block((48, 256), 0, 0),
                block((48, 256), 0, 0),
                block((64, FINE), 0, 0),
                block((64, FINE), 0, 0),
            ],
        ),
        name="edges",
    )(me, modes, modes, *[salinity] * 6)


def tails_kernel(chunk, from_south, from_north, out):
    row_id = iota((8, 128), 0)
    for r in range(G):
        rows = from_south if r < 8 else from_north
        p = r % 8
        tile = chunk[r]
        parts = (rows[p : p + 1, :128], rows[p : p + 1, 128:], rows[8 + p : 9 + p, :128], rows[8 + p : 9 + p, 128:])
        for i, part in enumerate(parts):
            tile = jnp.where(row_id == i, jnp.broadcast_to(part, (8, 128)), tile)
        out[r] = tile


def tails(chunk, from_south, from_north):
    tail = pl.BlockSpec((G, 8, 128), lambda i: (0, 4, 0))
    lines = pl.BlockSpec((16, 256), lambda i: (0, 0))
    return call(
        tails_kernel,
        sds(G, 40, 128),
        grid=(1,),
        in_specs=[tail, lines, lines],
        out_specs=tail,
        input_output_aliases={0: 0},
        name="tails",
    )(chunk, from_south, from_north)


def cmul(a, b, c, s):
    return a * c - b * s, a * s + b * c


def four(z):
    (ar, ai), (br, bi), (cr, ci), (dr, di) = z
    t0r, t0i, t1r, t1i = ar + cr, ai + ci, ar - cr, ai - ci
    t2r, t2i, t3r, t3i = br + dr, bi + di, br - dr, bi - di
    return (
        (t0r + t2r, t0i + t2i),
        (t1r - t3i, t1i + t3r),
        (t0r - t2r, t0i - t2i),
        (t1r + t3i, t1i - t3r),
    )


def sixteen(z):
    inner = [four([z[4 * g1 + g0] for g1 in range(4)]) for g0 in range(4)]
    out = [None] * 16
    for r0 in range(4):
        column = []
        for g0 in range(4):
            angle = 2 * math.pi * g0 * r0 / 16
            a, b = inner[g0][r0]
            column.append((a, b) if g0 * r0 == 0 else cmul(a, b, math.cos(angle), math.sin(angle)))
        for r1, value in enumerate(four(column)):
            out[4 * r1 + r0] = value
    return out


def inverse_kernel(recv, twc, tws, inv_high, inv_low, send, left_high, left_low, mid):
    row_id = iota((8, 128), 0)
    lane_id = iota((8, 128), 1)

    def put(r, top, part, value):
        high, low = halves(value)
        left_high[16 * r + 8 * top : 16 * r + 8 * top + 8, 128 * part : 128 * part + 128] = high
        left_low[16 * r + 8 * top : 16 * r + 8 * top + 8, 128 * part : 128 * part + 128] = low

    for h in range(2):
        z = [(recv[g, 16 * h : 16 * h + 8, :], recv[g, 16 * h + 8 : 16 * h + 16, :]) for g in range(G)]
        for r, (a, b) in enumerate(sixteen(z)):
            a, b = cmul(a, b, twc[r, h : h + 1, :], tws[r, h : h + 1, :])
            put(r, 0, h, a)
            put(r, 0, 2 + h, b)
    z = []
    for g in range(G):
        tile = jnp.where(row_id < 4, recv[g, 32:40, :], 0.0)
        z.append((tile, roll(tile, -2, 0)))
    for r, (a, b) in enumerate(sixteen(z)):
        a, b = cmul(a, b, twc[r], tws[r])
        for part, value in ((0, a), (2, b)):
            put(r, 1, part, jnp.where(row_id == 0, value, 0.0))
            put(r, 1, part + 1, jnp.where(row_id == 0, roll(value, -1, 0), 0.0))

    mid[...] = (
        mm(left_high[...], inv_high[...]) + mm(left_low[...], inv_high[...]) + mm(left_high[...], inv_low[...])
    )

    first, second, single = [], [], []
    for r in range(G):
        first.append(mid[16 * r : 16 * r + 8, 0:128])
        second.append(mid[16 * r : 16 * r + 8, 128:256])
        low = mid[16 * r + 8 : 16 * r + 16, 0:128]
        high = mid[16 * r + 8 : 16 * r + 16, 128:256]
        single.append(jnp.where(row_id == 0, low, roll(high, 1, 0)))
    for i in range(8):
        a, b = first[i], second[i]
        c, d = first[i + 8], second[i + 8]
        first[i], second[i], first[i + 8], second[i + 8] = a, c, b, d
        a, c = single[i], single[i + 8]
        single[i] = jnp.where(row_id == 0, a, roll(c, 1, 0))
        single[i + 8] = jnp.where(row_id == 0, roll(a, -1, 0), c)
    for bit in (4, 2, 1):
        upper = (lane_id // (16 * bit)) % 2 == 1
        for tiles in (first, second, single):
            for i in range(G):
                if i & bit:
                    continue
                a, b = tiles[i], tiles[i | bit]
                tiles[i] = jnp.where(upper, roll(b, 16 * bit, 1), a)
                tiles[i | bit] = jnp.where(upper, b, roll(a, -16 * bit, 1))

    left = [roll(second[d], 1, 1) for d in range(G)]
    right = [roll(first[d], 1, 1) for d in range(G)]
    side = [roll(single[d], 5, 1) for d in range(G)]
    for d in range(G):
        before, after = (d - 1) % G, (d + 1) % G
        own = jnp.where(lane_id == 0, left[before], jnp.where(lane_id == 1, right[after], 0.0))
        rim = own + roll(roll(own, -1, 0), 2, 1)
        base = jnp.where(row_id == 2, roll(single[d], 2, 0), 0.0)
        base = jnp.where(row_id == 6, roll(single[d], 5, 0), base)
        base = jnp.where((row_id == 3) & (lane_id == 4), roll(side[before], 2, 0), base)
        base = jnp.where((row_id == 3) & (lane_id == 5), roll(side[after], 3, 0), base)
        for g in range(4):
            tile = jnp.where(row_id < 2, roll(first[d], -2 * g, 0), base)
            tile = jnp.where((row_id == 4) | (row_id == 5), roll(second[d], 4 - 2 * g, 0), tile)
            tile = jnp.where((row_id == 3) & (lane_id < 4), roll(rim, 3 - 2 * g, 0), tile)
            send[16 * g + d] = tile


def inverse(recv):
    t = tables()
    twc, tws = map(jnp.asarray, t["tw"])
    high, low = map(jnp.asarray, t["inv"])
    return call(
        inverse_kernel,
        sds(64, 8, 128),
        scratch_shapes=[
            pltpu.VMEM((256, 512), BF16),
            pltpu.VMEM((256, 512), BF16),
            pltpu.VMEM((256, 256), F32),
        ],
        name="inverse",
    )(recv, twc, tws, high, low)


def fine_kernel(
    pos,
    recv,
    salinity,
    zlow,
    zhigh,
    from_south,
    from_north,
    west,
    east,
    rate,
    ym,
    yt,
    ref,
    edge,
    filt,
    fedge,
    cm,
    rm,
    out,
    spread,
    y_high,
    y_low,
    side,
    vel,
    total,
    warm,
):
    grp = pos[0]
    row_id = iota((8, 128), 0)
    lane_id = iota((8, 128), 1)

    def lines(f, q):
        main = [recv[pl.ds(f * 128 + i, 16, stride=8), :] for i in (q, 4 + q, 3)]
        south = recv[pl.ds(pl.multiple_of((f * 16 + 2 * grp + q) * 8, 8), 8), :]
        north = recv[pl.ds(pl.multiple_of((f * 16 + 8 + 2 * grp + q) * 8, 8), 8), :]
        parts = []
        for x, row in zip(main, (2, 6, 3)):
            s, n = roll(south, -row, 0), roll(north, 1 - row, 0)
            if row == 3:
                s, n = roll(s, 2 * q - 4, 1), roll(n, 2 * q - 4, 1)
            tile = jnp.where(row_id == 0, s, jnp.where(row_id == 1, n, 0.0))
            parts.append(jnp.concatenate([x, tile, jnp.zeros((8, 128), F32)], 0))
        return jnp.concatenate(parts, 1)

    def along_y(table, f, q):
        high, low = halves(lines(f, q))
        return mm(table[...], jnp.concatenate([high, low], 0))

    for f in range(3):
        for q in range(2):
            at = slice(64 * (2 * f + q), 64 * (2 * f + q) + 64)
            high, low = halves(along_y(ym, f, q) * 0.05)
            y_high[at, :] = high[:, :256]
            y_low[at, :] = low[:, :256]
            side[at, :] = mm(high[:, 256:], edge[q]) + mm(low[:, 256:], edge[q])
    for q in range(2):
        high, low = halves(along_y(yt, 3, q))
        warm[16 * q : 16 * q + 16, :] = (
            mm(high[:, :256], filt[...])
            + mm(low[:, :256], filt[...])
            + mm(high[:, 256:], fedge[q])
            + mm(low[:, 256:], fedge[q])
        )
    vel[...] = mm(y_high[...], ref[...]) + mm(y_low[...], ref[...])
    vel[:, :128] += side[:, :128]
    vel[:, FINE - 128 :] += side[:, 128:]

    west_t = west[0].T
    east_t = east[0].T
    last_row = iota((8, FINE), 0) == 7
    first_row = iota((8, FINE), 0) == 0
    last_lane = lane_id == 127
    first_lane = lane_id == 0

    def outer(rows, l):
        line = jnp.concatenate([rows[16 + 8 * j + l : 17 + 8 * j + l, :] for j in range(4)], 1)
        return jnp.broadcast_to(line, (8, FINE))

    for yb in range(8):
        ys = slice(8 * yb, 8 * yb + 8)
        for q in range(2):
            vx, vy, vz = (vel[64 * (2 * f + q) + 8 * yb : 64 * (2 * f + q) + 8 * yb + 8, :] for f in range(3))
            acc = None
            for l in range(4 * q, 4 * q + 4):
                c = salinity[l, ys, :]
                upper = salinity[l + 1, ys, :] if l < 7 else zhigh[ys, :]
                lower = salinity[l - 1, ys, :] if l > 0 else zlow[ys, :]
                if yb < 7:
                    north = salinity[l, 8 * yb + 1 : 8 * yb + 9, :]
                else:
                    north = jnp.where(last_row, outer(from_north, l), roll(c, -1, 0))
                if yb > 0:
                    south = salinity[l, 8 * yb - 1 : 8 * yb + 7, :]
                else:
                    south = jnp.where(first_row, outer(from_south, l), roll(c, 1, 0))
                at = (l % 2) * 64 + 8 * yb
                ecol = jnp.broadcast_to(east_t[at : at + 8, 4 + l // 2 : 5 + l // 2], (8, 128))
                wcol = jnp.broadcast_to(west_t[at : at + 8, 4 + l // 2 : 5 + l // 2], (8, 128))
                e = roll(c, -1, 1)
                w = roll(c, 1, 1)
                e = jnp.concatenate([e[:, :-128], jnp.where(last_lane, ecol, e[:, -128:])], 1)
                w = jnp.concatenate([jnp.where(first_lane, wcol, w[:, :128]), w[:, 128:]], 1)
                k = rate[l] * 0.1
                new = (
                    c
                    + k * (((e + w) + (north + south)) + (upper + lower) - 6.0 * c)
                    - (vx * (e - w) + vy * (north - south) + vz * (upper - lower))
                )
                out[l, ys, :] = new
                acc = new if acc is None else acc + new
            total[64 * q + 8 * yb : 64 * q + 8 * yb + 8, :] = acc
    high, low = halves(total[...])
    high, low = halves(mm(high, cm[...]) + mm(low, cm[...]))
    mean = warm[...] - mm(rm[...], jnp.concatenate([high, low], 0))
    for a in range(G):
        spread[a] = mean


def fine(pos, recv1, recv2, salinity, zlow, zhigh, from_south, from_north, rate):
    t = tables()
    whole = lambda x: pl.BlockSpec(x.shape, lambda i, m, n=x.ndim: (0,) * n)
    consts = [jnp.asarray(t[name]) for name in ("ym", "yt", "ref", "edge", "filt", "fedge", "cm", "rm")]
    recv2 = recv2.reshape(512, 128)
    arrays = [recv2, salinity, zlow, zhigh, from_south, from_north]
    near = lambda step: pl.BlockSpec((1, 8, 128), lambda i, m: ((m[1] + step) % G, 4, 0))
    return call(
        fine_kernel,
        (sds(8, 64, FINE), sds(G, 32, 256)),
        grid_spec=pltpu.PrefetchScalarGridSpec(
            num_scalar_prefetch=1,
            grid=(1,),
            in_specs=[whole(x) for x in arrays]
            + [near(G - 1), near(1), pl.BlockSpec(memory_space=pltpu.SMEM)]
            + [whole(x) for x in consts],
            out_specs=[
                pl.BlockSpec((8, 64, FINE), lambda i, m: (0, 0, 0)),
                pl.BlockSpec((G, 32, 256), lambda i, m: (0, 0, 0)),
            ],
            scratch_shapes=[
                pltpu.VMEM((384, 256), BF16),
                pltpu.VMEM((384, 256), BF16),
                pltpu.VMEM((384, 256), F32),
                pltpu.VMEM((384, FINE), F32),
                pltpu.VMEM((128, FINE), F32),
                pltpu.VMEM((32, 256), F32),
            ],
        ),
        name="fine",
    )(pos, *arrays, recv1, recv1, rate, *consts)


def table_kernel(pos, base, high, low):
    turns = (iota((16, 128), 0) * pos[1]) % G
    angle = turns.astype(F32) * (2.0 * math.pi / G)
    cos = jnp.concatenate([jnp.cos(angle)] * 2, 1)
    sin = -jnp.concatenate([jnp.sin(angle)] * 2, 1)
    for t in range(G):
        rows = slice(16 * t, 16 * t + 16)
        real, imag = base[rows, :256], base[rows, 256:]
        for at, value in ((0, real * cos - imag * sin), (256, real * sin + imag * cos)):
            high[rows, at : at + 256], low[rows, at : at + 256] = halves(value)


def table(pos):
    whole = pl.BlockSpec((256, 512), lambda i, m: (0, 0))
    return call(
        table_kernel,
        (sds(256, 512, dtype=BF16), sds(256, 512, dtype=BF16)),
        grid_spec=pltpu.PrefetchScalarGridSpec(
            num_scalar_prefetch=1, grid=(1,), in_specs=[whole], out_specs=[whole, whole]
        ),
        name="table",
    )(pos, jnp.asarray(tables()["fwd"]))


def forward_kernel(recv, table_high, table_low, comb_cos, comb_sin, out, left_high, left_low, mid):
    for a in range(G):
        high, low = halves(recv[a])
        left_high[32 * a : 32 * a + 32, :] = high
        left_low[32 * a : 32 * a + 32, :] = low
    mid[...] = (
        mm(left_high[...], table_high[...]) + mm(left_low[...], table_high[...]) + mm(left_high[...], table_low[...])
    )
    real = imag = jnp.zeros((32, 256), F32)
    for a in range(G):
        c, s = comb_cos[a : a + 1, :], comb_sin[a : a + 1, :]
        x, y = mid[32 * a : 32 * a + 32, :256], mid[32 * a : 32 * a + 32, 256:]
        real = real + (x * c + y * s)
        imag = imag + (y * c - x * s)
    for g in range(4):
        out[g, 0:32, :] = real
        out[g, 32:64, :] = imag


def forward(recv, high, low):
    cos, sin = map(jnp.asarray, tables()["comb"])
    return call(
        forward_kernel,
        sds(4, 64, 256),
        scratch_shapes=[
            pltpu.VMEM((512, 256), BF16),
            pltpu.VMEM((512, 256), BF16),
            pltpu.VMEM((512, 512), F32),
        ],
        name="forward",
    )(recv, high, low, cos, sin)


def shifted(array, axis, step):
    count = lax.axis_size(axis)
    return lax.ppermute(array, axis, [(i, (i + step) % count) for i in range(count)])


def per_device(coarse_modes, salinity, viscosity, forcing_gain, diffusivity):
    me = lax.axis_index(GX).astype(jnp.int32)
    pos = jnp.stack([lax.axis_index("grp").astype(jnp.int32), me])
    modes = coarse_modes.reshape(256, 256)
    chunk, up, down, low_face, high_face = edges(pos[1:], modes, salinity)
    from_south = shifted(up, "gy", 1)
    from_north = shifted(down, "gy", -1)
    zlow = shifted(high_face, "grp", 1)
    zhigh = shifted(low_face, "grp", -1)
    chunk = tails(chunk, from_south, from_north)
    recv1 = lax.all_to_all(chunk, GX, 0, 0, tiled=True)
    recv2 = lax.all_to_all(inverse(recv1), GRP_GX, 0, 0, tiled=True)
    salinity_next, spread = fine(
        pos, recv1, recv2, salinity, zlow, zhigh, from_south, from_north, diffusivity
    )
    recv3 = lax.all_to_all(spread, GX, 0, 0, tiled=True)
    recv4 = lax.all_to_all(forward(recv3, *table(pos)), "grp", 0, 0, tiled=True)
    spectrum = recv4.reshape(4, 2, 2, 16, W).transpose(1, 0, 2, 3, 4).reshape(2, 8, 16, W)
    mode_index = me * W + lax.broadcasted_iota(jnp.int32, (W,), 0)
    wavenumber = jnp.where(mode_index < NV // 2, mode_index, mode_index - NV)
    scaled_wave = 2.0 * math.pi / NV * wavenumber.astype(F32)
    damping = jnp.exp(-viscosity[0] * scaled_wave * scaled_wave)
    coarse_next = damping * coarse_modes + forcing_gain[0] * spectrum[None]
    return (salinity_next, coarse_next)


def solution(mesh):
    finer = Mesh(
        mesh.devices.reshape(mesh.shape["grp"], 2, 8, mesh.shape["gy"]),
        ("grp", "gx_0", "gx_1", "gy"),
    )
    in_specs = (P("grp", None, None, "gy", GX), P("grp", "gy", GX), P("grp"), P("grp"), P("grp"))
    out_specs = (P("grp", "gy", GX), P("grp", None, None, "gy", GX))
    return jax.shard_map(
        per_device, mesh=finer, in_specs=in_specs, out_specs=out_specs, check_vma=False
    )
```

```python
import functools
import math

import jax
import jax.numpy as jnp
import numpy as np
from jax import lax
from jax.experimental import pallas as pl
from jax.experimental.pallas import tpu as pltpu
from jax.sharding import Mesh
from jax.sharding import PartitionSpec as P

GX = ("gx_0", "gx_1")
GRP_GX = ("grp", "gx_0", "gx_1")
F32 = jnp.float32
BF16 = jnp.bfloat16
G = 16
NV = 4096
W = 256
FINE = 1024


def split_table(table):
    table = np.asarray(table, np.float64)
    high = table.astype(np.float32).astype(jnp.bfloat16)
    low = (table - high.astype(np.float64)).astype(np.float32).astype(jnp.bfloat16)
    return high, low


@functools.cache
def tables():
    out = {}
    k = np.arange(W)
    angle = 2 * np.pi * (np.outer(k, k) % W) / W
    norm = NV ** -0.5
    out["inv"] = split_table(np.concatenate([np.cos(angle), -np.sin(angle)], 0) * norm)
    r = np.arange(G)
    angle = 2 * np.pi * np.outer(r, k) / NV
    twc = np.zeros((G, 8, 128), np.float32)
    tws = np.zeros((G, 8, 128), np.float32)
    twc[:, :2] = np.cos(angle).reshape(G, 2, 128)
    tws[:, :2] = np.sin(angle).reshape(G, 2, 128)
    out["tw"] = (twc, tws)
    lanes = 16 * (k % 16) + k // 16
    order = np.argsort(lanes)
    assert np.array_equal(order, 16 * (k % 16) + k // 16)
    full = np.zeros((W + 2, FINE))
    for n in range(FINE):
        c, s = divmod(n, 4)
        o = (s + 0.5) / 4 - 0.5
        full[c + 1, n] += 1 - abs(o)
        full[c + 1 + (1 if o > 0 else -1), n] += abs(o)
    out["ref"] = full[1:-1][order].astype(jnp.bfloat16)
    edge = np.zeros((2, 128, 256))
    filt = np.zeros((W + 2, W))
    for b in range(W):
        filt[b : b + 3, b] = (0.125, 0.75, 0.125)
    out["filt"] = filt[1:-1][order].astype(jnp.bfloat16)
    fedge = np.zeros((2, 128, 256))
    for q in range(2):
        edge[q, 2 * q, :128] = full[0, :128]
        edge[q, 2 * q + 1, 128:] = full[-1, -128:]
        fedge[q, 2 * q] = filt[0]
        fedge[q, 2 * q + 1] = filt[-1]
    out["edge"] = edge.astype(jnp.bfloat16)
    out["fedge"] = fedge.astype(jnp.bfloat16)
    ym = np.zeros((64, 32))
    yt = np.zeros((16, 32))
    place = lambda c: 16 if c < 0 else 17 if c > 15 else c
    for n in range(64):
        c, s = divmod(n, 4)
        o = (s + 0.5) / 4 - 0.5
        ym[n, c] += 1 - abs(o)
        ym[n, place(c + (1 if o > 0 else -1))] += abs(o)
    for c in range(16):
        yt[c, c] += 0.75
        yt[c, place(c - 1)] += 0.125
        yt[c, place(c + 1)] += 0.125
    out["ym"] = np.concatenate([ym, ym], 1).astype(jnp.bfloat16)
    out["yt"] = np.concatenate([yt, yt], 1).astype(jnp.bfloat16)
    cm = np.zeros((FINE, W))
    cm[np.arange(FINE), np.arange(FINE) // 4] = 1.0 / 4
    out["cm"] = cm.astype(jnp.bfloat16)
    rm = np.zeros((32, 128))
    rm[np.arange(128) // 4, np.arange(128)] = 1.0 / 16
    out["rm"] = np.concatenate([rm, rm], 1).astype(jnp.bfloat16)
    g = np.arange(G)
    angle = 2 * np.pi * np.outer(k, k) / NV
    out["fwd"] = (np.concatenate([np.cos(angle), -np.sin(angle)], 1) * norm).astype(np.float32)
    angle = 2 * np.pi * (np.outer(g, k) % G) / G
    out["comb"] = (np.cos(angle).astype(np.float32), np.sin(angle).astype(np.float32))
    return out


def halves(x):
    high = x.astype(BF16)
    low = (x - high.astype(F32)).astype(BF16)
    return high, low


def mm(a, b):
    return jnp.dot(a, b, preferred_element_type=F32)


VM = pl.BlockSpec(memory_space=pltpu.VMEM)
SM = pl.BlockSpec(memory_space=pltpu.SMEM)
HB = pl.BlockSpec(memory_space=pltpu.HBM)


def call(kernel, out_shape, in_specs, out_specs, limit=12, **kw):
    inner = pl.pallas_call(
        kernel,
        out_shape=out_shape,
        in_specs=in_specs,
        out_specs=out_specs,
        compiler_params=pltpu.CompilerParams(vmem_limit_bytes=limit << 20),
        **kw,
    )

    def placed(*args):
        return inner(
            *[x if spec is not HB else pltpu.with_memory_space_constraint(x, pltpu.HBM) for x, spec in zip(args, in_specs)]
        )

    return placed


def fetch(pairs, sems, first=0):
    copies = [pltpu.make_async_copy(src, dst, sems.at[first + i]) for i, (src, dst) in enumerate(pairs)]
    for copy in copies:
        copy.start()
    return copies


def sds(*shape, dtype=F32):
    return jax.ShapeDtypeStruct(shape, dtype)


def iota(shape, dim):
    return lax.broadcasted_iota(jnp.int32, shape, dim)


def roll(x, shift, axis):
    return pltpu.roll(x, shift % x.shape[axis], axis)


def edges_kernel(me, modes, sal, chunk, up, down, zlow, zhigh, modes_a, modes_b, south, north, west, east, sems):
    copies = fetch(
        (
            (modes.at[:, 0:128], modes_a),
            (modes.at[:, 128:256], modes_b),
            (sal.at[:, 0:8, :], south),
            (sal.at[:, 56:64, :], north),
            (sal.at[:, :, 0:128], west),
            (sal.at[:, :, FINE - 128 :], east),
            (sal.at[0], zlow),
            (sal.at[7], zhigh),
        ),
        sems,
    )
    for copy in copies[:4]:
        copy.wait()
    for dst, rows, row, line in ((up, north, 7, 15), (down, south, 0, 0)):
        dst[0:16, :128] = modes_a[pl.ds(line, 16, stride=16), :]
        dst[0:16, 128:] = modes_b[pl.ds(line, 16, stride=16), :]
        face = rows[:, row, :]
        for j in range(4):
            dst[16 + 8 * j : 24 + 8 * j, :] = face[:, 256 * j : 256 * j + 256]
    zero = jnp.zeros((8, 128), F32)
    for r in range(G):
        chunk[r, 0:16, :] = modes_a[pl.ds(r, 16, stride=16), :]
        chunk[r, 16:32, :] = modes_b[pl.ds(r, 16, stride=16), :]
        chunk[r, 32:40, :] = zero
    row_id = iota((8, 128), 0)

    def column(block, lane):
        tile = zero
        for i in range(4):
            both = jnp.concatenate([block[2 * i], block[2 * i + 1]], 0).T
            line = jnp.broadcast_to(both[lane : lane + 1, :], (8, 128))
            tile = jnp.where(row_id == 4 + i, line, tile)
        return tile

    for copy in copies[4:6]:
        copy.wait()
    chunk[(me[0] + 1) % G, 32:40, :] = column(east, 127)
    chunk[(me[0] + G - 1) % G, 32:40, :] = column(west, 0)
    for copy in copies[6:]:
        copy.wait()


def edges(me, modes, salinity):
    return call(
        edges_kernel,
        (sds(G, 40, 128), sds(48, 256), sds(48, 256), sds(64, FINE), sds(64, FINE)),
        [SM, HB, HB],
        [VM, VM, VM, HB, HB],
        scratch_shapes=[
            pltpu.VMEM((256, 128), F32),
            pltpu.VMEM((256, 128), F32),
            pltpu.VMEM((8, 8, FINE), F32),
            pltpu.VMEM((8, 8, FINE), F32),
            pltpu.VMEM((8, 64, 128), F32),
            pltpu.VMEM((8, 64, 128), F32),
            pltpu.SemaphoreType.DMA((8,)),
        ],
        name="edges",
    )(me, modes, salinity)


def tails_kernel(chunk, from_south, from_north, out):
    row_id = iota((8, 128), 0)
    for r in range(G):
        rows = from_south if r < 8 else from_north
        p = r % 8
        tile = chunk[r, 32:40, :]
        parts = (rows[p : p + 1, :128], rows[p : p + 1, 128:], rows[8 + p : 9 + p, :128], rows[8 + p : 9 + p, 128:])
        for i, part in enumerate(parts):
            tile = jnp.where(row_id == i, jnp.broadcast_to(part, (8, 128)), tile)
        out[r, 0:32, :] = chunk[r, 0:32, :]
        out[r, 32:40, :] = tile


def tails(chunk, from_south, from_north):
    return call(tails_kernel, sds(G, 40, 128), [VM] * 3, VM, name="tails")(chunk, from_south, from_north)


def cmul(a, b, c, s):
    return a * c - b * s, a * s + b * c


def four(z):
    (ar, ai), (br, bi), (cr, ci), (dr, di) = z
    t0r, t0i, t1r, t1i = ar + cr, ai + ci, ar - cr, ai - ci
    t2r, t2i, t3r, t3i = br + dr, bi + di, br - dr, bi - di
    return (
        (t0r + t2r, t0i + t2i),
        (t1r - t3i, t1i + t3r),
        (t0r - t2r, t0i - t2i),
        (t1r + t3i, t1i - t3r),
    )


def sixteen(z):
    inner = [four([z[4 * g1 + g0] for g1 in range(4)]) for g0 in range(4)]
    out = [None] * 16
    for r0 in range(4):
        column = []
        for g0 in range(4):
            angle = 2 * math.pi * g0 * r0 / 16
            a, b = inner[g0][r0]
            column.append((a, b) if g0 * r0 == 0 else cmul(a, b, math.cos(angle), math.sin(angle)))
        for r1, value in enumerate(four(column)):
            out[4 * r1 + r0] = value
    return out


def inverse_kernel(recv, twc_hbm, tws_hbm, high_hbm, low_hbm, send, left_high, left_low, mid, twc, tws, inv_high, inv_low, sems):
    copies = fetch(((twc_hbm, twc), (tws_hbm, tws), (high_hbm, inv_high), (low_hbm, inv_low)), sems)
    for copy in copies[:2]:
        copy.wait()

    row_id = iota((8, 128), 0)
    lane_id = iota((8, 128), 1)

    def put(r, top, part, value):
        high, low = halves(value)
        left_high[16 * r + 8 * top : 16 * r + 8 * top + 8, 128 * part : 128 * part + 128] = high
        left_low[16 * r + 8 * top : 16 * r + 8 * top + 8, 128 * part : 128 * part + 128] = low

    for h in range(2):
        z = [(recv[g, 16 * h : 16 * h + 8, :], recv[g, 16 * h + 8 : 16 * h + 16, :]) for g in range(G)]
        for r, (a, b) in enumerate(sixteen(z)):
            a, b = cmul(a, b, twc[r, h : h + 1, :], tws[r, h : h + 1, :])
            put(r, 0, h, a)
            put(r, 0, 2 + h, b)
    z = []
    for g in range(G):
        tile = jnp.where(row_id < 4, recv[g, 32:40, :], 0.0)
        z.append((tile, roll(tile, -2, 0)))
    for r, (a, b) in enumerate(sixteen(z)):
        a, b = cmul(a, b, twc[r], tws[r])
        for part, value in ((0, a), (2, b)):
            put(r, 1, part, jnp.where(row_id == 0, value, 0.0))
            put(r, 1, part + 1, jnp.where(row_id == 0, roll(value, -1, 0), 0.0))

    for copy in copies[2:]:
        copy.wait()
    mid[...] = (
        mm(left_high[...], inv_high[...]) + mm(left_low[...], inv_high[...]) + mm(left_high[...], inv_low[...])
    )

    first, second, single = [], [], []
    for r in range(G):
        first.append(mid[16 * r : 16 * r + 8, 0:128])
        second.append(mid[16 * r : 16 * r + 8, 128:256])
        low = mid[16 * r + 8 : 16 * r + 16, 0:128]
        high = mid[16 * r + 8 : 16 * r + 16, 128:256]
        single.append(jnp.where(row_id == 0, low, roll(high, 1, 0)))
    for i in range(8):
        a, b = first[i], second[i]
        c, d = first[i + 8], second[i + 8]
        first[i], second[i], first[i + 8], second[i + 8] = a, c, b, d
        a, c = single[i], single[i + 8]
        single[i] = jnp.where(row_id == 0, a, roll(c, 1, 0))
        single[i + 8] = jnp.where(row_id == 0, roll(a, -1, 0), c)
    for bit in (4, 2, 1):
        upper = (lane_id // (16 * bit)) % 2 == 1
        for tiles in (first, second, single):
            for i in range(G):
                if i & bit:
                    continue
                a, b = tiles[i], tiles[i | bit]
                tiles[i] = jnp.where(upper, roll(b, 16 * bit, 1), a)
                tiles[i | bit] = jnp.where(upper, b, roll(a, -16 * bit, 1))

    left = [roll(second[d], 1, 1) for d in range(G)]
    right = [roll(first[d], 1, 1) for d in range(G)]
    side = [roll(single[d], 5, 1) for d in range(G)]
    for d in range(G):
        before, after = (d - 1) % G, (d + 1) % G
        own = jnp.where(lane_id == 0, left[before], jnp.where(lane_id == 1, right[after], 0.0))
        rim = own + roll(roll(own, -1, 0), 2, 1)
        base = jnp.where(row_id == 2, roll(single[d], 2, 0), 0.0)
        base = jnp.where(row_id == 6, roll(single[d], 5, 0), base)
        base = jnp.where((row_id == 3) & (lane_id == 4), roll(side[before], 2, 0), base)
        base = jnp.where((row_id == 3) & (lane_id == 5), roll(side[after], 3, 0), base)
        for g in range(4):
            tile = jnp.where(row_id < 2, roll(first[d], -2 * g, 0), base)
            tile = jnp.where((row_id == 4) | (row_id == 5), roll(second[d], 4 - 2 * g, 0), tile)
            tile = jnp.where((row_id == 3) & (lane_id < 4), roll(rim, 3 - 2 * g, 0), tile)
            send[16 * g + d] = tile


def inverse(recv):
    t = tables()
    twc, tws = map(jnp.asarray, t["tw"])
    high, low = map(jnp.asarray, t["inv"])
    return call(
        inverse_kernel,
        sds(64, 8, 128),
        [VM, HB, HB, HB, HB],
        VM,
        scratch_shapes=[
            pltpu.VMEM((256, 512), BF16),
            pltpu.VMEM((256, 512), BF16),
            pltpu.VMEM((256, 256), F32),
            pltpu.VMEM((G, 8, 128), F32),
            pltpu.VMEM((G, 8, 128), F32),
            pltpu.VMEM((512, 256), BF16),
            pltpu.VMEM((512, 256), BF16),
            pltpu.SemaphoreType.DMA((4,)),
        ],
        name="inverse",
    )(recv, twc, tws, high, low)


CONSTS = ("ym", "edge", "yt", "filt", "fedge", "ref", "cm", "rm")


def fine_kernel(me, grp_ref, rate_hbm, recv, edge_cols, salinity, zlow, zhigh, from_south, from_north, *rest):
    hbm, (out, spread), rest = rest[:8], rest[8:10], rest[10:]
    (y_high, y_low, side, vel, total, warm, new_sal), consts, (rate, sems, out_sems) = rest[:7], rest[7:15], rest[15:]
    *copies, rates = fetch(tuple(zip(hbm, consts)) + ((rate_hbm, rate),), sems)
    copies = dict(zip(CONSTS, copies))
    ym, edge, yt, filt, fedge, ref, cm, rm = consts
    grp = grp_ref[0]
    copies["ym"].wait()
    copies["edge"].wait()
    row_id = iota((8, 128), 0)
    lane_id = iota((8, 128), 1)

    def lines(f, q):
        main = [recv[pl.ds(f * 128 + i, 16, stride=8), :] for i in (q, 4 + q, 3)]
        south = recv[pl.ds(pl.multiple_of((f * 16 + 2 * grp + q) * 8, 8), 8), :]
        north = recv[pl.ds(pl.multiple_of((f * 16 + 8 + 2 * grp + q) * 8, 8), 8), :]
        parts = []
        for x, row in zip(main, (2, 6, 3)):
            s, n = roll(south, -row, 0), roll(north, 1 - row, 0)
            if row == 3:
                s, n = roll(s, 2 * q - 4, 1), roll(n, 2 * q - 4, 1)
            tile = jnp.where(row_id == 0, s, jnp.where(row_id == 1, n, 0.0))
            parts.append(jnp.concatenate([x, tile, jnp.zeros((8, 128), F32)], 0))
        return jnp.concatenate(parts, 1)

    def along_y(table, f, q):
        high, low = halves(lines(f, q))
        return mm(table[...], jnp.concatenate([high, low], 0))

    for f in range(3):
        for q in range(2):
            at = slice(64 * (2 * f + q), 64 * (2 * f + q) + 64)
            high, low = halves(along_y(ym, f, q) * 0.05)
            y_high[at, :] = high[:, :256]
            y_low[at, :] = low[:, :256]
            side[at, :] = mm(high[:, 256:], edge[q]) + mm(low[:, 256:], edge[q])
    for name in ("yt", "filt", "fedge"):
        copies[name].wait()
    for q in range(2):
        high, low = halves(along_y(yt, 3, q))
        warm[16 * q : 16 * q + 16, :] = (
            mm(high[:, :256], filt[...])
            + mm(low[:, :256], filt[...])
            + mm(high[:, 256:], fedge[q])
            + mm(low[:, 256:], fedge[q])
        )
    copies["ref"].wait()
    vel[...] = mm(y_high[...], ref[...]) + mm(y_low[...], ref[...])
    vel[:, :128] += side[:, :128]
    vel[:, FINE - 128 :] += side[:, 128:]

    west_t = edge_cols[(me[0] + G - 1) % G, 32:40, :].T
    east_t = edge_cols[(me[0] + 1) % G, 32:40, :].T
    last_row = iota((8, FINE), 0) == 7
    first_row = iota((8, FINE), 0) == 0
    last_lane = lane_id == 127
    first_lane = lane_id == 0

    def outer(rows, l):
        line = jnp.concatenate([rows[16 + 8 * j + l : 17 + 8 * j + l, :] for j in range(4)], 1)
        return jnp.broadcast_to(line, (8, FINE))

    rates.wait()
    stores = []
    for yb in range(8):
        ys = slice(8 * yb, 8 * yb + 8)
        for q in range(2):
            vx, vy, vz = (vel[64 * (2 * f + q) + 8 * yb : 64 * (2 * f + q) + 8 * yb + 8, :] for f in range(3))
            acc = None
            for l in range(4 * q, 4 * q + 4):
                c = salinity[l, ys, :]
                upper = salinity[l + 1, ys, :] if l < 7 else zhigh[ys, :]
                lower = salinity[l - 1, ys, :] if l > 0 else zlow[ys, :]
                if yb < 7:
                    north = salinity[l, 8 * yb + 1 : 8 * yb + 9, :]
                else:
                    north = jnp.where(last_row, outer(from_north, l), roll(c, -1, 0))
                if yb > 0:
                    south = salinity[l, 8 * yb - 1 : 8 * yb + 7, :]
                else:
                    south = jnp.where(first_row, outer(from_south, l), roll(c, 1, 0))
                at = (l % 2) * 64 + 8 * yb
                ecol = jnp.broadcast_to(east_t[at : at + 8, 4 + l // 2 : 5 + l // 2], (8, 128))
                wcol = jnp.broadcast_to(west_t[at : at + 8, 4 + l // 2 : 5 + l // 2], (8, 128))
                e = roll(c, -1, 1)
                w = roll(c, 1, 1)
                e = jnp.concatenate([e[:, :-128], jnp.where(last_lane, ecol, e[:, -128:])], 1)
                w = jnp.concatenate([jnp.where(first_lane, wcol, w[:, :128]), w[:, 128:]], 1)
                k = rate[l] * 0.1
                new = (
                    c
                    + k * (((e + w) + (north + south)) + (upper + lower) - 6.0 * c)
                    - (vx * (e - w) + vy * (north - south) + vz * (upper - lower))
                )
                new_sal[l, ys, :] = new
                acc = new if acc is None else acc + new
            total[64 * q + 8 * yb : 64 * q + 8 * yb + 8, :] = acc
        stores.append(pltpu.make_async_copy(new_sal.at[:, ys, :], out.at[:, ys, :], out_sems.at[yb]))
        stores[-1].start()
    copies["cm"].wait()
    copies["rm"].wait()
    high, low = halves(total[...])
    high, low = halves(mm(high, cm[...]) + mm(low, cm[...]))
    mean = warm[...] - mm(rm[...], jnp.concatenate([high, low], 0))
    for a in range(G):
        spread[a] = mean
    for store in stores:
        store.wait()


def fine(me, grp, recv1, recv2, salinity, zlow, zhigh, from_south, from_north, rate):
    consts = [jnp.asarray(tables()[name]) for name in CONSTS]
    arrays = [recv2.reshape(512, 128), recv1, salinity, zlow, zhigh, from_south, from_north]
    return call(
        fine_kernel,
        (sds(8, 64, FINE), sds(G, 32, 256)),
        [SM, SM, HB] + [VM] * len(arrays) + [HB] * len(consts),
        [HB, VM],
        scratch_shapes=[
            pltpu.VMEM((384, 256), BF16),
            pltpu.VMEM((384, 256), BF16),
            pltpu.VMEM((384, 256), F32),
            pltpu.VMEM((384, FINE), F32),
            pltpu.VMEM((128, FINE), F32),
            pltpu.VMEM((32, 256), F32),
            pltpu.VMEM((8, 64, FINE), F32),
        ]
        + [pltpu.VMEM(x.shape, x.dtype) for x in consts]
        + [pltpu.SMEM((8,), F32), pltpu.SemaphoreType.DMA((len(consts) + 1,)), pltpu.SemaphoreType.DMA((8,))],
        limit=24,
        name="fine",
    )(me, grp, rate, *arrays, *consts)


def table_kernel(me, base, high, low):
    turns = (iota((16, 128), 0) * me[0]) % G
    angle = turns.astype(F32) * (2.0 * math.pi / G)
    cos = jnp.concatenate([jnp.cos(angle)] * 2, 1)
    sin = -jnp.concatenate([jnp.sin(angle)] * 2, 1)
    for t in range(G):
        rows = slice(16 * t, 16 * t + 16)
        real, imag = base[rows, :256], base[rows, 256:]
        for at, value in ((0, real * cos - imag * sin), (256, real * sin + imag * cos)):
            high[rows, at : at + 256], low[rows, at : at + 256] = halves(value)


def table(me):
    return call(
        table_kernel,
        (sds(256, 512, dtype=BF16), sds(256, 512, dtype=BF16)),
        [SM, VM],
        [VM, VM],
        name="table",
    )(me, jnp.asarray(tables()["fwd"]))


def forward_kernel(recv, table_high, table_low, cos_hbm, sin_hbm, out, left_high, left_low, mid, comb_cos, comb_sin, sems):
    copies = fetch(((cos_hbm, comb_cos), (sin_hbm, comb_sin)), sems)
    for a in range(G):
        high, low = halves(recv[a])
        left_high[32 * a : 32 * a + 32, :] = high
        left_low[32 * a : 32 * a + 32, :] = low
    mid[...] = (
        mm(left_high[...], table_high[...]) + mm(left_low[...], table_high[...]) + mm(left_high[...], table_low[...])
    )
    for copy in copies:
        copy.wait()
    real = imag = jnp.zeros((32, 256), F32)
    for a in range(G):
        c, s = comb_cos[a : a + 1, :], comb_sin[a : a + 1, :]
        x, y = mid[32 * a : 32 * a + 32, :256], mid[32 * a : 32 * a + 32, 256:]
        real = real + (x * c + y * s)
        imag = imag + (y * c - x * s)
    for g in range(4):
        out[g, 0:32, :] = real
        out[g, 32:64, :] = imag


def forward(recv, high, low):
    cos, sin = map(jnp.asarray, tables()["comb"])
    return call(
        forward_kernel,
        sds(4, 64, 256),
        [VM, VM, VM, HB, HB],
        VM,
        scratch_shapes=[
            pltpu.VMEM((512, 256), BF16),
            pltpu.VMEM((512, 256), BF16),
            pltpu.VMEM((512, 512), F32),
            pltpu.VMEM((G, 256), F32),
            pltpu.VMEM((G, 256), F32),
            pltpu.SemaphoreType.DMA((2,)),
        ],
        name="forward",
    )(recv, high, low, cos, sin)


def finish_kernel(me, viscosity, gain, recv, modes, out):
    index = me[0] * W + iota((8, W), 1)
    number = jnp.where(index < NV // 2, index, index - NV).astype(F32)
    wave = (2.0 * math.pi / NV) * number
    damping = jnp.exp(-viscosity[0] * wave * wave)[0:1, :]
    for c in range(2):
        for g in range(4):
            at = slice(128 * c + 32 * g, 128 * c + 32 * g + 32)
            out[at, :] = damping * modes[at, :] + gain[0] * recv[g, 32 * c : 32 * c + 32, :]


def finish(me, viscosity, gain, recv, modes):
    return call(finish_kernel, sds(256, W), [SM, SM, SM, VM, VM], VM, name="finish")(
        me, viscosity, gain, recv, modes
    )


def shifted(array, axis, step):
    count = lax.axis_size(axis)
    return lax.ppermute(array, axis, [(i, (i + step) % count) for i in range(count)])


def per_device(coarse_modes, salinity, viscosity, forcing_gain, diffusivity):
    me = lax.axis_index(GX).astype(jnp.int32).reshape(1)
    grp = lax.axis_index("grp").astype(jnp.int32).reshape(1)
    modes = coarse_modes.reshape(256, 256)
    chunk, up, down, low_face, high_face = edges(me, modes, salinity)
    zlow = shifted(high_face, "grp", 1)
    zhigh = shifted(low_face, "grp", -1)
    from_south = shifted(up, "gy", 1)
    from_north = shifted(down, "gy", -1)
    weights = table(me)
    from_south, from_north, zlow, zhigh, weights = lax.optimization_barrier(
        (from_south, from_north, zlow, zhigh, weights)
    )
    chunk = tails(chunk, from_south, from_north)
    recv1 = lax.all_to_all(chunk, GX, 0, 0, tiled=True)
    recv2 = lax.all_to_all(inverse(recv1), GRP_GX, 0, 0, tiled=True)
    salinity_next, spread = fine(
        me, grp, recv1, recv2, salinity, zlow, zhigh, from_south, from_north, diffusivity
    )
    recv3 = lax.all_to_all(spread, GX, 0, 0, tiled=True)
    recv4 = lax.all_to_all(forward(recv3, *weights), "grp", 0, 0, tiled=True)
    coarse_next = finish(me, viscosity, forcing_gain, recv4, modes)
    return (salinity_next, coarse_next.reshape(coarse_modes.shape))


def solution(mesh):
    finer = Mesh(
        mesh.devices.reshape(mesh.shape["grp"], 2, 8, mesh.shape["gy"]),
        ("grp", "gx_0", "gx_1", "gy"),
    )
    in_specs = (P("grp", None, None, "gy", GX), P("grp", "gy", GX), P("grp"), P("grp"), P("grp"))
    out_specs = (P("grp", "gy", GX), P("grp", None, None, "gy", GX))
    return jax.shard_map(
        per_device, mesh=finer, in_specs=in_specs, out_specs=out_specs, check_vma=False
    )
```

```python
import functools
import math

import jax
import jax.numpy as jnp
import numpy as np
from jax import lax
from jax.experimental import pallas as pl
from jax.experimental.pallas import tpu as pltpu
from jax.sharding import Mesh
from jax.sharding import PartitionSpec as P

GX = ("gx_0", "gx_1")
GRP_GX = ("grp", "gx_0", "gx_1")
F32 = jnp.float32
BF16 = jnp.bfloat16
G = 16
NV = 4096
W = 256
FINE = 1024


def split_table(table):
    table = np.asarray(table, np.float64)
    high = table.astype(np.float32).astype(jnp.bfloat16)
    low = (table - high.astype(np.float64)).astype(np.float32).astype(jnp.bfloat16)
    return high, low


@functools.cache
def tables():
    out = {}
    k = np.arange(W)
    angle = 2 * np.pi * (np.outer(k, k) % W) / W
    norm = NV ** -0.5
    out["inv"] = split_table(np.concatenate([np.cos(angle), -np.sin(angle)], 0) * norm)
    r = np.arange(G)
    angle = 2 * np.pi * np.outer(r, k) / NV
    twc = np.zeros((G, 8, 128), np.float32)
    tws = np.zeros((G, 8, 128), np.float32)
    twc[:, :2] = np.cos(angle).reshape(G, 2, 128)
    tws[:, :2] = np.sin(angle).reshape(G, 2, 128)
    out["tw"] = (twc, tws)
    lanes = 16 * (k % 16) + k // 16
    order = np.argsort(lanes)
    assert np.array_equal(order, 16 * (k % 16) + k // 16)
    full = np.zeros((W + 2, FINE))
    for n in range(FINE):
        c, s = divmod(n, 4)
        o = (s + 0.5) / 4 - 0.5
        full[c + 1, n] += 1 - abs(o)
        full[c + 1 + (1 if o > 0 else -1), n] += abs(o)
    out["ref"] = full[1:-1][order].astype(jnp.bfloat16)
    edge = np.zeros((2, 128, 256))
    filt = np.zeros((W + 2, W))
    for b in range(W):
        filt[b : b + 3, b] = (0.125, 0.75, 0.125)
    out["filt"] = filt[1:-1][order].astype(jnp.bfloat16)
    fedge = np.zeros((2, 128, 256))
    for q in range(2):
        edge[q, 2 * q, :128] = full[0, :128]
        edge[q, 2 * q + 1, 128:] = full[-1, -128:]
        fedge[q, 2 * q] = filt[0]
        fedge[q, 2 * q + 1] = filt[-1]
    out["edge"] = edge.astype(jnp.bfloat16)
    out["fedge"] = fedge.astype(jnp.bfloat16)
    ym = np.zeros((64, 32))
    yt = np.zeros((16, 32))
    place = lambda c: 16 if c < 0 else 17 if c > 15 else c
    for n in range(64):
        c, s = divmod(n, 4)
        o = (s + 0.5) / 4 - 0.5
        ym[n, c] += 1 - abs(o)
        ym[n, place(c + (1 if o > 0 else -1))] += abs(o)
    for c in range(16):
        yt[c, c] += 0.75
        yt[c, place(c - 1)] += 0.125
        yt[c, place(c + 1)] += 0.125
    out["ym"] = np.concatenate([ym, ym], 1).astype(jnp.bfloat16)
    out["yt"] = np.concatenate([yt, yt], 1).astype(jnp.bfloat16)
    cm = np.zeros((512, 128))
    cm[np.arange(512), np.arange(512) // 4] = 1.0 / 4
    out["cm"] = cm.astype(jnp.bfloat16)
    rm = np.zeros((32, 128))
    rm[np.arange(128) // 4, np.arange(128)] = 1.0 / 16
    out["rm"] = np.concatenate([rm, rm], 1).astype(jnp.bfloat16)
    g = np.arange(G)
    fine_angle = 2 * np.pi * np.outer(g, k) / NV
    coarse_angle = 2 * np.pi * (np.outer(g, k) % W) / W
    out["fwd"] = tuple(
        x.astype(np.float32)
        for x in (
            np.concatenate([np.cos(fine_angle), -np.sin(fine_angle)], 1) * norm,
            np.concatenate([np.cos(coarse_angle), -np.sin(coarse_angle)], 1),
        )
    )
    angle = 2 * np.pi * (np.outer(g, k) % G) / G
    out["comb"] = (np.cos(angle).astype(np.float32), np.sin(angle).astype(np.float32))
    return out


def halves(x):
    high = x.astype(BF16)
    low = (x - high.astype(F32)).astype(BF16)
    return high, low


def mm(a, b):
    return jnp.dot(a, b, preferred_element_type=F32)


VM = pl.BlockSpec(memory_space=pltpu.VMEM)
SM = pl.BlockSpec(memory_space=pltpu.SMEM)
HB = pl.BlockSpec(memory_space=pltpu.HBM)


def call(kernel, out_shape, in_specs, out_specs, limit=12, **kw):
    inner = pl.pallas_call(
        kernel,
        out_shape=out_shape,
        in_specs=in_specs,
        out_specs=out_specs,
        compiler_params=pltpu.CompilerParams(vmem_limit_bytes=limit << 20),
        **kw,
    )

    def placed(*args):
        return inner(
            *[x if spec is not HB else pltpu.with_memory_space_constraint(x, pltpu.HBM) for x, spec in zip(args, in_specs)]
        )

    return placed


def fetch(pairs, sems, first=0):
    copies = [pltpu.make_async_copy(src, dst, sems.at[first + i]) for i, (src, dst) in enumerate(pairs)]
    for copy in copies:
        copy.start()
    return copies


def sds(*shape, dtype=F32):
    return jax.ShapeDtypeStruct(shape, dtype)


def vds(*shape, dtype=F32):
    return pltpu.VMEM(shape, dtype)


def hds(*shape, dtype=F32):
    return pltpu.HBM(shape, dtype)


def iota(shape, dim):
    return lax.broadcasted_iota(jnp.int32, shape, dim)


def roll(x, shift, axis):
    return pltpu.roll(x, shift % x.shape[axis], axis)


def lines_kernel(modes, sal, up, down, ends, south, north, sems):
    copies = fetch(
        (
            (modes.at[:, 0:8, :], ends.at[0]),
            (modes.at[:, 8:16, :], ends.at[1]),
            (sal.at[:, 0:8, :], south),
            (sal.at[:, 56:64, :], north),
        ),
        sems,
    )
    for copy in copies:
        copy.wait()
    for dst, rows, end, row in ((up, north, 1, 7), (down, south, 0, 0)):
        dst[0:16, :] = ends[end, :, row, :]
        face = rows[:, row, :]
        for j in range(4):
            dst[16 + 8 * j : 24 + 8 * j, :] = face[:, 256 * j : 256 * j + 256]


def outer_lines(modes, salinity):
    return call(
        lines_kernel,
        (vds(48, 256), vds(48, 256)),
        [HB, HB],
        [VM, VM],
        scratch_shapes=[
            pltpu.VMEM((2, 16, 8, 256), F32),
            pltpu.VMEM((8, 8, FINE), F32),
            pltpu.VMEM((8, 8, FINE), F32),
            pltpu.SemaphoreType.DMA((4,)),
        ],
        name="outer_lines",
    )(modes.reshape(16, 16, 256), salinity)


def pack_kernel(me, modes, sal, chunk, low_face, high_face, modes_a, modes_b, west, east, sems):
    copies = fetch(
        (
            (modes.at[:, 0:128], modes_a),
            (modes.at[:, 128:256], modes_b),
            (sal.at[:, :, 0:128], west),
            (sal.at[:, :, FINE - 128 :], east),
            (sal.at[0], low_face),
            (sal.at[7], high_face),
        ),
        sems,
    )
    for copy in copies[:2]:
        copy.wait()
    zero = jnp.zeros((8, 128), F32)
    for r in range(G):
        chunk[r, 0:16, :] = modes_a[pl.ds(r, 16, stride=16), :]
        chunk[r, 16:32, :] = modes_b[pl.ds(r, 16, stride=16), :]
        chunk[r, 32:40, :] = zero
    row_id = iota((8, 128), 0)

    def column(block, lane):
        tile = zero
        for i in range(4):
            both = jnp.concatenate([block[2 * i], block[2 * i + 1]], 0).T
            line = jnp.broadcast_to(both[lane : lane + 1, :], (8, 128))
            tile = jnp.where(row_id == 4 + i, line, tile)
        return tile

    for copy in copies[2:4]:
        copy.wait()
    chunk[(me[0] + 1) % G, 32:40, :] = column(east, 127)
    chunk[(me[0] + G - 1) % G, 32:40, :] = column(west, 0)
    for copy in copies[4:]:
        copy.wait()


def pack(me, modes, salinity):
    return call(
        pack_kernel,
        (vds(G, 40, 128), hds(64, FINE), hds(64, FINE)),
        [SM, HB, HB],
        [VM, HB, HB],
        scratch_shapes=[
            pltpu.VMEM((256, 128), F32),
            pltpu.VMEM((256, 128), F32),
            pltpu.VMEM((8, 64, 128), F32),
            pltpu.VMEM((8, 64, 128), F32),
            pltpu.SemaphoreType.DMA((6,)),
        ],
        name="pack",
    )(me, modes, salinity)


def tails_kernel(chunk, from_south, from_north, out):
    row_id = iota((8, 128), 0)
    for r in range(G):
        rows = from_south if r < 8 else from_north
        p = r % 8
        tile = chunk[r, 32:40, :]
        parts = (rows[p : p + 1, :128], rows[p : p + 1, 128:], rows[8 + p : 9 + p, :128], rows[8 + p : 9 + p, 128:])
        for i, part in enumerate(parts):
            tile = jnp.where(row_id == i, jnp.broadcast_to(part, (8, 128)), tile)
        out[r, 0:32, :] = chunk[r, 0:32, :]
        out[r, 32:40, :] = tile


def tails(chunk, from_south, from_north):
    return call(tails_kernel, sds(G, 40, 128), [VM] * 3, VM, name="tails")(chunk, from_south, from_north)


def cmul(a, b, c, s):
    return a * c - b * s, a * s + b * c


def four(z):
    (ar, ai), (br, bi), (cr, ci), (dr, di) = z
    t0r, t0i, t1r, t1i = ar + cr, ai + ci, ar - cr, ai - ci
    t2r, t2i, t3r, t3i = br + dr, bi + di, br - dr, bi - di
    return (
        (t0r + t2r, t0i + t2i),
        (t1r - t3i, t1i + t3r),
        (t0r - t2r, t0i - t2i),
        (t1r + t3i, t1i - t3r),
    )


def sixteen(z):
    inner = [four([z[4 * g1 + g0] for g1 in range(4)]) for g0 in range(4)]
    out = [None] * 16
    for r0 in range(4):
        column = []
        for g0 in range(4):
            angle = 2 * math.pi * g0 * r0 / 16
            a, b = inner[g0][r0]
            column.append((a, b) if g0 * r0 == 0 else cmul(a, b, math.cos(angle), math.sin(angle)))
        for r1, value in enumerate(four(column)):
            out[4 * r1 + r0] = value
    return out


def inverse_kernel(recv, twc, tws, inv_high, inv_low, send, left_high, left_low, mid):
    row_id = iota((8, 128), 0)
    lane_id = iota((8, 128), 1)

    def put(r, top, part, value):
        high, low = halves(value)
        left_high[16 * r + 8 * top : 16 * r + 8 * top + 8, 128 * part : 128 * part + 128] = high
        left_low[16 * r + 8 * top : 16 * r + 8 * top + 8, 128 * part : 128 * part + 128] = low

    for h in range(2):
        z = [(recv[g, 16 * h : 16 * h + 8, :], recv[g, 16 * h + 8 : 16 * h + 16, :]) for g in range(G)]
        for r, (a, b) in enumerate(sixteen(z)):
            a, b = cmul(a, b, twc[r, h : h + 1, :], tws[r, h : h + 1, :])
            put(r, 0, h, a)
            put(r, 0, 2 + h, b)
    z = []
    for g in range(G):
        tile = jnp.where(row_id < 4, recv[g, 32:40, :], 0.0)
        z.append((tile, roll(tile, -2, 0)))
    for r, (a, b) in enumerate(sixteen(z)):
        a, b = cmul(a, b, twc[r], tws[r])
        for part, value in ((0, a), (2, b)):
            put(r, 1, part, jnp.where(row_id == 0, value, 0.0))
            put(r, 1, part + 1, jnp.where(row_id == 0, roll(value, -1, 0), 0.0))

    mid[...] = (
        mm(left_high[...], inv_high[...]) + mm(left_low[...], inv_high[...]) + mm(left_high[...], inv_low[...])
    )

    first, second, single = [], [], []
    for r in range(G):
        first.append(mid[16 * r : 16 * r + 8, 0:128])
        second.append(mid[16 * r : 16 * r + 8, 128:256])
        low = mid[16 * r + 8 : 16 * r + 16, 0:128]
        high = mid[16 * r + 8 : 16 * r + 16, 128:256]
        single.append(jnp.where(row_id == 0, low, roll(high, 1, 0)))
    for i in range(8):
        a, b = first[i], second[i]
        c, d = first[i + 8], second[i + 8]
        first[i], second[i], first[i + 8], second[i + 8] = a, c, b, d
        a, c = single[i], single[i + 8]
        single[i] = jnp.where(row_id == 0, a, roll(c, 1, 0))
        single[i + 8] = jnp.where(row_id == 0, roll(a, -1, 0), c)
    for bit in (4, 2, 1):
        upper = (lane_id // (16 * bit)) % 2 == 1
        for tiles in (first, second, single):
            for i in range(G):
                if i & bit:
                    continue
                a, b = tiles[i], tiles[i | bit]
                tiles[i] = jnp.where(upper, roll(b, 16 * bit, 1), a)
                tiles[i | bit] = jnp.where(upper, b, roll(a, -16 * bit, 1))

    left = [roll(second[d], 1, 1) for d in range(G)]
    right = [roll(first[d], 1, 1) for d in range(G)]
    side = [roll(single[d], 5, 1) for d in range(G)]
    for d in range(G):
        before, after = (d - 1) % G, (d + 1) % G
        own = jnp.where(lane_id == 0, left[before], jnp.where(lane_id == 1, right[after], 0.0))
        rim = own + roll(roll(own, -1, 0), 2, 1)
        base = jnp.where(row_id == 2, roll(single[d], 2, 0), 0.0)
        base = jnp.where(row_id == 6, roll(single[d], 5, 0), base)
        base = jnp.where((row_id == 3) & (lane_id == 4), roll(side[before], 2, 0), base)
        base = jnp.where((row_id == 3) & (lane_id == 5), roll(side[after], 3, 0), base)
        for g in range(4):
            tile = jnp.where(row_id < 2, roll(first[d], -2 * g, 0), base)
            tile = jnp.where((row_id == 4) | (row_id == 5), roll(second[d], 4 - 2 * g, 0), tile)
            tile = jnp.where((row_id == 3) & (lane_id < 4), roll(rim, 3 - 2 * g, 0), tile)
            send[16 * g + d] = tile


def inverse(recv, twc, tws, high, low):
    return call(
        inverse_kernel,
        sds(64, 8, 128),
        [VM] * 5,
        VM,
        scratch_shapes=[
            pltpu.VMEM((256, 512), BF16),
            pltpu.VMEM((256, 512), BF16),
            pltpu.VMEM((256, 256), F32),
        ],
        name="inverse",
    )(recv, twc, tws, high, low)


def still_kernel(me, rate_hbm, sal_hbm, zlow_hbm, zhigh_hbm, edge_cols, from_south, from_north, parts_hbm, rate, salinity, zlow, zhigh, parts, sems, out_sems):
    copies = fetch(((rate_hbm, rate), (sal_hbm, salinity), (zlow_hbm, zlow), (zhigh_hbm, zhigh)), sems)
    west_t = edge_cols[(me[0] + G - 1) % G, 32:40, :].T
    east_t = edge_cols[(me[0] + 1) % G, 32:40, :].T
    last_row = iota((8, FINE), 0) == 7
    first_row = iota((8, FINE), 0) == 0
    last_lane = iota((8, 128), 1) == 127
    first_lane = iota((8, 128), 1) == 0

    def outer(rows, l):
        line = jnp.concatenate([rows[16 + 8 * j + l : 17 + 8 * j + l, :] for j in range(4)], 1)
        return jnp.broadcast_to(line, (8, FINE))

    for copy in copies:
        copy.wait()
    stores = []
    for yb in range(8):
        ys = slice(8 * yb, 8 * yb + 8)
        for l in range(8):
            c = salinity[l, ys, :]
            upper = salinity[l + 1, ys, :] if l < 7 else zhigh[ys, :]
            lower = salinity[l - 1, ys, :] if l > 0 else zlow[ys, :]
            if yb < 7:
                north = salinity[l, 8 * yb + 1 : 8 * yb + 9, :]
            else:
                north = jnp.where(last_row, outer(from_north, l), roll(c, -1, 0))
            if yb > 0:
                south = salinity[l, 8 * yb - 1 : 8 * yb + 7, :]
            else:
                south = jnp.where(first_row, outer(from_south, l), roll(c, 1, 0))
            at = (l % 2) * 64 + 8 * yb
            ecol = jnp.broadcast_to(east_t[at : at + 8, 4 + l // 2 : 5 + l // 2], (8, 128))
            wcol = jnp.broadcast_to(west_t[at : at + 8, 4 + l // 2 : 5 + l // 2], (8, 128))
            e = roll(c, -1, 1)
            w = roll(c, 1, 1)
            e = jnp.concatenate([e[:, :-128], jnp.where(last_lane, ecol, e[:, -128:])], 1)
            w = jnp.concatenate([jnp.where(first_lane, wcol, w[:, :128]), w[:, 128:]], 1)
            k = rate[l] * 0.1
            parts[0, l, ys, :] = c + k * (((e + w) + (north + south)) + (upper + lower) - 6.0 * c)
            parts[1, l, ys, :] = (e - w) * 0.05
            parts[2, l, ys, :] = (north - south) * 0.05
            parts[3, l, ys, :] = (upper - lower) * 0.05
        stores.append(pltpu.make_async_copy(parts.at[:, :, ys, :], parts_hbm.at[:, :, ys, :], out_sems.at[yb]))
        stores[-1].start()
    for store in stores:
        store.wait()


def still(me, rate, salinity, zlow, zhigh, recv1, from_south, from_north):
    return call(
        still_kernel,
        hds(4, 8, 64, FINE),
        [SM, HB, HB, HB, HB, VM, VM, VM],
        HB,
        scratch_shapes=[
            pltpu.SMEM((8,), F32),
            pltpu.VMEM((8, 64, FINE), F32),
            pltpu.VMEM((64, FINE), F32),
            pltpu.VMEM((64, FINE), F32),
            pltpu.VMEM((4, 8, 64, FINE), F32),
            pltpu.SemaphoreType.DMA((4,)),
            pltpu.SemaphoreType.DMA((8,)),
        ],
        limit=24,
        name="still",
    )(me, rate, salinity, zlow, zhigh, recv1, from_south, from_north)


CONSTS = ("ym", "edge", "yt", "filt", "fedge", "ref", "cm", "rm")


def fine_kernel(grp_ref, parts_hbm, recv, *rest):
    hbm, (out, spread), rest = rest[:8], rest[8:10], rest[10:]
    (y_high, y_low, side, vel, total, warm, new_sal, parts), consts, (sems, in_sems, out_sems) = (
        rest[:8],
        rest[8:16],
        rest[16:],
    )
    copies = dict(zip(CONSTS, fetch(tuple(zip(hbm, consts)), sems)))
    rows = [slice(8 * yb, 8 * yb + 8) for yb in range(8)]
    loads = fetch([(parts_hbm.at[:, :, ys, :], parts.at[:, :, ys, :]) for ys in rows], in_sems)
    ym, edge, yt, filt, fedge, ref, cm, rm = consts
    grp = grp_ref[0]
    copies["ym"].wait()
    copies["edge"].wait()
    row_id = iota((8, 128), 0)
    lane_id = iota((8, 128), 1)

    def lines(f, q):
        main = [recv[pl.ds(f * 128 + i, 16, stride=8), :] for i in (q, 4 + q, 3)]
        south = recv[pl.ds(pl.multiple_of((f * 16 + 2 * grp + q) * 8, 8), 8), :]
        north = recv[pl.ds(pl.multiple_of((f * 16 + 8 + 2 * grp + q) * 8, 8), 8), :]
        parts = []
        for x, row in zip(main, (2, 6, 3)):
            s, n = roll(south, -row, 0), roll(north, 1 - row, 0)
            if row == 3:
                s, n = roll(s, 2 * q - 4, 1), roll(n, 2 * q - 4, 1)
            tile = jnp.where(row_id == 0, s, jnp.where(row_id == 1, n, 0.0))
            parts.append(jnp.concatenate([x, tile, jnp.zeros((8, 128), F32)], 0))
        return jnp.concatenate(parts, 1)

    def along_y(table, f, q):
        high, low = halves(lines(f, q))
        return mm(table[...], jnp.concatenate([high, low], 0))

    for f in range(3):
        for q in range(2):
            at = slice(64 * (2 * f + q), 64 * (2 * f + q) + 64)
            high, low = halves(along_y(ym, f, q))
            y_high[at, :] = high[:, :256]
            y_low[at, :] = low[:, :256]
            side[at, :] = mm(high[:, 256:], edge[q]) + mm(low[:, 256:], edge[q])
    for name in ("yt", "filt", "fedge"):
        copies[name].wait()
    for q in range(2):
        high, low = halves(along_y(yt, 3, q))
        warm[16 * q : 16 * q + 16, :] = (
            mm(high[:, :256], filt[...])
            + mm(low[:, :256], filt[...])
            + mm(high[:, 256:], fedge[q])
            + mm(low[:, 256:], fedge[q])
        )
    copies["ref"].wait()
    vel[...] = mm(y_high[...], ref[...]) + mm(y_low[...], ref[...])
    vel[:, :128] += side[:, :128]
    vel[:, FINE - 128 :] += side[:, 128:]

    stores = []
    for yb in range(8):
        ys = rows[yb]
        loads[yb].wait()
        for q in range(2):
            vx, vy, vz = (vel[64 * (2 * f + q) + 8 * yb : 64 * (2 * f + q) + 8 * yb + 8, :] for f in range(3))
            acc = None
            for l in range(4 * q, 4 * q + 4):
                new = parts[0, l, ys, :] - (vx * parts[1, l, ys, :] + vy * parts[2, l, ys, :] + vz * parts[3, l, ys, :])
                new_sal[l, ys, :] = new
                acc = new if acc is None else acc + new
            total[64 * q + 8 * yb : 64 * q + 8 * yb + 8, :] = acc
        stores.append(pltpu.make_async_copy(new_sal.at[:, ys, :], out.at[:, ys, :], out_sems.at[yb]))
        stores[-1].start()
    copies["cm"].wait()
    copies["rm"].wait()
    high, low = halves(total[...])
    means = [mm(high[:, at], cm[...]) + mm(low[:, at], cm[...]) for at in (slice(0, 512), slice(512, FINE))]
    high, low = halves(jnp.concatenate(means, 1))
    mean = warm[...] - mm(rm[...], jnp.concatenate([high, low], 0))
    for a in range(G):
        spread[a] = mean
    for store in stores:
        store.wait()


def fine(grp, parts, recv2):
    consts = [jnp.asarray(tables()[name]) for name in CONSTS]
    return call(
        fine_kernel,
        (sds(8, 64, FINE), vds(G, 32, 256)),
        [SM, HB, VM] + [HB] * len(consts),
        [HB, VM],
        scratch_shapes=[
            pltpu.VMEM((384, 256), BF16),
            pltpu.VMEM((384, 256), BF16),
            pltpu.VMEM((384, 256), F32),
            pltpu.VMEM((384, FINE), F32),
            pltpu.VMEM((128, FINE), F32),
            pltpu.VMEM((32, 256), F32),
            pltpu.VMEM((8, 64, FINE), F32),
            pltpu.VMEM((4, 8, 64, FINE), F32),
        ]
        + [pltpu.VMEM(x.shape, x.dtype) for x in consts]
        + [pltpu.SemaphoreType.DMA((n,)) for n in (len(consts), 8, 8)],
        limit=32,
        name="fine",
    )(grp, parts, recv2.reshape(512, 128), *consts)


def stage_kernel(me, inner_hbm, outer_hbm, *rest):
    count = (len(rest) - 5) // 2
    hbm, dst, (high, low, inner, outer, sems) = rest[:count], rest[count : 2 * count], rest[2 * count :]
    copies = fetch(((inner_hbm, inner), (outer_hbm, outer)) + tuple(zip(hbm, dst)), sems)
    turns = (iota((16, 128), 0) * me[0]) % G
    angle = turns.astype(F32) * (2.0 * math.pi / G)
    cos = jnp.concatenate([jnp.cos(angle)] * 2, 1)
    sin = -jnp.concatenate([jnp.sin(angle)] * 2, 1)
    copies[0].wait()
    copies[1].wait()
    real, imag = cmul(inner[:, :256], inner[:, 256:], cos, sin)
    for t in range(G):
        rows = slice(16 * t, 16 * t + 16)
        value = cmul(real, imag, outer[t : t + 1, :256], outer[t : t + 1, 256:])
        for at in range(2):
            high[rows, 256 * at : 256 * at + 256], low[rows, 256 * at : 256 * at + 256] = halves(value[at])
    for copy in copies[2:]:
        copy.wait()


def stage(me):
    t = tables()
    consts = [jnp.asarray(x) for x in (*t["tw"], *t["inv"], *t["comb"])]
    out = call(
        stage_kernel,
        [vds(*x.shape, dtype=x.dtype) for x in consts] + [vds(256, 512, dtype=BF16)] * 2,
        [SM, HB, HB] + [HB] * len(consts),
        [VM] * (len(consts) + 2),
        scratch_shapes=[
            pltpu.VMEM((G, 512), F32),
            pltpu.VMEM((G, 512), F32),
            pltpu.SemaphoreType.DMA((len(consts) + 2,)),
        ],
        name="stage",
    )(me, *map(jnp.asarray, t["fwd"]), *consts)
    return out[0:4], out[4:6], out[6:8]


def forward_kernel(recv, table_high, table_low, comb_cos, comb_sin, out, left_high, left_low, mid):
    for a in range(G):
        high, low = halves(recv[a])
        left_high[32 * a : 32 * a + 32, :] = high
        left_low[32 * a : 32 * a + 32, :] = low
    mid[...] = (
        mm(left_high[...], table_high[...]) + mm(left_low[...], table_high[...]) + mm(left_high[...], table_low[...])
    )
    real = imag = jnp.zeros((32, 256), F32)
    for a in range(G):
        c, s = comb_cos[a : a + 1, :], comb_sin[a : a + 1, :]
        x, y = mid[32 * a : 32 * a + 32, :256], mid[32 * a : 32 * a + 32, 256:]
        real = real + (x * c + y * s)
        imag = imag + (y * c - x * s)
    for g in range(4):
        out[g, 0:32, :] = real
        out[g, 32:64, :] = imag


def forward(recv, high, low, cos, sin):
    return call(
        forward_kernel,
        sds(4, 64, 256),
        [VM] * 5,
        VM,
        scratch_shapes=[
            pltpu.VMEM((512, 256), BF16),
            pltpu.VMEM((512, 256), BF16),
            pltpu.VMEM((512, 512), F32),
        ],
        name="forward",
    )(recv, high, low, cos, sin)


def finish_kernel(me, viscosity, gain, recv, modes, out):
    index = me[0] * W + iota((8, W), 1)
    number = jnp.where(index < NV // 2, index, index - NV).astype(F32)
    wave = (2.0 * math.pi / NV) * number
    damping = jnp.exp(-viscosity[0] * wave * wave)[0:1, :]
    for c in range(2):
        for g in range(4):
            at = slice(128 * c + 32 * g, 128 * c + 32 * g + 32)
            out[at, :] = damping * modes[at, :] + gain[0] * recv[g, 32 * c : 32 * c + 32, :]


def finish(me, viscosity, gain, recv, modes):
    return call(finish_kernel, sds(256, W), [SM, SM, SM, VM, VM], VM, name="finish")(
        me, viscosity, gain, recv, modes
    )


def shifted(array, axis, step):
    count = lax.axis_size(axis)
    return lax.ppermute(array, axis, [(i, (i + step) % count) for i in range(count)])


def per_device(coarse_modes, salinity, viscosity, forcing_gain, diffusivity):
    me = lax.axis_index(GX).astype(jnp.int32).reshape(1)
    grp = lax.axis_index("grp").astype(jnp.int32).reshape(1)
    modes = coarse_modes.reshape(256, 256)
    up, down = outer_lines(modes, salinity)
    from_south = shifted(up, "gy", 1)
    from_north = shifted(down, "gy", -1)
    chunk, low_face, high_face = pack(me, modes, salinity)
    chunk = tails(chunk, from_south, from_north)
    recv1 = lax.all_to_all(chunk, GX, 0, 0, tiled=True)
    inv, comb, weights = stage(me)
    zlow = shifted(high_face, "grp", 1)
    zhigh = shifted(low_face, "grp", -1)
    recv1, zlow, zhigh = lax.optimization_barrier((recv1, zlow, zhigh))
    send2 = inverse(recv1, *inv)
    recv2 = lax.all_to_all(send2, GRP_GX, 0, 0, tiled=True)
    parts = still(me, diffusivity, salinity, zlow, zhigh, recv1, from_south, from_north)
    salinity_next, spread = fine(grp, parts, recv2)
    recv3 = lax.all_to_all(spread, GX, 0, 0, tiled=True)
    recv4 = lax.all_to_all(forward(recv3, *weights, *comb), "grp", 0, 0, tiled=True)
    coarse_next = finish(me, viscosity, forcing_gain, recv4, modes)
    return (salinity_next, coarse_next.reshape(coarse_modes.shape))


def solution(mesh):
    finer = Mesh(
        mesh.devices.reshape(mesh.shape["grp"], 2, 8, mesh.shape["gy"]),
        ("grp", "gx_0", "gx_1", "gy"),
    )
    in_specs = (P("grp", None, None, "gy", GX), P("grp", "gy", GX), P("grp"), P("grp"), P("grp"))
    out_specs = (P("grp", "gy", GX), P("grp", None, None, "gy", GX))
    return jax.shard_map(
        per_device, mesh=finer, in_specs=in_specs, out_specs=out_specs, check_vma=False
    )
```

```python
import functools
import math

import jax
import jax.numpy as jnp
import numpy as np
from jax import lax
from jax.experimental import pallas as pl
from jax.experimental.pallas import tpu as pltpu
from jax.sharding import Mesh
from jax.sharding import PartitionSpec as P

GX = ("gx_0", "gx_1")
GRP_GX = ("grp", "gx_0", "gx_1")
F32 = jnp.float32
BF16 = jnp.bfloat16
G = 16
NV = 4096
W = 256
FINE = 1024


def split_table(table):
    table = np.asarray(table, np.float64)
    high = table.astype(np.float32).astype(jnp.bfloat16)
    low = (table - high.astype(np.float64)).astype(np.float32).astype(jnp.bfloat16)
    return high, low


@functools.cache
def tables():
    out = {}
    k = np.arange(W)
    angle = 2 * np.pi * (np.outer(k, k) % W) / W
    norm = NV ** -0.5
    out["inv"] = split_table(np.concatenate([np.cos(angle), -np.sin(angle)], 0) * norm)
    r = np.arange(G)
    angle = 2 * np.pi * np.outer(r, k) / NV
    twc = np.zeros((G, 8, 128), np.float32)
    tws = np.zeros((G, 8, 128), np.float32)
    twc[:, :2] = np.cos(angle).reshape(G, 2, 128)
    tws[:, :2] = np.sin(angle).reshape(G, 2, 128)
    out["tw"] = (twc, tws)
    lanes = 16 * (k % 16) + k // 16
    order = np.argsort(lanes)
    assert np.array_equal(order, 16 * (k % 16) + k // 16)
    full = np.zeros((W + 2, FINE))
    for n in range(FINE):
        c, s = divmod(n, 4)
        o = (s + 0.5) / 4 - 0.5
        full[c + 1, n] += 1 - abs(o)
        full[c + 1 + (1 if o > 0 else -1), n] += abs(o)
    out["ref"] = full[1:-1][order].astype(jnp.bfloat16)
    edge = np.zeros((2, 128, 256))
    filt = np.zeros((W + 2, W))
    for b in range(W):
        filt[b : b + 3, b] = (0.125, 0.75, 0.125)
    out["filt"] = filt[1:-1][order].astype(jnp.bfloat16)
    fedge = np.zeros((2, 128, 256))
    for q in range(2):
        edge[q, 2 * q, :128] = full[0, :128]
        edge[q, 2 * q + 1, 128:] = full[-1, -128:]
        fedge[q, 2 * q] = filt[0]
        fedge[q, 2 * q + 1] = filt[-1]
    out["edge"] = edge.astype(jnp.bfloat16)
    out["fedge"] = fedge.astype(jnp.bfloat16)
    ym = np.zeros((64, 32))
    yt = np.zeros((16, 32))
    place = lambda c: 16 if c < 0 else 17 if c > 15 else c
    for n in range(64):
        c, s = divmod(n, 4)
        o = (s + 0.5) / 4 - 0.5
        ym[n, c] += 1 - abs(o)
        ym[n, place(c + (1 if o > 0 else -1))] += abs(o)
    for c in range(16):
        yt[c, c] += 0.75
        yt[c, place(c - 1)] += 0.125
        yt[c, place(c + 1)] += 0.125
    out["ym"] = np.concatenate([ym, ym], 1).astype(jnp.bfloat16)
    out["yt"] = np.concatenate([yt, yt], 1).astype(jnp.bfloat16)
    cm = np.zeros((512, 128))
    cm[np.arange(512), np.arange(512) // 4] = 1.0 / 4
    out["cm"] = cm.astype(jnp.bfloat16)
    rm = np.zeros((32, 128))
    rm[np.arange(128) // 4, np.arange(128)] = 1.0 / 16
    out["rm"] = np.concatenate([rm, rm], 1).astype(jnp.bfloat16)
    g = np.arange(G)
    fine_angle = 2 * np.pi * np.outer(g, k) / NV
    coarse_angle = 2 * np.pi * (np.outer(g, k) % W) / W
    out["fwd"] = tuple(
        x.astype(np.float32)
        for x in (
            np.concatenate([np.cos(fine_angle), -np.sin(fine_angle)], 1) * norm,
            np.concatenate([np.cos(coarse_angle), -np.sin(coarse_angle)], 1),
        )
    )
    angle = 2 * np.pi * (np.outer(g, k) % G) / G
    out["comb"] = (np.cos(angle).astype(np.float32), np.sin(angle).astype(np.float32))
    return out


def halves(x):
    high = x.astype(BF16)
    low = (x - high.astype(F32)).astype(BF16)
    return high, low


def mm(a, b):
    return jnp.dot(a, b, preferred_element_type=F32)


VM = pl.BlockSpec(memory_space=pltpu.VMEM)
SM = pl.BlockSpec(memory_space=pltpu.SMEM)
HB = pl.BlockSpec(memory_space=pltpu.HBM)


def call(kernel, out_shape, in_specs, out_specs, limit=12, **kw):
    inner = pl.pallas_call(
        kernel,
        out_shape=out_shape,
        in_specs=in_specs,
        out_specs=out_specs,
        compiler_params=pltpu.CompilerParams(vmem_limit_bytes=limit << 20),
        **kw,
    )

    def placed(*args):
        return inner(
            *[x if spec is not HB else pltpu.with_memory_space_constraint(x, pltpu.HBM) for x, spec in zip(args, in_specs)]
        )

    return placed


def fetch(pairs, sems, first=0):
    copies = [pltpu.make_async_copy(src, dst, sems.at[first + i]) for i, (src, dst) in enumerate(pairs)]
    for copy in copies:
        copy.start()
    return copies


def sds(*shape, dtype=F32):
    return jax.ShapeDtypeStruct(shape, dtype)


def vds(*shape, dtype=F32):
    return pltpu.VMEM(shape, dtype)


def hds(*shape, dtype=F32):
    return pltpu.HBM(shape, dtype)


def iota(shape, dim):
    return lax.broadcasted_iota(jnp.int32, shape, dim)


def roll(x, shift, axis):
    return pltpu.roll(x, shift % x.shape[axis], axis)


def lines_kernel(modes, sal, up, down, ends, south, north, sems):
    copies = fetch(
        (
            (modes.at[:, 0:8, :], ends.at[0]),
            (modes.at[:, 8:16, :], ends.at[1]),
            (sal.at[:, 0:8, :], south),
            (sal.at[:, 56:64, :], north),
        ),
        sems,
    )
    for copy in copies:
        copy.wait()
    for dst, rows, end, row in ((up, north, 1, 7), (down, south, 0, 0)):
        dst[0:16, :] = ends[end, :, row, :]
        face = rows[:, row, :]
        for j in range(4):
            dst[16 + 8 * j : 24 + 8 * j, :] = face[:, 256 * j : 256 * j + 256]


def outer_lines(modes, salinity):
    return call(
        lines_kernel,
        (vds(48, 256), vds(48, 256)),
        [HB, HB],
        [VM, VM],
        scratch_shapes=[
            pltpu.VMEM((2, 16, 8, 256), F32),
            pltpu.VMEM((8, 8, FINE), F32),
            pltpu.VMEM((8, 8, FINE), F32),
            pltpu.SemaphoreType.DMA((4,)),
        ],
        name="outer_lines",
    )(modes.reshape(16, 16, 256), salinity)


def pack_kernel(me, modes, sal, chunk, tail, low_face, high_face, modes_a, modes_b, west, east, faces, lines, sems, out_sems):
    copies = fetch(
        (
            (modes.at[:, 0:128], modes_a),
            (modes.at[:, 128:256], modes_b),
            (sal.at[0], faces.at[0]),
            (sal.at[7], faces.at[1]),
            (sal.at[:, :, 0:128], west),
            (sal.at[:, :, FINE - 128 :], east),
        ),
        sems,
    )
    for copy in copies[:2]:
        copy.wait()
    zero = jnp.zeros((8, 128), F32)
    for r in range(G):
        lines[r, 0:16, :] = modes_a[pl.ds(r, 16, stride=16), :]
        lines[r, 16:32, :] = modes_b[pl.ds(r, 16, stride=16), :]
        tail[r] = zero
    stores = [pltpu.make_async_copy(lines, chunk.at[:, 0:32, :], out_sems.at[0])]
    stores[0].start()
    for i, face in enumerate((low_face, high_face)):
        copies[2 + i].wait()
        stores.append(pltpu.make_async_copy(faces.at[i], face, out_sems.at[1 + i]))
        stores[-1].start()
    row_id = iota((8, 128), 0)

    def column(block, lane):
        tile = zero
        for i in range(4):
            both = jnp.concatenate([block[2 * i], block[2 * i + 1]], 0).T
            line = jnp.broadcast_to(both[lane : lane + 1, :], (8, 128))
            tile = jnp.where(row_id == 4 + i, line, tile)
        return tile

    for copy in copies[4:]:
        copy.wait()
    tail[(me[0] + 1) % G] = column(east, 127)
    tail[(me[0] + G - 1) % G] = column(west, 0)
    for store in stores:
        store.wait()


def pack(me, modes, salinity):
    return call(
        pack_kernel,
        (hds(G, 40, 128), vds(G, 8, 128), hds(64, FINE), hds(64, FINE)),
        [SM, HB, HB],
        [HB, VM, HB, HB],
        scratch_shapes=[
            pltpu.VMEM((256, 128), F32),
            pltpu.VMEM((256, 128), F32),
            pltpu.VMEM((8, 64, 128), F32),
            pltpu.VMEM((8, 64, 128), F32),
            pltpu.VMEM((2, 64, FINE), F32),
            pltpu.VMEM((G, 32, 128), F32),
            pltpu.SemaphoreType.DMA((6,)),
            pltpu.SemaphoreType.DMA((3,)),
        ],
        name="pack",
    )(me, modes, salinity)


def tails_kernel(chunk, tail, from_south, from_north, out, tiles, sem):
    row_id = iota((8, 128), 0)
    for r in range(G):
        rows = from_south if r < 8 else from_north
        p = r % 8
        tile = tail[r]
        parts = (rows[p : p + 1, :128], rows[p : p + 1, 128:], rows[8 + p : 9 + p, :128], rows[8 + p : 9 + p, 128:])
        for i, part in enumerate(parts):
            tile = jnp.where(row_id == i, jnp.broadcast_to(part, (8, 128)), tile)
        tiles[r] = tile
    store = pltpu.make_async_copy(tiles, out.at[:, 32:40, :], sem)
    store.start()
    store.wait()


def tails(chunk, tail, from_south, from_north):
    return call(
        tails_kernel,
        hds(G, 40, 128),
        [HB, VM, VM, VM],
        HB,
        input_output_aliases={0: 0},
        scratch_shapes=[pltpu.VMEM((G, 8, 128), F32), pltpu.SemaphoreType.DMA],
        name="tails",
    )(chunk, tail, from_south, from_north)


def cmul(a, b, c, s):
    return a * c - b * s, a * s + b * c


def four(z):
    (ar, ai), (br, bi), (cr, ci), (dr, di) = z
    t0r, t0i, t1r, t1i = ar + cr, ai + ci, ar - cr, ai - ci
    t2r, t2i, t3r, t3i = br + dr, bi + di, br - dr, bi - di
    return (
        (t0r + t2r, t0i + t2i),
        (t1r - t3i, t1i + t3r),
        (t0r - t2r, t0i - t2i),
        (t1r + t3i, t1i - t3r),
    )


def sixteen(z):
    inner = [four([z[4 * g1 + g0] for g1 in range(4)]) for g0 in range(4)]
    out = [None] * 16
    for r0 in range(4):
        column = []
        for g0 in range(4):
            angle = 2 * math.pi * g0 * r0 / 16
            a, b = inner[g0][r0]
            column.append((a, b) if g0 * r0 == 0 else cmul(a, b, math.cos(angle), math.sin(angle)))
        for r1, value in enumerate(four(column)):
            out[4 * r1 + r0] = value
    return out


def inverse_kernel(recv, twc, tws, inv_high, inv_low, send, left_high, left_low, mid):
    row_id = iota((8, 128), 0)
    lane_id = iota((8, 128), 1)

    def put(r, top, part, value):
        high, low = halves(value)
        left_high[16 * r + 8 * top : 16 * r + 8 * top + 8, 128 * part : 128 * part + 128] = high
        left_low[16 * r + 8 * top : 16 * r + 8 * top + 8, 128 * part : 128 * part + 128] = low

    for h in range(2):
        z = [(recv[g, 16 * h : 16 * h + 8, :], recv[g, 16 * h + 8 : 16 * h + 16, :]) for g in range(G)]
        for r, (a, b) in enumerate(sixteen(z)):
            a, b = cmul(a, b, twc[r, h : h + 1, :], tws[r, h : h + 1, :])
            put(r, 0, h, a)
            put(r, 0, 2 + h, b)
    z = []
    for g in range(G):
        tile = jnp.where(row_id < 4, recv[g, 32:40, :], 0.0)
        z.append((tile, roll(tile, -2, 0)))
    for r, (a, b) in enumerate(sixteen(z)):
        a, b = cmul(a, b, twc[r], tws[r])
        for part, value in ((0, a), (2, b)):
            put(r, 1, part, jnp.where(row_id == 0, value, 0.0))
            put(r, 1, part + 1, jnp.where(row_id == 0, roll(value, -1, 0), 0.0))

    mid[...] = (
        mm(left_high[...], inv_high[...]) + mm(left_low[...], inv_high[...]) + mm(left_high[...], inv_low[...])
    )

    first, second, single = [], [], []
    for r in range(G):
        first.append(mid[16 * r : 16 * r + 8, 0:128])
        second.append(mid[16 * r : 16 * r + 8, 128:256])
        low = mid[16 * r + 8 : 16 * r + 16, 0:128]
        high = mid[16 * r + 8 : 16 * r + 16, 128:256]
        single.append(jnp.where(row_id == 0, low, roll(high, 1, 0)))
    for i in range(8):
        a, b = first[i], second[i]
        c, d = first[i + 8], second[i + 8]
        first[i], second[i], first[i + 8], second[i + 8] = a, c, b, d
        a, c = single[i], single[i + 8]
        single[i] = jnp.where(row_id == 0, a, roll(c, 1, 0))
        single[i + 8] = jnp.where(row_id == 0, roll(a, -1, 0), c)
    for bit in (4, 2, 1):
        upper = (lane_id // (16 * bit)) % 2 == 1
        for tiles in (first, second, single):
            for i in range(G):
                if i & bit:
                    continue
                a, b = tiles[i], tiles[i | bit]
                tiles[i] = jnp.where(upper, roll(b, 16 * bit, 1), a)
                tiles[i | bit] = jnp.where(upper, b, roll(a, -16 * bit, 1))

    left = [roll(second[d], 1, 1) for d in range(G)]
    right = [roll(first[d], 1, 1) for d in range(G)]
    side = [roll(single[d], 5, 1) for d in range(G)]
    for d in range(G):
        before, after = (d - 1) % G, (d + 1) % G
        own = jnp.where(lane_id == 0, left[before], jnp.where(lane_id == 1, right[after], 0.0))
        rim = own + roll(roll(own, -1, 0), 2, 1)
        base = jnp.where(row_id == 2, roll(single[d], 2, 0), 0.0)
        base = jnp.where(row_id == 6, roll(single[d], 5, 0), base)
        base = jnp.where((row_id == 3) & (lane_id == 4), roll(side[before], 2, 0), base)
        base = jnp.where((row_id == 3) & (lane_id == 5), roll(side[after], 3, 0), base)
        for g in range(4):
            tile = jnp.where(row_id < 2, roll(first[d], -2 * g, 0), base)
            tile = jnp.where((row_id == 4) | (row_id == 5), roll(second[d], 4 - 2 * g, 0), tile)
            tile = jnp.where((row_id == 3) & (lane_id < 4), roll(rim, 3 - 2 * g, 0), tile)
            send[16 * g + d] = tile


def inverse(recv, twc, tws, high, low):
    return call(
        inverse_kernel,
        sds(64, 8, 128),
        [VM] * 5,
        VM,
        scratch_shapes=[
            pltpu.VMEM((256, 512), BF16),
            pltpu.VMEM((256, 512), BF16),
            pltpu.VMEM((256, 256), F32),
        ],
        name="inverse",
    )(recv, twc, tws, high, low)


def still_kernel(me, rate_hbm, sal_hbm, zlow_hbm, zhigh_hbm, edge_cols, from_south, from_north, parts_hbm, rate, salinity, zlow, zhigh, parts, sems, out_sems):
    copies = fetch(((rate_hbm, rate), (sal_hbm, salinity), (zlow_hbm, zlow), (zhigh_hbm, zhigh)), sems)
    west_t = edge_cols[(me[0] + G - 1) % G, 32:40, :].T
    east_t = edge_cols[(me[0] + 1) % G, 32:40, :].T
    last_row = iota((8, FINE), 0) == 7
    first_row = iota((8, FINE), 0) == 0
    last_lane = iota((8, 128), 1) == 127
    first_lane = iota((8, 128), 1) == 0

    def outer(rows, l):
        line = jnp.concatenate([rows[16 + 8 * j + l : 17 + 8 * j + l, :] for j in range(4)], 1)
        return jnp.broadcast_to(line, (8, FINE))

    for copy in copies:
        copy.wait()
    stores = []
    for yb in range(8):
        ys = slice(8 * yb, 8 * yb + 8)
        for l in range(8):
            c = salinity[l, ys, :]
            upper = salinity[l + 1, ys, :] if l < 7 else zhigh[ys, :]
            lower = salinity[l - 1, ys, :] if l > 0 else zlow[ys, :]
            if yb < 7:
                north = salinity[l, 8 * yb + 1 : 8 * yb + 9, :]
            else:
                north = jnp.where(last_row, outer(from_north, l), roll(c, -1, 0))
            if yb > 0:
                south = salinity[l, 8 * yb - 1 : 8 * yb + 7, :]
            else:
                south = jnp.where(first_row, outer(from_south, l), roll(c, 1, 0))
            at = (l % 2) * 64 + 8 * yb
            ecol = jnp.broadcast_to(east_t[at : at + 8, 4 + l // 2 : 5 + l // 2], (8, 128))
            wcol = jnp.broadcast_to(west_t[at : at + 8, 4 + l // 2 : 5 + l // 2], (8, 128))
            e = roll(c, -1, 1)
            w = roll(c, 1, 1)
            e = jnp.concatenate([e[:, :-128], jnp.where(last_lane, ecol, e[:, -128:])], 1)
            w = jnp.concatenate([jnp.where(first_lane, wcol, w[:, :128]), w[:, 128:]], 1)
            k = rate[l] * 0.1
            parts[0, l, ys, :] = c + k * (((e + w) + (north + south)) + (upper + lower) - 6.0 * c)
            parts[1, l, ys, :] = (e - w) * 0.05
            parts[2, l, ys, :] = (north - south) * 0.05
            parts[3, l, ys, :] = (upper - lower) * 0.05
        stores.append(pltpu.make_async_copy(parts.at[:, :, ys, :], parts_hbm.at[:, :, ys, :], out_sems.at[yb]))
        stores[-1].start()
    for store in stores:
        store.wait()


def still(me, rate, salinity, zlow, zhigh, recv1, from_south, from_north):
    return call(
        still_kernel,
        hds(4, 8, 64, FINE),
        [SM, HB, HB, HB, HB, VM, VM, VM],
        HB,
        scratch_shapes=[
            pltpu.SMEM((8,), F32),
            pltpu.VMEM((8, 64, FINE), F32),
            pltpu.VMEM((64, FINE), F32),
            pltpu.VMEM((64, FINE), F32),
            pltpu.VMEM((4, 8, 64, FINE), F32),
            pltpu.SemaphoreType.DMA((4,)),
            pltpu.SemaphoreType.DMA((8,)),
        ],
        limit=24,
        name="still",
    )(me, rate, salinity, zlow, zhigh, recv1, from_south, from_north)


CONSTS = ("ym", "edge", "yt", "filt", "fedge", "ref", "cm", "rm")


def fine_kernel(grp_ref, parts_hbm, recv, *rest):
    hbm, (out, spread), rest = rest[:8], rest[8:10], rest[10:]
    (y_high, y_low, side, vel, total, warm, new_sal, parts), consts, (sems, in_sems, out_sems) = (
        rest[:8],
        rest[8:16],
        rest[16:],
    )
    copies = dict(zip(CONSTS, fetch(tuple(zip(hbm, consts)), sems)))
    rows = [slice(8 * yb, 8 * yb + 8) for yb in range(8)]
    loads = fetch([(parts_hbm.at[:, :, ys, :], parts.at[:, :, ys, :]) for ys in rows], in_sems)
    ym, edge, yt, filt, fedge, ref, cm, rm = consts
    grp = grp_ref[0]
    copies["ym"].wait()
    copies["edge"].wait()
    row_id = iota((8, 128), 0)
    lane_id = iota((8, 128), 1)

    def lines(f, q):
        main = [recv[pl.ds(f * 128 + i, 16, stride=8), :] for i in (q, 4 + q, 3)]
        south = recv[pl.ds(pl.multiple_of((f * 16 + 2 * grp + q) * 8, 8), 8), :]
        north = recv[pl.ds(pl.multiple_of((f * 16 + 8 + 2 * grp + q) * 8, 8), 8), :]
        parts = []
        for x, row in zip(main, (2, 6, 3)):
            s, n = roll(south, -row, 0), roll(north, 1 - row, 0)
            if row == 3:
                s, n = roll(s, 2 * q - 4, 1), roll(n, 2 * q - 4, 1)
            tile = jnp.where(row_id == 0, s, jnp.where(row_id == 1, n, 0.0))
            parts.append(jnp.concatenate([x, tile, jnp.zeros((8, 128), F32)], 0))
        return jnp.concatenate(parts, 1)

    def along_y(table, f, q):
        high, low = halves(lines(f, q))
        return mm(table[...], jnp.concatenate([high, low], 0))

    for f in range(3):
        for q in range(2):
            at = slice(64 * (2 * f + q), 64 * (2 * f + q) + 64)
            high, low = halves(along_y(ym, f, q))
            y_high[at, :] = high[:, :256]
            y_low[at, :] = low[:, :256]
            side[at, :] = mm(high[:, 256:], edge[q]) + mm(low[:, 256:], edge[q])
    for name in ("yt", "filt", "fedge"):
        copies[name].wait()
    for q in range(2):
        high, low = halves(along_y(yt, 3, q))
        warm[16 * q : 16 * q + 16, :] = (
            mm(high[:, :256], filt[...])
            + mm(low[:, :256], filt[...])
            + mm(high[:, 256:], fedge[q])
            + mm(low[:, 256:], fedge[q])
        )
    copies["ref"].wait()
    vel[...] = mm(y_high[...], ref[...]) + mm(y_low[...], ref[...])
    vel[:, :128] += side[:, :128]
    vel[:, FINE - 128 :] += side[:, 128:]

    stores = []
    for yb in range(8):
        ys = rows[yb]
        loads[yb].wait()
        for q in range(2):
            vx, vy, vz = (vel[64 * (2 * f + q) + 8 * yb : 64 * (2 * f + q) + 8 * yb + 8, :] for f in range(3))
            acc = None
            for l in range(4 * q, 4 * q + 4):
                new = parts[0, l, ys, :] - (vx * parts[1, l, ys, :] + vy * parts[2, l, ys, :] + vz * parts[3, l, ys, :])
                new_sal[l, ys, :] = new
                acc = new if acc is None else acc + new
            total[64 * q + 8 * yb : 64 * q + 8 * yb + 8, :] = acc
        stores.append(pltpu.make_async_copy(new_sal.at[:, ys, :], out.at[:, ys, :], out_sems.at[yb]))
        stores[-1].start()
    copies["cm"].wait()
    copies["rm"].wait()
    high, low = halves(total[...])
    means = [mm(high[:, at], cm[...]) + mm(low[:, at], cm[...]) for at in (slice(0, 512), slice(512, FINE))]
    high, low = halves(jnp.concatenate(means, 1))
    mean = warm[...] - mm(rm[...], jnp.concatenate([high, low], 0))
    for a in range(G):
        spread[a] = mean
    for store in stores:
        store.wait()


def fine(grp, parts, recv2):
    consts = [jnp.asarray(tables()[name]) for name in CONSTS]
    return call(
        fine_kernel,
        (sds(8, 64, FINE), vds(G, 32, 256)),
        [SM, HB, VM] + [HB] * len(consts),
        [HB, VM],
        scratch_shapes=[
            pltpu.VMEM((384, 256), BF16),
            pltpu.VMEM((384, 256), BF16),
            pltpu.VMEM((384, 256), F32),
            pltpu.VMEM((384, FINE), F32),
            pltpu.VMEM((128, FINE), F32),
            pltpu.VMEM((32, 256), F32),
            pltpu.VMEM((8, 64, FINE), F32),
            pltpu.VMEM((4, 8, 64, FINE), F32),
        ]
        + [pltpu.VMEM(x.shape, x.dtype) for x in consts]
        + [pltpu.SemaphoreType.DMA((n,)) for n in (len(consts), 8, 8)],
        limit=32,
        name="fine",
    )(grp, parts, recv2.reshape(512, 128), *consts)


def stage_kernel(me, inner_hbm, outer_hbm, *rest):
    count = (len(rest) - 5) // 2
    hbm, dst, (high, low, inner, outer, sems) = rest[:count], rest[count : 2 * count], rest[2 * count :]
    copies = fetch(((inner_hbm, inner), (outer_hbm, outer)) + tuple(zip(hbm, dst)), sems)
    turns = (iota((16, 128), 0) * me[0]) % G
    angle = turns.astype(F32) * (2.0 * math.pi / G)
    cos = jnp.concatenate([jnp.cos(angle)] * 2, 1)
    sin = -jnp.concatenate([jnp.sin(angle)] * 2, 1)
    copies[0].wait()
    copies[1].wait()
    real, imag = cmul(inner[:, :256], inner[:, 256:], cos, sin)
    for t in range(G):
        rows = slice(16 * t, 16 * t + 16)
        value = cmul(real, imag, outer[t : t + 1, :256], outer[t : t + 1, 256:])
        for at in range(2):
            high[rows, 256 * at : 256 * at + 256], low[rows, 256 * at : 256 * at + 256] = halves(value[at])
    for copy in copies[2:]:
        copy.wait()


def stage(me):
    t = tables()
    consts = [jnp.asarray(x) for x in (*t["tw"], *t["inv"], *t["comb"])]
    out = call(
        stage_kernel,
        [vds(*x.shape, dtype=x.dtype) for x in consts] + [vds(256, 512, dtype=BF16)] * 2,
        [SM, HB, HB] + [HB] * len(consts),
        [VM] * (len(consts) + 2),
        scratch_shapes=[
            pltpu.VMEM((G, 512), F32),
            pltpu.VMEM((G, 512), F32),
            pltpu.SemaphoreType.DMA((len(consts) + 2,)),
        ],
        name="stage",
    )(me, *map(jnp.asarray, t["fwd"]), *consts)
    return out[0:4], out[4:6], out[6:8]


def forward_kernel(recv, table_high, table_low, comb_cos, comb_sin, out, left_high, left_low, mid):
    for a in range(G):
        high, low = halves(recv[a])
        left_high[32 * a : 32 * a + 32, :] = high
        left_low[32 * a : 32 * a + 32, :] = low
    mid[...] = (
        mm(left_high[...], table_high[...]) + mm(left_low[...], table_high[...]) + mm(left_high[...], table_low[...])
    )
    real = imag = jnp.zeros((32, 256), F32)
    for a in range(G):
        c, s = comb_cos[a : a + 1, :], comb_sin[a : a + 1, :]
        x, y = mid[32 * a : 32 * a + 32, :256], mid[32 * a : 32 * a + 32, 256:]
        real = real + (x * c + y * s)
        imag = imag + (y * c - x * s)
    for g in range(4):
        out[g, 0:32, :] = real
        out[g, 32:64, :] = imag


def forward(recv, high, low, cos, sin):
    return call(
        forward_kernel,
        sds(4, 64, 256),
        [VM] * 5,
        VM,
        scratch_shapes=[
            pltpu.VMEM((512, 256), BF16),
            pltpu.VMEM((512, 256), BF16),
            pltpu.VMEM((512, 512), F32),
        ],
        name="forward",
    )(recv, high, low, cos, sin)


def finish_kernel(me, viscosity, gain, recv, modes, out):
    index = me[0] * W + iota((8, W), 1)
    number = jnp.where(index < NV // 2, index, index - NV).astype(F32)
    wave = (2.0 * math.pi / NV) * number
    damping = jnp.exp(-viscosity[0] * wave * wave)[0:1, :]
    for c in range(2):
        for g in range(4):
            at = slice(128 * c + 32 * g, 128 * c + 32 * g + 32)
            out[at, :] = damping * modes[at, :] + gain[0] * recv[g, 32 * c : 32 * c + 32, :]


def finish(me, viscosity, gain, recv, modes):
    return call(finish_kernel, sds(256, W), [SM, SM, SM, VM, VM], VM, name="finish")(
        me, viscosity, gain, recv, modes
    )


def shifted(array, axis, step):
    count = lax.axis_size(axis)
    return lax.ppermute(array, axis, [(i, (i + step) % count) for i in range(count)])


def per_device(coarse_modes, salinity, viscosity, forcing_gain, diffusivity):
    me = lax.axis_index(GX).astype(jnp.int32).reshape(1)
    grp = lax.axis_index("grp").astype(jnp.int32).reshape(1)
    modes = coarse_modes.reshape(256, 256)
    up, down = outer_lines(modes, salinity)
    from_south = shifted(up, "gy", 1)
    from_north = shifted(down, "gy", -1)
    chunk, tail, low_face, high_face = pack(me, modes, salinity)
    chunk = tails(chunk, tail, from_south, from_north)
    recv1 = lax.all_to_all(chunk, GX, 0, 0, tiled=True)
    inv, comb, weights = stage(me)
    zlow = shifted(high_face, "grp", 1)
    zhigh = shifted(low_face, "grp", -1)
    recv1, zlow, zhigh = lax.optimization_barrier((recv1, zlow, zhigh))
    send2 = inverse(recv1, *inv)
    recv2 = lax.all_to_all(send2, GRP_GX, 0, 0, tiled=True)
    parts = still(me, diffusivity, salinity, zlow, zhigh, recv1, from_south, from_north)
    salinity_next, spread = fine(grp, parts, recv2)
    recv3 = lax.all_to_all(spread, GX, 0, 0, tiled=True)
    recv4 = lax.all_to_all(forward(recv3, *weights, *comb), "grp", 0, 0, tiled=True)
    coarse_next = finish(me, viscosity, forcing_gain, recv4, modes)
    return (salinity_next, coarse_next.reshape(coarse_modes.shape))


def solution(mesh):
    finer = Mesh(
        mesh.devices.reshape(mesh.shape["grp"], 2, 8, mesh.shape["gy"]),
        ("grp", "gx_0", "gx_1", "gy"),
    )
    in_specs = (P("grp", None, None, "gy", GX), P("grp", "gy", GX), P("grp"), P("grp"), P("grp"))
    out_specs = (P("grp", "gy", GX), P("grp", None, None, "gy", GX))
    return jax.shard_map(
        per_device, mesh=finer, in_specs=in_specs, out_specs=out_specs, check_vma=False
    )
```

```python
import functools
import math

import jax
import jax.numpy as jnp
import numpy as np
from jax import lax
from jax.experimental import pallas as pl
from jax.experimental.pallas import tpu as pltpu
from jax.sharding import Mesh
from jax.sharding import PartitionSpec as P

GX = ("gx_0", "gx_1")
GRP_GX = ("grp", "gx_0", "gx_1")
F32 = jnp.float32
BF16 = jnp.bfloat16
G = 16
NV = 4096
W = 256
FINE = 1024


def split_table(table):
    table = np.asarray(table, np.float64)
    high = table.astype(np.float32).astype(jnp.bfloat16)
    low = (table - high.astype(np.float64)).astype(np.float32).astype(jnp.bfloat16)
    return high, low


@functools.cache
def tables():
    out = {}
    k = np.arange(W)
    angle = 2 * np.pi * (np.outer(k, k) % W) / W
    norm = NV ** -0.5
    out["inv"] = split_table(np.concatenate([np.cos(angle), -np.sin(angle)], 0) * norm)
    r = np.arange(G)
    angle = 2 * np.pi * np.outer(r, k) / NV
    twc = np.zeros((G, 8, 128), np.float32)
    tws = np.zeros((G, 8, 128), np.float32)
    twc[:, :2] = np.cos(angle).reshape(G, 2, 128)
    tws[:, :2] = np.sin(angle).reshape(G, 2, 128)
    out["tw"] = (twc, tws)
    lanes = 16 * (k % 16) + k // 16
    order = np.argsort(lanes)
    assert np.array_equal(order, 16 * (k % 16) + k // 16)
    full = np.zeros((W + 2, FINE))
    for n in range(FINE):
        c, s = divmod(n, 4)
        o = (s + 0.5) / 4 - 0.5
        full[c + 1, n] += 1 - abs(o)
        full[c + 1 + (1 if o > 0 else -1), n] += abs(o)
    out["ref"] = full[1:-1][order].astype(jnp.bfloat16)
    edge = np.zeros((2, 128, 256))
    filt = np.zeros((W + 2, W))
    for b in range(W):
        filt[b : b + 3, b] = (0.125, 0.75, 0.125)
    out["filt"] = filt[1:-1][order].astype(jnp.bfloat16)
    fedge = np.zeros((2, 128, 256))
    for q in range(2):
        edge[q, 2 * q, :128] = full[0, :128]
        edge[q, 2 * q + 1, 128:] = full[-1, -128:]
        fedge[q, 2 * q] = filt[0]
        fedge[q, 2 * q + 1] = filt[-1]
    out["edge"] = edge.astype(jnp.bfloat16)
    out["fedge"] = fedge.astype(jnp.bfloat16)
    ym = np.zeros((64, 32))
    yt = np.zeros((16, 32))
    place = lambda c: 16 if c < 0 else 17 if c > 15 else c
    for n in range(64):
        c, s = divmod(n, 4)
        o = (s + 0.5) / 4 - 0.5
        ym[n, c] += 1 - abs(o)
        ym[n, place(c + (1 if o > 0 else -1))] += abs(o)
    for c in range(16):
        yt[c, c] += 0.75
        yt[c, place(c - 1)] += 0.125
        yt[c, place(c + 1)] += 0.125
    out["ym"] = np.concatenate([ym, ym], 1).astype(jnp.bfloat16)
    out["yt"] = np.concatenate([yt, yt], 1).astype(jnp.bfloat16)
    cm = np.zeros((512, 128))
    cm[np.arange(512), np.arange(512) // 4] = 1.0 / 4
    out["cm"] = cm.astype(jnp.bfloat16)
    rm = np.zeros((32, 128))
    rm[np.arange(128) // 4, np.arange(128)] = 1.0 / 16
    out["rm"] = np.concatenate([rm, rm], 1).astype(jnp.bfloat16)
    g = np.arange(G)
    fine_angle = 2 * np.pi * np.outer(g, k) / NV
    coarse_angle = 2 * np.pi * (np.outer(g, k) % W) / W
    out["fwd"] = tuple(
        x.astype(np.float32)
        for x in (
            np.concatenate([np.cos(fine_angle), -np.sin(fine_angle)], 1) * norm,
            np.concatenate([np.cos(coarse_angle), -np.sin(coarse_angle)], 1),
        )
    )
    angle = 2 * np.pi * (np.outer(g, k) % G) / G
    out["comb"] = (np.cos(angle).astype(np.float32), np.sin(angle).astype(np.float32))
    return out


def halves(x):
    high = x.astype(BF16)
    low = (x - high.astype(F32)).astype(BF16)
    return high, low


def mm(a, b):
    return jnp.dot(a, b, preferred_element_type=F32)


VM = pl.BlockSpec(memory_space=pltpu.VMEM)
SM = pl.BlockSpec(memory_space=pltpu.SMEM)
HB = pl.BlockSpec(memory_space=pltpu.HBM)


def call(kernel, out_shape, in_specs, out_specs, limit=12, **kw):
    inner = pl.pallas_call(
        kernel,
        out_shape=out_shape,
        in_specs=in_specs,
        out_specs=out_specs,
        compiler_params=pltpu.CompilerParams(vmem_limit_bytes=limit << 20),
        **kw,
    )

    def placed(*args):
        return inner(
            *[x if spec is not HB else pltpu.with_memory_space_constraint(x, pltpu.HBM) for x, spec in zip(args, in_specs)]
        )

    return placed


def fetch(pairs, sems, first=0):
    copies = [pltpu.make_async_copy(src, dst, sems.at[first + i]) for i, (src, dst) in enumerate(pairs)]
    for copy in copies:
        copy.start()
    return copies


def sds(*shape, dtype=F32):
    return jax.ShapeDtypeStruct(shape, dtype)


def vds(*shape, dtype=F32):
    return pltpu.VMEM(shape, dtype)


def hds(*shape, dtype=F32):
    return pltpu.HBM(shape, dtype)


def iota(shape, dim):
    return lax.broadcasted_iota(jnp.int32, shape, dim)


def roll(x, shift, axis):
    return pltpu.roll(x, shift % x.shape[axis], axis)


def lines_kernel(modes, sal, up, down, ends, south, north, sems):
    copies = fetch(
        (
            (modes.at[:, 0:8, :], ends.at[0]),
            (modes.at[:, 8:16, :], ends.at[1]),
            (sal.at[:, 0:8, :], south),
            (sal.at[:, 56:64, :], north),
        ),
        sems,
    )
    for copy in copies:
        copy.wait()
    for dst, rows, end, row in ((up, north, 1, 7), (down, south, 0, 0)):
        dst[0:16, :] = ends[end, :, row, :]
        face = rows[:, row, :]
        for j in range(4):
            dst[16 + 8 * j : 24 + 8 * j, :] = face[:, 256 * j : 256 * j + 256]


def outer_lines(modes, salinity):
    return call(
        lines_kernel,
        (vds(48, 256), vds(48, 256)),
        [HB, HB],
        [VM, VM],
        scratch_shapes=[
            pltpu.VMEM((2, 16, 8, 256), F32),
            pltpu.VMEM((8, 8, FINE), F32),
            pltpu.VMEM((8, 8, FINE), F32),
            pltpu.SemaphoreType.DMA((4,)),
        ],
        name="outer_lines",
    )(modes.reshape(16, 16, 256), salinity)


def pack_kernel(me, modes, sal, chunk, tail, low_face, high_face, modes_a, modes_b, west, east, faces, lines, sems, out_sems):
    copies = fetch(
        (
            (modes.at[:, 0:128], modes_a),
            (modes.at[:, 128:256], modes_b),
            (sal.at[0], faces.at[0]),
            (sal.at[7], faces.at[1]),
            (sal.at[:, :, 0:128], west),
            (sal.at[:, :, FINE - 128 :], east),
        ),
        sems,
    )
    for copy in copies[:2]:
        copy.wait()
    zero = jnp.zeros((8, 128), F32)
    for r in range(G):
        lines[r, 0:16, :] = modes_a[pl.ds(r, 16, stride=16), :]
        lines[r, 16:32, :] = modes_b[pl.ds(r, 16, stride=16), :]
        tail[r] = zero
    stores = [pltpu.make_async_copy(lines, chunk.at[:, 0:32, :], out_sems.at[0])]
    stores[0].start()
    for i, face in enumerate((low_face, high_face)):
        copies[2 + i].wait()
        stores.append(pltpu.make_async_copy(faces.at[i], face, out_sems.at[1 + i]))
        stores[-1].start()
    row_id = iota((8, 128), 0)

    def column(block, lane):
        tile = zero
        for i in range(4):
            both = jnp.concatenate([block[2 * i], block[2 * i + 1]], 0).T
            line = jnp.broadcast_to(both[lane : lane + 1, :], (8, 128))
            tile = jnp.where(row_id == 4 + i, line, tile)
        return tile

    for copy in copies[4:]:
        copy.wait()
    tail[(me[0] + 1) % G] = column(east, 127)
    tail[(me[0] + G - 1) % G] = column(west, 0)
    for store in stores:
        store.wait()


def pack(me, modes, salinity):
    return call(
        pack_kernel,
        (hds(G, 40, 128), vds(G, 8, 128), hds(64, FINE), hds(64, FINE)),
        [SM, HB, HB],
        [HB, VM, HB, HB],
        scratch_shapes=[
            pltpu.VMEM((256, 128), F32),
            pltpu.VMEM((256, 128), F32),
            pltpu.VMEM((8, 64, 128), F32),
            pltpu.VMEM((8, 64, 128), F32),
            pltpu.VMEM((2, 64, FINE), F32),
            pltpu.VMEM((G, 32, 128), F32),
            pltpu.SemaphoreType.DMA((6,)),
            pltpu.SemaphoreType.DMA((3,)),
        ],
        name="pack",
    )(me, modes, salinity)


def tails_kernel(chunk, tail, from_south, from_north, out, tiles, sem):
    row_id = iota((8, 128), 0)
    for r in range(G):
        rows = from_south if r < 8 else from_north
        p = r % 8
        tile = tail[r]
        parts = (rows[p : p + 1, :128], rows[p : p + 1, 128:], rows[8 + p : 9 + p, :128], rows[8 + p : 9 + p, 128:])
        for i, part in enumerate(parts):
            tile = jnp.where(row_id == i, jnp.broadcast_to(part, (8, 128)), tile)
        tiles[r] = tile
    store = pltpu.make_async_copy(tiles, out.at[:, 32:40, :], sem)
    store.start()
    store.wait()


def tails(chunk, tail, from_south, from_north):
    return call(
        tails_kernel,
        hds(G, 40, 128),
        [HB, VM, VM, VM],
        HB,
        input_output_aliases={0: 0},
        scratch_shapes=[pltpu.VMEM((G, 8, 128), F32), pltpu.SemaphoreType.DMA],
        name="tails",
    )(chunk, tail, from_south, from_north)


def cmul(a, b, c, s):
    return a * c - b * s, a * s + b * c


def four(z):
    (ar, ai), (br, bi), (cr, ci), (dr, di) = z
    t0r, t0i, t1r, t1i = ar + cr, ai + ci, ar - cr, ai - ci
    t2r, t2i, t3r, t3i = br + dr, bi + di, br - dr, bi - di
    return (
        (t0r + t2r, t0i + t2i),
        (t1r - t3i, t1i + t3r),
        (t0r - t2r, t0i - t2i),
        (t1r + t3i, t1i - t3r),
    )


def sixteen(z):
    inner = [four([z[4 * g1 + g0] for g1 in range(4)]) for g0 in range(4)]
    out = [None] * 16
    for r0 in range(4):
        column = []
        for g0 in range(4):
            angle = 2 * math.pi * g0 * r0 / 16
            a, b = inner[g0][r0]
            column.append((a, b) if g0 * r0 == 0 else cmul(a, b, math.cos(angle), math.sin(angle)))
        for r1, value in enumerate(four(column)):
            out[4 * r1 + r0] = value
    return out


def inverse_kernel(recv, twc, tws, inv_high, inv_low, send, left_high, left_low, mid):
    row_id = iota((8, 128), 0)
    lane_id = iota((8, 128), 1)

    def put(r, top, part, value):
        high, low = halves(value)
        left_high[16 * r + 8 * top : 16 * r + 8 * top + 8, 128 * part : 128 * part + 128] = high
        left_low[16 * r + 8 * top : 16 * r + 8 * top + 8, 128 * part : 128 * part + 128] = low

    for h in range(2):
        z = [(recv[g, 16 * h : 16 * h + 8, :], recv[g, 16 * h + 8 : 16 * h + 16, :]) for g in range(G)]
        for r, (a, b) in enumerate(sixteen(z)):
            a, b = cmul(a, b, twc[r, h : h + 1, :], tws[r, h : h + 1, :])
            put(r, 0, h, a)
            put(r, 0, 2 + h, b)
    z = []
    for g in range(G):
        tile = jnp.where(row_id < 4, recv[g, 32:40, :], 0.0)
        z.append((tile, roll(tile, -2, 0)))
    for r, (a, b) in enumerate(sixteen(z)):
        a, b = cmul(a, b, twc[r], tws[r])
        for part, value in ((0, a), (2, b)):
            put(r, 1, part, jnp.where(row_id == 0, value, 0.0))
            put(r, 1, part + 1, jnp.where(row_id == 0, roll(value, -1, 0), 0.0))

    mid[...] = (
        mm(left_high[...], inv_high[...]) + mm(left_low[...], inv_high[...]) + mm(left_high[...], inv_low[...])
    )

    first, second, single = [], [], []
    for r in range(G):
        first.append(mid[16 * r : 16 * r + 8, 0:128])
        second.append(mid[16 * r : 16 * r + 8, 128:256])
        low = mid[16 * r + 8 : 16 * r + 16, 0:128]
        high = mid[16 * r + 8 : 16 * r + 16, 128:256]
        single.append(jnp.where(row_id == 0, low, roll(high, 1, 0)))
    for i in range(8):
        a, b = first[i], second[i]
        c, d = first[i + 8], second[i + 8]
        first[i], second[i], first[i + 8], second[i + 8] = a, c, b, d
        a, c = single[i], single[i + 8]
        single[i] = jnp.where(row_id == 0, a, roll(c, 1, 0))
        single[i + 8] = jnp.where(row_id == 0, roll(a, -1, 0), c)
    for bit in (4, 2, 1):
        upper = (lane_id // (16 * bit)) % 2 == 1
        for tiles in (first, second, single):
            for i in range(G):
                if i & bit:
                    continue
                a, b = tiles[i], tiles[i | bit]
                tiles[i] = jnp.where(upper, roll(b, 16 * bit, 1), a)
                tiles[i | bit] = jnp.where(upper, b, roll(a, -16 * bit, 1))

    left = [roll(second[d], 1, 1) for d in range(G)]
    right = [roll(first[d], 1, 1) for d in range(G)]
    side = [roll(single[d], 5, 1) for d in range(G)]
    for d in range(G):
        before, after = (d - 1) % G, (d + 1) % G
        own = jnp.where(lane_id == 0, left[before], jnp.where(lane_id == 1, right[after], 0.0))
        rim = own + roll(roll(own, -1, 0), 2, 1)
        base = jnp.where(row_id == 2, roll(single[d], 2, 0), 0.0)
        base = jnp.where(row_id == 6, roll(single[d], 5, 0), base)
        base = jnp.where((row_id == 3) & (lane_id == 4), roll(side[before], 2, 0), base)
        base = jnp.where((row_id == 3) & (lane_id == 5), roll(side[after], 3, 0), base)
        for g in range(4):
            tile = jnp.where(row_id < 2, roll(first[d], -2 * g, 0), base)
            tile = jnp.where((row_id == 4) | (row_id == 5), roll(second[d], 4 - 2 * g, 0), tile)
            tile = jnp.where((row_id == 3) & (lane_id < 4), roll(rim, 3 - 2 * g, 0), tile)
            send[16 * g + d] = tile


def inverse(recv, twc, tws, high, low):
    return call(
        inverse_kernel,
        sds(64, 8, 128),
        [VM] * 5,
        VM,
        scratch_shapes=[
            pltpu.VMEM((256, 512), BF16),
            pltpu.VMEM((256, 512), BF16),
            pltpu.VMEM((256, 256), F32),
        ],
        name="inverse",
    )(recv, twc, tws, high, low)


EARLY = ("ym", "edge")
LATE = ("ref", "yt", "filt", "fedge", "cm", "rm")


def still_kernel(me, rate_hbm, sal_hbm, zlow_hbm, zhigh_hbm, edge_cols, from_south, from_north, *rest):
    count = len(EARLY)
    hbm, parts_hbm, kept, rest = rest[:count], rest[count], rest[count + 1 : 2 * count + 1], rest[2 * count + 1 :]
    rate, salinity, zlow, zhigh, parts, sems, const_sems, out_sems = rest
    copies = fetch(((rate_hbm, rate), (sal_hbm, salinity), (zlow_hbm, zlow), (zhigh_hbm, zhigh)), sems)
    stores = fetch(tuple(zip(hbm, kept)), const_sems)
    west_t = edge_cols[(me[0] + G - 1) % G, 32:40, :].T
    east_t = edge_cols[(me[0] + 1) % G, 32:40, :].T
    last_row = iota((8, FINE), 0) == 7
    first_row = iota((8, FINE), 0) == 0
    last_lane = iota((8, 128), 1) == 127
    first_lane = iota((8, 128), 1) == 0

    def outer(rows, l):
        line = jnp.concatenate([rows[16 + 8 * j + l : 17 + 8 * j + l, :] for j in range(4)], 1)
        return jnp.broadcast_to(line, (8, FINE))

    for copy in copies:
        copy.wait()
    for yb in range(8):
        ys = slice(8 * yb, 8 * yb + 8)
        for l in range(8):
            c = salinity[l, ys, :]
            upper = salinity[l + 1, ys, :] if l < 7 else zhigh[ys, :]
            lower = salinity[l - 1, ys, :] if l > 0 else zlow[ys, :]
            if yb < 7:
                north = salinity[l, 8 * yb + 1 : 8 * yb + 9, :]
            else:
                north = jnp.where(last_row, outer(from_north, l), roll(c, -1, 0))
            if yb > 0:
                south = salinity[l, 8 * yb - 1 : 8 * yb + 7, :]
            else:
                south = jnp.where(first_row, outer(from_south, l), roll(c, 1, 0))
            at = (l % 2) * 64 + 8 * yb
            ecol = jnp.broadcast_to(east_t[at : at + 8, 4 + l // 2 : 5 + l // 2], (8, 128))
            wcol = jnp.broadcast_to(west_t[at : at + 8, 4 + l // 2 : 5 + l // 2], (8, 128))
            e = roll(c, -1, 1)
            w = roll(c, 1, 1)
            e = jnp.concatenate([e[:, :-128], jnp.where(last_lane, ecol, e[:, -128:])], 1)
            w = jnp.concatenate([jnp.where(first_lane, wcol, w[:, :128]), w[:, 128:]], 1)
            k = rate[l] * 0.1
            parts[0, l, ys, :] = c + k * (((e + w) + (north + south)) + (upper + lower) - 6.0 * c)
            parts[1, l, ys, :] = (e - w) * 0.05
            parts[2, l, ys, :] = (north - south) * 0.05
            parts[3, l, ys, :] = (upper - lower) * 0.05
        stores.append(pltpu.make_async_copy(parts.at[:, :, ys, :], parts_hbm.at[:, :, ys, :], out_sems.at[yb]))
        stores[-1].start()
    for store in stores:
        store.wait()


def still(me, rate, salinity, zlow, zhigh, recv1, from_south, from_north):
    consts = [jnp.asarray(tables()[name]) for name in EARLY]
    return call(
        still_kernel,
        [hds(4, 8, 64, FINE)] + [vds(*x.shape, dtype=x.dtype) for x in consts],
        [SM, HB, HB, HB, HB, VM, VM, VM] + [HB] * len(consts),
        [HB] + [VM] * len(consts),
        scratch_shapes=[
            pltpu.SMEM((8,), F32),
            pltpu.VMEM((8, 64, FINE), F32),
            pltpu.VMEM((64, FINE), F32),
            pltpu.VMEM((64, FINE), F32),
            pltpu.VMEM((4, 8, 64, FINE), F32),
            pltpu.SemaphoreType.DMA((4,)),
            pltpu.SemaphoreType.DMA((len(consts),)),
            pltpu.SemaphoreType.DMA((8,)),
        ],
        limit=24,
        name="still",
    )(me, rate, salinity, zlow, zhigh, recv1, from_south, from_north, *consts)


def fine_kernel(grp_ref, parts_hbm, recv, ym, edge, *rest):
    count = len(LATE)
    hbm, (out, spread), consts, rest = rest[:count], rest[count : count + 2], rest[count + 2 : 2 * count + 2], rest[2 * count + 2 :]
    y_high, y_low, side, vel, total, warm, parts, in_sems, sems = rest
    ref, yt, filt, fedge, cm, rm = consts
    copies = dict(zip(LATE, fetch(tuple(zip(hbm, consts)), sems)))
    rows = [slice(8 * yb, 8 * yb + 8) for yb in range(8)]
    loads = fetch([(parts_hbm.at[:, :, ys, :], parts.at[:, :, ys, :]) for ys in rows], in_sems)
    grp = grp_ref[0]
    row_id = iota((8, 128), 0)
    lane_id = iota((8, 128), 1)

    def lines(f, q):
        main = [recv[pl.ds(f * 128 + i, 16, stride=8), :] for i in (q, 4 + q, 3)]
        south = recv[pl.ds(pl.multiple_of((f * 16 + 2 * grp + q) * 8, 8), 8), :]
        north = recv[pl.ds(pl.multiple_of((f * 16 + 8 + 2 * grp + q) * 8, 8), 8), :]
        parts = []
        for x, row in zip(main, (2, 6, 3)):
            s, n = roll(south, -row, 0), roll(north, 1 - row, 0)
            if row == 3:
                s, n = roll(s, 2 * q - 4, 1), roll(n, 2 * q - 4, 1)
            tile = jnp.where(row_id == 0, s, jnp.where(row_id == 1, n, 0.0))
            parts.append(jnp.concatenate([x, tile, jnp.zeros((8, 128), F32)], 0))
        return jnp.concatenate(parts, 1)

    def along_y(table, f, q):
        high, low = halves(lines(f, q))
        return mm(table[...], jnp.concatenate([high, low], 0))

    for f in range(3):
        for q in range(2):
            at = slice(64 * (2 * f + q), 64 * (2 * f + q) + 64)
            high, low = halves(along_y(ym, f, q))
            y_high[at, :] = high[:, :256]
            y_low[at, :] = low[:, :256]
            side[at, :] = mm(high[:, 256:], edge[q]) + mm(low[:, 256:], edge[q])
    for name in ("yt", "filt", "fedge"):
        copies[name].wait()
    for q in range(2):
        high, low = halves(along_y(yt, 3, q))
        warm[16 * q : 16 * q + 16, :] = (
            mm(high[:, :256], filt[...])
            + mm(low[:, :256], filt[...])
            + mm(high[:, 256:], fedge[q])
            + mm(low[:, 256:], fedge[q])
        )
    copies["ref"].wait()
    vel[...] = mm(y_high[...], ref[...]) + mm(y_low[...], ref[...])
    vel[:, :128] += side[:, :128]
    vel[:, FINE - 128 :] += side[:, 128:]

    for yb in range(8):
        ys = rows[yb]
        loads[yb].wait()
        for q in range(2):
            vx, vy, vz = (vel[64 * (2 * f + q) + 8 * yb : 64 * (2 * f + q) + 8 * yb + 8, :] for f in range(3))
            acc = None
            for l in range(4 * q, 4 * q + 4):
                new = parts[0, l, ys, :] - (vx * parts[1, l, ys, :] + vy * parts[2, l, ys, :] + vz * parts[3, l, ys, :])
                out[l, ys, :] = new
                acc = new if acc is None else acc + new
            total[64 * q + 8 * yb : 64 * q + 8 * yb + 8, :] = acc
    copies["cm"].wait()
    copies["rm"].wait()
    high, low = halves(total[...])
    means = [mm(high[:, at], cm[...]) + mm(low[:, at], cm[...]) for at in (slice(0, 512), slice(512, FINE))]
    high, low = halves(jnp.concatenate(means, 1))
    mean = warm[...] - mm(rm[...], jnp.concatenate([high, low], 0))
    for a in range(G):
        spread[a] = mean


def fine(grp, parts, recv2, early):
    late = [jnp.asarray(tables()[name]) for name in LATE]
    return call(
        fine_kernel,
        (vds(8, 64, FINE), vds(G, 32, 256)),
        [SM, HB, VM] + [VM] * len(early) + [HB] * len(late),
        [VM, VM],
        scratch_shapes=[pltpu.VMEM(x.shape, x.dtype) for x in late]
        + [
            pltpu.VMEM((384, 256), BF16),
            pltpu.VMEM((384, 256), BF16),
            pltpu.VMEM((384, 256), F32),
            pltpu.VMEM((384, FINE), F32),
            pltpu.VMEM((128, FINE), F32),
            pltpu.VMEM((32, 256), F32),
            pltpu.VMEM((4, 8, 64, FINE), F32),
            pltpu.SemaphoreType.DMA((8,)),
            pltpu.SemaphoreType.DMA((len(late),)),
        ],
        limit=24,
        name="fine",
    )(grp, parts, recv2.reshape(512, 128), *early, *late)


def stage_kernel(me, inner_hbm, outer_hbm, *rest):
    count = (len(rest) - 5) // 2
    hbm, dst, (high, low, inner, outer, sems) = rest[:count], rest[count : 2 * count], rest[2 * count :]
    copies = fetch(((inner_hbm, inner), (outer_hbm, outer)) + tuple(zip(hbm, dst)), sems)
    turns = (iota((16, 128), 0) * me[0]) % G
    angle = turns.astype(F32) * (2.0 * math.pi / G)
    cos = jnp.concatenate([jnp.cos(angle)] * 2, 1)
    sin = -jnp.concatenate([jnp.sin(angle)] * 2, 1)
    copies[0].wait()
    copies[1].wait()
    real, imag = cmul(inner[:, :256], inner[:, 256:], cos, sin)
    for t in range(G):
        rows = slice(16 * t, 16 * t + 16)
        value = cmul(real, imag, outer[t : t + 1, :256], outer[t : t + 1, 256:])
        for at in range(2):
            high[rows, 256 * at : 256 * at + 256], low[rows, 256 * at : 256 * at + 256] = halves(value[at])
    for copy in copies[2:]:
        copy.wait()


def stage(me):
    t = tables()
    consts = [jnp.asarray(x) for x in (*t["tw"], *t["inv"], *t["comb"])]
    out = call(
        stage_kernel,
        [vds(*x.shape, dtype=x.dtype) for x in consts] + [vds(256, 512, dtype=BF16)] * 2,
        [SM, HB, HB] + [HB] * len(consts),
        [VM] * (len(consts) + 2),
        scratch_shapes=[
            pltpu.VMEM((G, 512), F32),
            pltpu.VMEM((G, 512), F32),
            pltpu.SemaphoreType.DMA((len(consts) + 2,)),
        ],
        name="stage",
    )(me, *map(jnp.asarray, t["fwd"]), *consts)
    return out[0:4], out[4:6], out[6:8]


def forward_kernel(recv, table_high, table_low, comb_cos, comb_sin, out, left_high, left_low, mid):
    for a in range(G):
        high, low = halves(recv[a])
        left_high[32 * a : 32 * a + 32, :] = high
        left_low[32 * a : 32 * a + 32, :] = low
    mid[...] = (
        mm(left_high[...], table_high[...]) + mm(left_low[...], table_high[...]) + mm(left_high[...], table_low[...])
    )
    real = imag = jnp.zeros((32, 256), F32)
    for a in range(G):
        c, s = comb_cos[a : a + 1, :], comb_sin[a : a + 1, :]
        x, y = mid[32 * a : 32 * a + 32, :256], mid[32 * a : 32 * a + 32, 256:]
        real = real + (x * c + y * s)
        imag = imag + (y * c - x * s)
    for g in range(4):
        out[g, 0:32, :] = real
        out[g, 32:64, :] = imag


def forward(recv, high, low, cos, sin):
    return call(
        forward_kernel,
        sds(4, 64, 256),
        [VM] * 5,
        VM,
        scratch_shapes=[
            pltpu.VMEM((512, 256), BF16),
            pltpu.VMEM((512, 256), BF16),
            pltpu.VMEM((512, 512), F32),
        ],
        name="forward",
    )(recv, high, low, cos, sin)


def finish_kernel(me, viscosity, gain, recv, modes, out):
    index = me[0] * W + iota((8, W), 1)
    number = jnp.where(index < NV // 2, index, index - NV).astype(F32)
    wave = (2.0 * math.pi / NV) * number
    damping = jnp.exp(-viscosity[0] * wave * wave)[0:1, :]
    for c in range(2):
        for g in range(4):
            at = slice(128 * c + 32 * g, 128 * c + 32 * g + 32)
            out[at, :] = damping * modes[at, :] + gain[0] * recv[g, 32 * c : 32 * c + 32, :]


def finish(me, viscosity, gain, recv, modes):
    return call(finish_kernel, sds(256, W), [SM, SM, SM, VM, VM], VM, name="finish")(
        me, viscosity, gain, recv, modes
    )


def shifted(array, axis, step):
    count = lax.axis_size(axis)
    return lax.ppermute(array, axis, [(i, (i + step) % count) for i in range(count)])


def per_device(coarse_modes, salinity, viscosity, forcing_gain, diffusivity):
    me = lax.axis_index(GX).astype(jnp.int32).reshape(1)
    grp = lax.axis_index("grp").astype(jnp.int32).reshape(1)
    modes = coarse_modes.reshape(256, 256)
    up, down = outer_lines(modes, salinity)
    from_south = shifted(up, "gy", 1)
    from_north = shifted(down, "gy", -1)
    chunk, tail, low_face, high_face = pack(me, modes, salinity)
    chunk = tails(chunk, tail, from_south, from_north)
    recv1 = lax.all_to_all(chunk, GX, 0, 0, tiled=True)
    inv, comb, weights = stage(me)
    zlow = shifted(high_face, "grp", 1)
    zhigh = shifted(low_face, "grp", -1)
    recv1, zlow, zhigh = lax.optimization_barrier((recv1, zlow, zhigh))
    send2 = inverse(recv1, *inv)
    recv2 = lax.all_to_all(send2, GRP_GX, 0, 0, tiled=True)
    parts, *early = still(me, diffusivity, salinity, zlow, zhigh, recv1, from_south, from_north)
    salinity_next, spread = fine(grp, parts, recv2, early)
    recv3 = lax.all_to_all(spread, GX, 0, 0, tiled=True)
    recv4 = lax.all_to_all(forward(recv3, *weights, *comb), "grp", 0, 0, tiled=True)
    coarse_next = finish(me, viscosity, forcing_gain, recv4, modes)
    return (salinity_next, coarse_next.reshape(coarse_modes.shape))


def solution(mesh):
    finer = Mesh(
        mesh.devices.reshape(mesh.shape["grp"], 2, 8, mesh.shape["gy"]),
        ("grp", "gx_0", "gx_1", "gy"),
    )
    in_specs = (P("grp", None, None, "gy", GX), P("grp", "gy", GX), P("grp"), P("grp"), P("grp"))
    out_specs = (P("grp", "gy", GX), P("grp", None, None, "gy", GX))
    return jax.shard_map(
        per_device, mesh=finer, in_specs=in_specs, out_specs=out_specs, check_vma=False
    )
```

```python
import functools
import math

import jax
import jax.numpy as jnp
import numpy as np
from jax import lax
from jax.experimental import pallas as pl
from jax.experimental.pallas import tpu as pltpu
from jax.sharding import Mesh
from jax.sharding import PartitionSpec as P

GX = ("gx_0", "gx_1")
GRP_GX = ("grp", "gx_0", "gx_1")
F32 = jnp.float32
BF16 = jnp.bfloat16
G = 16
NV = 4096
W = 256
FINE = 1024


def split_table(table):
    table = np.asarray(table, np.float64)
    high = table.astype(np.float32).astype(jnp.bfloat16)
    low = (table - high.astype(np.float64)).astype(np.float32).astype(jnp.bfloat16)
    return high, low


@functools.cache
def tables():
    out = {}
    k = np.arange(W)
    angle = 2 * np.pi * (np.outer(k, k) % W) / W
    norm = NV ** -0.5
    out["inv"] = split_table(np.concatenate([np.cos(angle), -np.sin(angle)], 0) * norm)
    r = np.arange(G)
    angle = 2 * np.pi * np.outer(r, k) / NV
    twc = np.zeros((G, 8, 128), np.float32)
    tws = np.zeros((G, 8, 128), np.float32)
    twc[:, :2] = np.cos(angle).reshape(G, 2, 128)
    tws[:, :2] = np.sin(angle).reshape(G, 2, 128)
    out["tw"] = (twc, tws)
    lanes = 16 * (k % 16) + k // 16
    order = np.argsort(lanes)
    assert np.array_equal(order, 16 * (k % 16) + k // 16)
    full = np.zeros((W + 2, FINE))
    for n in range(FINE):
        c, s = divmod(n, 4)
        o = (s + 0.5) / 4 - 0.5
        full[c + 1, n] += 1 - abs(o)
        full[c + 1 + (1 if o > 0 else -1), n] += abs(o)
    out["ref"] = full[1:-1][order].astype(jnp.bfloat16)
    edge = np.zeros((128, 256))
    edge[0, :128] = full[0, :128]
    edge[1, 128:] = full[-1, -128:]
    out["edge"] = edge.astype(jnp.bfloat16)
    ym = np.zeros((64, 32))
    yt = np.zeros((16, 32))
    place = lambda c: 16 if c < 0 else 17 if c > 15 else c
    for n in range(64):
        c, s = divmod(n, 4)
        o = (s + 0.5) / 4 - 0.5
        ym[n, c] += 1 - abs(o)
        ym[n, place(c + (1 if o > 0 else -1))] += abs(o)
    for c in range(16):
        yt[c, c] += 0.75
        yt[c, place(c - 1)] += 0.125
        yt[c, place(c + 1)] += 0.125
    out["ym"] = np.concatenate([ym, ym], 1).astype(jnp.bfloat16)
    out["yt"] = np.concatenate([yt, yt], 1).astype(jnp.bfloat16)
    cm = np.zeros((512, 128))
    cm[np.arange(512), np.arange(512) // 4] = 1.0 / 4
    out["cm"] = cm.astype(jnp.bfloat16)
    rm = np.zeros((32, 128))
    rm[np.arange(128) // 4, np.arange(128)] = 1.0 / 16
    out["rm"] = np.concatenate([rm, rm], 1).astype(jnp.bfloat16)
    g = np.arange(G)
    fine_angle = 2 * np.pi * np.outer(g, k) / NV
    coarse_angle = 2 * np.pi * (np.outer(g, k) % W) / W
    out["fwd"] = tuple(
        x.astype(np.float32)
        for x in (
            np.concatenate([np.cos(fine_angle), -np.sin(fine_angle)], 1) * norm,
            np.concatenate([np.cos(coarse_angle), -np.sin(coarse_angle)], 1),
        )
    )
    angle = 2 * np.pi * (np.outer(g, k) % G) / G
    out["comb"] = (np.cos(angle).astype(np.float32), np.sin(angle).astype(np.float32))
    return out


def halves(x):
    high = x.astype(BF16)
    low = (x - high.astype(F32)).astype(BF16)
    return high, low


def mm(a, b):
    return jnp.dot(a, b, preferred_element_type=F32)


VM = pl.BlockSpec(memory_space=pltpu.VMEM)
SM = pl.BlockSpec(memory_space=pltpu.SMEM)
HB = pl.BlockSpec(memory_space=pltpu.HBM)


def call(kernel, out_shape, in_specs, out_specs, limit=12, **kw):
    inner = pl.pallas_call(
        kernel,
        out_shape=out_shape,
        in_specs=in_specs,
        out_specs=out_specs,
        compiler_params=pltpu.CompilerParams(vmem_limit_bytes=limit << 20),
        **kw,
    )

    def placed(*args):
        return inner(
            *[x if spec is not HB else pltpu.with_memory_space_constraint(x, pltpu.HBM) for x, spec in zip(args, in_specs)]
        )

    return placed


def fetch(pairs, sems, first=0):
    copies = [pltpu.make_async_copy(src, dst, sems.at[first + i]) for i, (src, dst) in enumerate(pairs)]
    for copy in copies:
        copy.start()
    return copies


def sds(*shape, dtype=F32):
    return jax.ShapeDtypeStruct(shape, dtype)


def vds(*shape, dtype=F32):
    return pltpu.VMEM(shape, dtype)


def hds(*shape, dtype=F32):
    return pltpu.HBM(shape, dtype)


def iota(shape, dim):
    return lax.broadcasted_iota(jnp.int32, shape, dim)


def roll(x, shift, axis):
    return pltpu.roll(x, shift % x.shape[axis], axis)


def lines_kernel(modes, sal, up, down, ends, south, north, sems):
    copies = fetch(
        (
            (modes.at[:, 0:8, :], ends.at[0]),
            (modes.at[:, 8:16, :], ends.at[1]),
            (sal.at[:, 0:8, :], south),
            (sal.at[:, 56:64, :], north),
        ),
        sems,
    )
    for copy in copies:
        copy.wait()
    for dst, rows, end, row in ((up, north, 1, 7), (down, south, 0, 0)):
        dst[0:16, :] = ends[end, :, row, :]
        face = rows[:, row, :]
        for j in range(4):
            dst[16 + 8 * j : 24 + 8 * j, :] = face[:, 256 * j : 256 * j + 256]


def outer_lines(modes, salinity):
    return call(
        lines_kernel,
        (vds(48, 256), vds(48, 256)),
        [HB, HB],
        [VM, VM],
        scratch_shapes=[
            pltpu.VMEM((2, 16, 8, 256), F32),
            pltpu.VMEM((8, 8, FINE), F32),
            pltpu.VMEM((8, 8, FINE), F32),
            pltpu.SemaphoreType.DMA((4,)),
        ],
        name="outer_lines",
    )(modes.reshape(16, 16, 256), salinity)


def pack_kernel(me, modes, sal, chunk, tail, low_face, high_face, modes_a, modes_b, west, east, faces, lines, sems, out_sems):
    copies = fetch(
        (
            (modes.at[:, 0:128], modes_a),
            (modes.at[:, 128:256], modes_b),
            (sal.at[0], faces.at[0]),
            (sal.at[7], faces.at[1]),
            (sal.at[:, :, 0:128], west),
            (sal.at[:, :, FINE - 128 :], east),
        ),
        sems,
    )
    for copy in copies[:2]:
        copy.wait()
    zero = jnp.zeros((8, 128), F32)
    for r in range(G):
        lines[r, 0:16, :] = modes_a[pl.ds(r, 16, stride=16), :]
        lines[r, 16:32, :] = modes_b[pl.ds(r, 16, stride=16), :]
        tail[r] = zero
    stores = [pltpu.make_async_copy(lines, chunk.at[:, 0:32, :], out_sems.at[0])]
    stores[0].start()
    for i, face in enumerate((low_face, high_face)):
        copies[2 + i].wait()
        stores.append(pltpu.make_async_copy(faces.at[i], face, out_sems.at[1 + i]))
        stores[-1].start()
    row_id = iota((8, 128), 0)

    def column(block, lane):
        tile = zero
        for i in range(4):
            both = jnp.concatenate([block[2 * i], block[2 * i + 1]], 0).T
            line = jnp.broadcast_to(both[lane : lane + 1, :], (8, 128))
            tile = jnp.where(row_id == 4 + i, line, tile)
        return tile

    for copy in copies[4:]:
        copy.wait()
    tail[(me[0] + 1) % G] = column(east, 127)
    tail[(me[0] + G - 1) % G] = column(west, 0)
    for store in stores:
        store.wait()


def pack(me, modes, salinity):
    return call(
        pack_kernel,
        (hds(G, 40, 128), vds(G, 8, 128), hds(64, FINE), hds(64, FINE)),
        [SM, HB, HB],
        [HB, VM, HB, HB],
        scratch_shapes=[
            pltpu.VMEM((256, 128), F32),
            pltpu.VMEM((256, 128), F32),
            pltpu.VMEM((8, 64, 128), F32),
            pltpu.VMEM((8, 64, 128), F32),
            pltpu.VMEM((2, 64, FINE), F32),
            pltpu.VMEM((G, 32, 128), F32),
            pltpu.SemaphoreType.DMA((6,)),
            pltpu.SemaphoreType.DMA((3,)),
        ],
        name="pack",
    )(me, modes, salinity)


def tails_kernel(chunk, tail, from_south, from_north, out, tiles, sem):
    row_id = iota((8, 128), 0)
    for r in range(G):
        rows = from_south if r < 8 else from_north
        p = r % 8
        tile = tail[r]
        parts = (rows[p : p + 1, :128], rows[p : p + 1, 128:], rows[8 + p : 9 + p, :128], rows[8 + p : 9 + p, 128:])
        for i, part in enumerate(parts):
            tile = jnp.where(row_id == i, jnp.broadcast_to(part, (8, 128)), tile)
        tiles[r] = tile
    store = pltpu.make_async_copy(tiles, out.at[:, 32:40, :], sem)
    store.start()
    store.wait()


def tails(chunk, tail, from_south, from_north):
    return call(
        tails_kernel,
        hds(G, 40, 128),
        [HB, VM, VM, VM],
        HB,
        input_output_aliases={0: 0},
        scratch_shapes=[pltpu.VMEM((G, 8, 128), F32), pltpu.SemaphoreType.DMA],
        name="tails",
    )(chunk, tail, from_south, from_north)


def cmul(a, b, c, s):
    return a * c - b * s, a * s + b * c


def four(z):
    (ar, ai), (br, bi), (cr, ci), (dr, di) = z
    t0r, t0i, t1r, t1i = ar + cr, ai + ci, ar - cr, ai - ci
    t2r, t2i, t3r, t3i = br + dr, bi + di, br - dr, bi - di
    return (
        (t0r + t2r, t0i + t2i),
        (t1r - t3i, t1i + t3r),
        (t0r - t2r, t0i - t2i),
        (t1r + t3i, t1i - t3r),
    )


def sixteen(z):
    inner = [four([z[4 * g1 + g0] for g1 in range(4)]) for g0 in range(4)]
    out = [None] * 16
    for r0 in range(4):
        column = []
        for g0 in range(4):
            angle = 2 * math.pi * g0 * r0 / 16
            a, b = inner[g0][r0]
            column.append((a, b) if g0 * r0 == 0 else cmul(a, b, math.cos(angle), math.sin(angle)))
        for r1, value in enumerate(four(column)):
            out[4 * r1 + r0] = value
    return out


def inverse_kernel(recv, twc, tws, inv_high, inv_low, send_hbm, left_high, left_low, mid, send, sems):
    row_id = iota((8, 128), 0)
    lane_id = iota((8, 128), 1)

    def put(r, top, part, value):
        high, low = halves(value)
        left_high[16 * r + 8 * top : 16 * r + 8 * top + 8, 128 * part : 128 * part + 128] = high
        left_low[16 * r + 8 * top : 16 * r + 8 * top + 8, 128 * part : 128 * part + 128] = low

    for h in range(2):
        z = [(recv[g, 16 * h : 16 * h + 8, :], recv[g, 16 * h + 8 : 16 * h + 16, :]) for g in range(G)]
        for r, (a, b) in enumerate(sixteen(z)):
            a, b = cmul(a, b, twc[r, h : h + 1, :], tws[r, h : h + 1, :])
            put(r, 0, h, a)
            put(r, 0, 2 + h, b)
    z = []
    for g in range(G):
        tile = jnp.where(row_id < 4, recv[g, 32:40, :], 0.0)
        z.append((tile, roll(tile, -2, 0)))
    for r, (a, b) in enumerate(sixteen(z)):
        a, b = cmul(a, b, twc[r], tws[r])
        for part, value in ((0, a), (2, b)):
            put(r, 1, part, jnp.where(row_id == 0, value, 0.0))
            put(r, 1, part + 1, jnp.where(row_id == 0, roll(value, -1, 0), 0.0))

    mid[...] = (
        mm(left_high[...], inv_high[...]) + mm(left_low[...], inv_high[...]) + mm(left_high[...], inv_low[...])
    )

    first, second, single = [], [], []
    for r in range(G):
        first.append(mid[16 * r : 16 * r + 8, 0:128])
        second.append(mid[16 * r : 16 * r + 8, 128:256])
        low = mid[16 * r + 8 : 16 * r + 16, 0:128]
        high = mid[16 * r + 8 : 16 * r + 16, 128:256]
        single.append(jnp.where(row_id == 0, low, roll(high, 1, 0)))
    for i in range(8):
        a, b = first[i], second[i]
        c, d = first[i + 8], second[i + 8]
        first[i], second[i], first[i + 8], second[i + 8] = a, c, b, d
        a, c = single[i], single[i + 8]
        single[i] = jnp.where(row_id == 0, a, roll(c, 1, 0))
        single[i + 8] = jnp.where(row_id == 0, roll(a, -1, 0), c)
    for bit in (4, 2, 1):
        upper = (lane_id // (16 * bit)) % 2 == 1
        for tiles in (first, second, single):
            for i in range(G):
                if i & bit:
                    continue
                a, b = tiles[i], tiles[i | bit]
                tiles[i] = jnp.where(upper, roll(b, 16 * bit, 1), a)
                tiles[i | bit] = jnp.where(upper, b, roll(a, -16 * bit, 1))

    left = [roll(second[d], 1, 1) for d in range(G)]
    right = [roll(first[d], 1, 1) for d in range(G)]
    side = [roll(single[d], 5, 1) for d in range(G)]
    stores = []
    for d in range(G):
        before, after = (d - 1) % G, (d + 1) % G
        own = jnp.where(lane_id == 0, left[before], jnp.where(lane_id == 1, right[after], 0.0))
        rim = own + roll(roll(own, -1, 0), 2, 1)
        base = jnp.where(row_id == 2, roll(single[d], 2, 0), 0.0)
        base = jnp.where(row_id == 6, roll(single[d], 5, 0), base)
        base = jnp.where((row_id == 3) & (lane_id == 4), roll(side[before], 2, 0), base)
        base = jnp.where((row_id == 3) & (lane_id == 5), roll(side[after], 3, 0), base)
        for g in range(4):
            tile = jnp.where(row_id < 2, roll(first[d], -2 * g, 0), base)
            tile = jnp.where((row_id == 4) | (row_id == 5), roll(second[d], 4 - 2 * g, 0), tile)
            tile = jnp.where((row_id == 3) & (lane_id < 4), roll(rim, 3 - 2 * g, 0), tile)
            send[g, d] = tile
        if d % 4 == 3:
            ds = slice(d - 3, d + 1)
            stores += fetch(((send.at[:, ds], send_hbm.at[:, ds]),), sems, d // 4)
    for store in stores:
        store.wait()


def inverse(recv, twc, tws, high, low):
    return call(
        inverse_kernel,
        hds(4, G, 8, 128),
        [VM] * 5,
        HB,
        scratch_shapes=[
            pltpu.VMEM((256, 512), BF16),
            pltpu.VMEM((256, 512), BF16),
            pltpu.VMEM((256, 256), F32),
            pltpu.VMEM((4, G, 8, 128), F32),
            pltpu.SemaphoreType.DMA((4,)),
        ],
        name="inverse",
    )(recv, twc, tws, high, low).reshape(64, 8, 128)


EARLY = ("ym", "yt", "edge", "ref", "rm", "cm")


def still_kernel(me, rate_hbm, sal_hbm, zlow_hbm, zhigh_hbm, edge_cols, from_south, from_north, *rest):
    count = len(EARLY)
    hbm, (base, parts_hbm), kept, rest = rest[:count], rest[count : count + 2], rest[count + 2 : 2 * count + 2], rest[2 * count + 2 :]
    rate, salinity, zlow, zhigh, parts, sems, const_sems, out_sems = rest
    copies = fetch(((rate_hbm, rate), (sal_hbm, salinity), (zlow_hbm, zlow), (zhigh_hbm, zhigh)), sems)
    stores = fetch(tuple(zip(hbm, kept)), const_sems)
    west_t = edge_cols[(me[0] + G - 1) % G, 32:40, :].T
    east_t = edge_cols[(me[0] + 1) % G, 32:40, :].T
    last_row = iota((8, FINE), 0) == 7
    first_row = iota((8, FINE), 0) == 0
    last_lane = iota((8, 128), 1) == 127
    first_lane = iota((8, 128), 1) == 0

    def outer(rows, l):
        line = jnp.concatenate([rows[16 + 8 * j + l : 17 + 8 * j + l, :] for j in range(4)], 1)
        return jnp.broadcast_to(line, (8, FINE))

    for copy in copies:
        copy.wait()
    for yb in range(8):
        ys = slice(8 * yb, 8 * yb + 8)
        for l in range(8):
            c = salinity[l, ys, :]
            upper = salinity[l + 1, ys, :] if l < 7 else zhigh[ys, :]
            lower = salinity[l - 1, ys, :] if l > 0 else zlow[ys, :]
            if yb < 7:
                north = salinity[l, 8 * yb + 1 : 8 * yb + 9, :]
            else:
                north = jnp.where(last_row, outer(from_north, l), roll(c, -1, 0))
            if yb > 0:
                south = salinity[l, 8 * yb - 1 : 8 * yb + 7, :]
            else:
                south = jnp.where(first_row, outer(from_south, l), roll(c, 1, 0))
            at = (l % 2) * 64 + 8 * yb
            ecol = jnp.broadcast_to(east_t[at : at + 8, 4 + l // 2 : 5 + l // 2], (8, 128))
            wcol = jnp.broadcast_to(west_t[at : at + 8, 4 + l // 2 : 5 + l // 2], (8, 128))
            e = roll(c, -1, 1)
            w = roll(c, 1, 1)
            e = jnp.concatenate([e[:, :-128], jnp.where(last_lane, ecol, e[:, -128:])], 1)
            w = jnp.concatenate([jnp.where(first_lane, wcol, w[:, :128]), w[:, 128:]], 1)
            k = rate[l] * 0.1
            base[l, ys, :] = c + k * (((e + w) + (north + south)) + (upper + lower) - 6.0 * c)
            parts[0, l, ys, :] = (e - w) * 0.05
            parts[1, l, ys, :] = (north - south) * 0.05
            parts[2, l, ys, :] = (upper - lower) * 0.05
        stores.append(pltpu.make_async_copy(parts.at[:, :, ys, :], parts_hbm.at[:, :, ys, :], out_sems.at[yb]))
        stores[-1].start()
    for store in stores:
        store.wait()


def still(me, rate, salinity, zlow, zhigh, recv1, from_south, from_north):
    consts = [jnp.asarray(tables()[name]) for name in EARLY]
    return call(
        still_kernel,
        [vds(8, 64, FINE), hds(3, 8, 64, FINE)] + [vds(*x.shape, dtype=x.dtype) for x in consts],
        [SM, HB, HB, HB, HB, VM, VM, VM] + [HB] * len(consts),
        [VM, HB] + [VM] * len(consts),
        scratch_shapes=[
            pltpu.SMEM((8,), F32),
            pltpu.VMEM((8, 64, FINE), F32),
            pltpu.VMEM((64, FINE), F32),
            pltpu.VMEM((64, FINE), F32),
            pltpu.VMEM((3, 8, 64, FINE), F32),
            pltpu.SemaphoreType.DMA((4,)),
            pltpu.SemaphoreType.DMA((len(consts),)),
            pltpu.SemaphoreType.DMA((8,)),
        ],
        limit=24,
        name="still",
    )(me, rate, salinity, zlow, zhigh, recv1, from_south, from_north, *consts)


def fine_kernel(
    grp_ref,
    base,
    parts_hbm,
    recv,
    ym,
    yt,
    edge,
    ref,
    rm,
    cm,
    out,
    spread,
    y_high,
    y_low,
    side_high,
    side_low,
    vel,
    total,
    parts,
    in_sems,
):
    rows = [slice(8 * yb, 8 * yb + 8) for yb in range(8)]
    loads = fetch([(parts_hbm.at[:, :, ys, :], parts.at[:, :, ys, :]) for ys in rows], in_sems)
    grp = grp_ref[0]
    row_id = iota((8, 128), 0)
    lane_id = iota((8, 128), 1)

    def lines(f, q):
        main = [recv[pl.ds(f * 128 + i, 16, stride=8), :] for i in (q, 4 + q, 3)]
        south = recv[pl.ds(pl.multiple_of((f * 16 + 2 * grp + q) * 8, 8), 8), :]
        north = recv[pl.ds(pl.multiple_of((f * 16 + 8 + 2 * grp + q) * 8, 8), 8), :]
        parts = []
        for x, row in zip(main, (2, 6, 3)):
            s, n = roll(south, -row, 0), roll(north, 1 - row, 0)
            if row == 3:
                x, s, n = roll(x, -2 * q, 1), roll(s, -4, 1), roll(n, -4, 1)
            tile = jnp.where(row_id == 0, s, jnp.where(row_id == 1, n, 0.0))
            parts.append(jnp.concatenate([x, tile, jnp.zeros((8, 128), F32)], 0))
        return jnp.concatenate(parts, 1)

    def along_y(table, f, q):
        high, low = halves(lines(f, q))
        return mm(table[...], jnp.concatenate([high, low], 0))

    for f in range(4):
        for q in range(2):
            at = slice(64 * (2 * f + q), 64 * (2 * f + q) + 64) if f < 3 else slice(384 + 16 * q, 400 + 16 * q)
            high, low = halves(along_y(ym if f < 3 else yt, f, q))
            y_high[at, :], side_high[at, :] = high[:, :256], high[:, 256:]
            y_low[at, :], side_low[at, :] = low[:, :256], low[:, 256:]
    vel[...] = mm(y_high[...], ref[...]) + mm(y_low[...], ref[...])
    side = mm(side_high[...], edge[...]) + mm(side_low[...], edge[...])
    vel[:, :128] += side[:, :128]
    vel[:, FINE - 128 :] += side[:, 128:]

    for yb in range(8):
        ys = rows[yb]
        loads[yb].wait()
        for q in range(2):
            vx, vy, vz = (vel[64 * (2 * f + q) + 8 * yb : 64 * (2 * f + q) + 8 * yb + 8, :] for f in range(3))
            acc = None
            for l in range(4 * q, 4 * q + 4):
                new = base[l, ys, :] - (vx * parts[0, l, ys, :] + vy * parts[1, l, ys, :] + vz * parts[2, l, ys, :])
                out[l, ys, :] = new
                acc = new if acc is None else acc + new
            total[64 * q + 8 * yb : 64 * q + 8 * yb + 8, :] = acc
    high, low = halves(total[...])
    high, low = halves(vel[384:416, :] - mm(rm[...], jnp.concatenate([high, low], 0)))
    means = [mm(high[:, at], cm[...]) + mm(low[:, at], cm[...]) for at in (slice(0, 512), slice(512, FINE))]
    mean = jnp.concatenate(means, 1)
    for a in range(G):
        spread[a] = mean


def fine(grp, base, parts, recv2, consts):
    return call(
        fine_kernel,
        (vds(8, 64, FINE), vds(G, 32, 256)),
        [SM, VM, HB, VM] + [VM] * len(consts),
        [VM, VM],
        input_output_aliases={1: 0},
        scratch_shapes=[
            pltpu.VMEM((416, 256), BF16),
            pltpu.VMEM((416, 256), BF16),
            pltpu.VMEM((416, 128), BF16),
            pltpu.VMEM((416, 128), BF16),
            pltpu.VMEM((416, FINE), F32),
            pltpu.VMEM((128, FINE), F32),
            pltpu.VMEM((3, 8, 64, FINE), F32),
            pltpu.SemaphoreType.DMA((8,)),
        ],
        limit=20,
        name="fine",
    )(grp, base, parts, recv2.reshape(512, 128), *consts)


def stage_kernel(me, inner_hbm, outer_hbm, *rest):
    count = (len(rest) - 8) // 2
    hbm, dst, rest = rest[:count], rest[count : 2 * count], rest[2 * count :]
    high_hbm, low_hbm, high, low, inner, outer, sems, out_sems = rest
    copies = fetch(((inner_hbm, inner), (outer_hbm, outer)) + tuple(zip(hbm, dst)), sems)
    turns = (iota((16, 128), 0) * me[0]) % G
    angle = turns.astype(F32) * (2.0 * math.pi / G)
    cos = jnp.concatenate([jnp.cos(angle)] * 2, 1)
    sin = -jnp.concatenate([jnp.sin(angle)] * 2, 1)
    copies[0].wait()
    copies[1].wait()
    real, imag = cmul(inner[:, :256], inner[:, 256:], cos, sin)
    for t in range(G):
        rows = slice(16 * t, 16 * t + 16)
        value = cmul(real, imag, outer[t : t + 1, :256], outer[t : t + 1, 256:])
        for at in range(2):
            high[rows, 256 * at : 256 * at + 256], low[rows, 256 * at : 256 * at + 256] = halves(value[at])
    for copy in copies[2:] + fetch(((high, high_hbm), (low, low_hbm)), out_sems):
        copy.wait()


def stage(me):
    t = tables()
    consts = [jnp.asarray(x) for x in (*t["tw"], *t["inv"])]
    out = call(
        stage_kernel,
        [vds(*x.shape, dtype=x.dtype) for x in consts] + [hds(256, 512, dtype=BF16)] * 2,
        [SM, HB, HB] + [HB] * len(consts),
        [VM] * len(consts) + [HB] * 2,
        scratch_shapes=[
            pltpu.VMEM((256, 512), BF16),
            pltpu.VMEM((256, 512), BF16),
            pltpu.VMEM((G, 512), F32),
            pltpu.VMEM((G, 512), F32),
            pltpu.SemaphoreType.DMA((len(consts) + 2,)),
            pltpu.SemaphoreType.DMA((2,)),
        ],
        name="stage",
    )(me, *map(jnp.asarray, t["fwd"]), *consts)
    return out[0:4], out[4:6]


def forward_kernel(recv, table_high, table_low, cos_hbm, sin_hbm, out, left_high, left_low, mid, comb_cos, comb_sin, sems):
    copies = fetch(((cos_hbm, comb_cos), (sin_hbm, comb_sin)), sems)
    for a in range(G):
        high, low = halves(recv[a])
        left_high[32 * a : 32 * a + 32, :] = high
        left_low[32 * a : 32 * a + 32, :] = low
    mid[...] = (
        mm(left_high[...], table_high[...]) + mm(left_low[...], table_high[...]) + mm(left_high[...], table_low[...])
    )
    for copy in copies:
        copy.wait()
    real = imag = jnp.zeros((32, 256), F32)
    for a in range(G):
        c, s = comb_cos[a : a + 1, :], comb_sin[a : a + 1, :]
        x, y = mid[32 * a : 32 * a + 32, :256], mid[32 * a : 32 * a + 32, 256:]
        real = real + (x * c + y * s)
        imag = imag + (y * c - x * s)
    for g in range(4):
        out[g, 0:32, :] = real
        out[g, 32:64, :] = imag


def forward(recv, high, low):
    return call(
        forward_kernel,
        sds(4, 64, 256),
        [VM, VM, VM, HB, HB],
        VM,
        scratch_shapes=[
            pltpu.VMEM((512, 256), BF16),
            pltpu.VMEM((512, 256), BF16),
            pltpu.VMEM((512, 512), F32),
            pltpu.VMEM((G, 256), F32),
            pltpu.VMEM((G, 256), F32),
            pltpu.SemaphoreType.DMA((2,)),
        ],
        name="forward",
    )(recv, high, low, *map(jnp.asarray, tables()["comb"]))


def finish_kernel(me, viscosity, gain, recv, modes, out):
    index = me[0] * W + iota((8, W), 1)
    number = jnp.where(index < NV // 2, index, index - NV).astype(F32)
    wave = (2.0 * math.pi / NV) * number
    damping = jnp.exp(-viscosity[0] * wave * wave)[0:1, :]
    for c in range(2):
        for g in range(4):
            at = slice(128 * c + 32 * g, 128 * c + 32 * g + 32)
            out[at, :] = damping * modes[at, :] + gain[0] * recv[g, 32 * c : 32 * c + 32, :]


def finish(me, viscosity, gain, recv, modes):
    return call(finish_kernel, sds(256, W), [SM, SM, SM, VM, VM], VM, name="finish")(
        me, viscosity, gain, recv, modes
    )


def shifted(array, axis, step):
    count = lax.axis_size(axis)
    return lax.ppermute(array, axis, [(i, (i + step) % count) for i in range(count)])


def per_device(coarse_modes, salinity, viscosity, forcing_gain, diffusivity):
    me = lax.axis_index(GX).astype(jnp.int32).reshape(1)
    grp = lax.axis_index("grp").astype(jnp.int32).reshape(1)
    modes = coarse_modes.reshape(256, 256)
    up, down = outer_lines(modes, salinity)
    from_south = shifted(up, "gy", 1)
    from_north = shifted(down, "gy", -1)
    chunk, tail, low_face, high_face = pack(me, modes, salinity)
    chunk = tails(chunk, tail, from_south, from_north)
    recv1 = lax.all_to_all(chunk, GX, 0, 0, tiled=True)
    inv, weights = stage(me)
    zlow = shifted(high_face, "grp", 1)
    zhigh = shifted(low_face, "grp", -1)
    recv1, zlow, zhigh = lax.optimization_barrier((recv1, zlow, zhigh))
    send2 = inverse(recv1, *inv)
    recv2 = lax.all_to_all(send2, GRP_GX, 0, 0, tiled=True)
    base, parts, *consts = still(me, diffusivity, salinity, zlow, zhigh, recv1, from_south, from_north)
    salinity_next, spread = fine(grp, base, parts, recv2, consts)
    recv3 = lax.all_to_all(spread, GX, 0, 0, tiled=True)
    recv4 = lax.all_to_all(forward(recv3, *weights), "grp", 0, 0, tiled=True)
    coarse_next = finish(me, viscosity, forcing_gain, recv4, modes)
    return (salinity_next, coarse_next.reshape(coarse_modes.shape))


def solution(mesh):
    finer = Mesh(
        mesh.devices.reshape(mesh.shape["grp"], 2, 8, mesh.shape["gy"]),
        ("grp", "gx_0", "gx_1", "gy"),
    )
    in_specs = (P("grp", None, None, "gy", GX), P("grp", "gy", GX), P("grp"), P("grp"), P("grp"))
    out_specs = (P("grp", "gy", GX), P("grp", None, None, "gy", GX))
    return jax.shard_map(
        per_device, mesh=finer, in_specs=in_specs, out_specs=out_specs, check_vma=False
    )
```

```python
import functools
import math

import jax
import jax.numpy as jnp
import numpy as np
from jax import lax
from jax.experimental import pallas as pl
from jax.experimental.pallas import tpu as pltpu
from jax.sharding import Mesh
from jax.sharding import PartitionSpec as P

GX = ("gx_0", "gx_1")
GRP_GX = ("grp", "gx_0", "gx_1")
F32 = jnp.float32
BF16 = jnp.bfloat16
G = 16
NV = 4096
W = 256
FINE = 1024


def split_table(table):
    table = np.asarray(table, np.float64)
    high = table.astype(np.float32).astype(jnp.bfloat16)
    low = (table - high.astype(np.float64)).astype(np.float32).astype(jnp.bfloat16)
    return high, low


@functools.cache
def tables():
    out = {}
    k = np.arange(W)
    angle = 2 * np.pi * (np.outer(k, k) % W) / W
    norm = NV ** -0.5
    out["inv"] = split_table(np.concatenate([np.cos(angle), -np.sin(angle)], 0) * norm)
    r = np.arange(G)
    angle = 2 * np.pi * np.outer(r, k) / NV
    twc = np.zeros((G, 8, 128), np.float32)
    tws = np.zeros((G, 8, 128), np.float32)
    twc[:, :2] = np.cos(angle).reshape(G, 2, 128)
    tws[:, :2] = np.sin(angle).reshape(G, 2, 128)
    out["tw"] = (twc, tws)
    lanes = 16 * (k % 16) + k // 16
    order = np.argsort(lanes)
    assert np.array_equal(order, 16 * (k % 16) + k // 16)
    full = np.zeros((W + 2, FINE))
    for n in range(FINE):
        c, s = divmod(n, 4)
        o = (s + 0.5) / 4 - 0.5
        full[c + 1, n] += 1 - abs(o)
        full[c + 1 + (1 if o > 0 else -1), n] += abs(o)
    out["ref"] = full[1:-1][order].astype(jnp.bfloat16)
    edge = np.zeros((128, 256))
    edge[0, :128] = full[0, :128]
    edge[1, 128:] = full[-1, -128:]
    out["edge"] = edge.astype(jnp.bfloat16)
    ym = np.zeros((64, 32))
    yt = np.zeros((16, 32))
    place = lambda c: 16 if c < 0 else 17 if c > 15 else c
    for n in range(64):
        c, s = divmod(n, 4)
        o = (s + 0.5) / 4 - 0.5
        ym[n, c] += 1 - abs(o)
        ym[n, place(c + (1 if o > 0 else -1))] += abs(o)
    for c in range(16):
        yt[c, c] += 0.75
        yt[c, place(c - 1)] += 0.125
        yt[c, place(c + 1)] += 0.125
    out["ym"] = np.concatenate([ym, ym], 1).astype(jnp.bfloat16)
    out["yt"] = np.concatenate([yt, yt], 1).astype(jnp.bfloat16)
    cm = np.zeros((512, 128))
    cm[np.arange(512), np.arange(512) // 4] = 1.0 / 4
    out["cm"] = cm.astype(jnp.bfloat16)
    rm = np.zeros((32, 128))
    rm[np.arange(128) // 4, np.arange(128)] = 1.0 / 16
    out["rm"] = np.concatenate([rm, rm], 1).astype(jnp.bfloat16)
    g = np.arange(G)
    fine_angle = 2 * np.pi * np.outer(g, k) / NV
    coarse_angle = 2 * np.pi * (np.outer(g, k) % W) / W
    out["fwd"] = tuple(
        x.astype(np.float32)
        for x in (
            np.concatenate([np.cos(fine_angle), -np.sin(fine_angle)], 1) * norm,
            np.concatenate([np.cos(coarse_angle), -np.sin(coarse_angle)], 1),
        )
    )
    return out


def halves(x):
    high = x.astype(BF16)
    low = (x - high.astype(F32)).astype(BF16)
    return high, low


def mm(a, b):
    return jnp.dot(a, b, preferred_element_type=F32)


VM = pl.BlockSpec(memory_space=pltpu.VMEM)
SM = pl.BlockSpec(memory_space=pltpu.SMEM)
HB = pl.BlockSpec(memory_space=pltpu.HBM)


def call(kernel, out_shape, in_specs, out_specs, limit=12, **kw):
    inner = pl.pallas_call(
        kernel,
        out_shape=out_shape,
        in_specs=in_specs,
        out_specs=out_specs,
        compiler_params=pltpu.CompilerParams(vmem_limit_bytes=limit << 20),
        **kw,
    )

    def placed(*args):
        return inner(
            *[x if spec is not HB else pltpu.with_memory_space_constraint(x, pltpu.HBM) for x, spec in zip(args, in_specs)]
        )

    return placed


def fetch(pairs, sems, first=0):
    copies = [pltpu.make_async_copy(src, dst, sems.at[first + i]) for i, (src, dst) in enumerate(pairs)]
    for copy in copies:
        copy.start()
    return copies


def sds(*shape, dtype=F32):
    return jax.ShapeDtypeStruct(shape, dtype)


def vds(*shape, dtype=F32):
    return pltpu.VMEM(shape, dtype)


def hds(*shape, dtype=F32):
    return pltpu.HBM(shape, dtype)


def iota(shape, dim):
    return lax.broadcasted_iota(jnp.int32, shape, dim)


def roll(x, shift, axis):
    return pltpu.roll(x, shift % x.shape[axis], axis)


def lines_kernel(modes, sal, up, down, ends, south, north, sems):
    copies = fetch(
        (
            (modes.at[:, 0:8, :], ends.at[0]),
            (modes.at[:, 8:16, :], ends.at[1]),
            (sal.at[:, 0:8, :], south),
            (sal.at[:, 56:64, :], north),
        ),
        sems,
    )
    for copy in copies:
        copy.wait()
    for dst, rows, end, row in ((up, north, 1, 7), (down, south, 0, 0)):
        dst[0:16, :] = ends[end, :, row, :]
        face = rows[:, row, :]
        for j in range(4):
            dst[16 + 8 * j : 24 + 8 * j, :] = face[:, 256 * j : 256 * j + 256]


def outer_lines(modes, salinity):
    return call(
        lines_kernel,
        (vds(48, 256), vds(48, 256)),
        [HB, HB],
        [VM, VM],
        scratch_shapes=[
            pltpu.VMEM((2, 16, 8, 256), F32),
            pltpu.VMEM((8, 8, FINE), F32),
            pltpu.VMEM((8, 8, FINE), F32),
            pltpu.SemaphoreType.DMA((4,)),
        ],
        name="outer_lines",
    )(modes.reshape(16, 16, 256), salinity)


def pack_kernel(me, modes, sal, chunk, low_face, high_face, modes_a, modes_b, west, east, faces, sems, out_sems):
    copies = fetch(
        (
            (modes.at[:, 0:128], modes_a),
            (modes.at[:, 128:256], modes_b),
            (sal.at[0], faces.at[0]),
            (sal.at[7], faces.at[1]),
            (sal.at[:, :, 0:128], west),
            (sal.at[:, :, FINE - 128 :], east),
        ),
        sems,
    )
    for copy in copies[:2]:
        copy.wait()
    zero = jnp.zeros((8, 128), F32)
    for r in range(G):
        chunk[r, 0:16, :] = modes_a[pl.ds(r, 16, stride=16), :]
        chunk[r, 16:32, :] = modes_b[pl.ds(r, 16, stride=16), :]
        chunk[r, 32:40, :] = zero
    stores = []
    for i, face in enumerate((low_face, high_face)):
        copies[2 + i].wait()
        stores.append(pltpu.make_async_copy(faces.at[i], face, out_sems.at[i]))
        stores[-1].start()
    row_id = iota((8, 128), 0)

    def column(block, lane):
        tile = zero
        for i in range(4):
            both = jnp.concatenate([block[2 * i], block[2 * i + 1]], 0).T
            line = jnp.broadcast_to(both[lane : lane + 1, :], (8, 128))
            tile = jnp.where(row_id == 4 + i, line, tile)
        return tile

    for copy in copies[4:]:
        copy.wait()
    chunk[(me[0] + 1) % G, 32:40, :] = column(east, 127)
    chunk[(me[0] + G - 1) % G, 32:40, :] = column(west, 0)
    for store in stores:
        store.wait()


def pack(me, modes, salinity):
    return call(
        pack_kernel,
        (vds(G, 40, 128), hds(64, FINE), hds(64, FINE)),
        [SM, HB, HB],
        [VM, HB, HB],
        scratch_shapes=[
            pltpu.VMEM((256, 128), F32),
            pltpu.VMEM((256, 128), F32),
            pltpu.VMEM((8, 64, 128), F32),
            pltpu.VMEM((8, 64, 128), F32),
            pltpu.VMEM((2, 64, FINE), F32),
            pltpu.SemaphoreType.DMA((6,)),
            pltpu.SemaphoreType.DMA((2,)),
        ],
        name="pack",
    )(me, modes, salinity)


def tails_kernel(chunk, from_south, from_north, out):
    row_id = iota((8, 128), 0)
    for r in range(G):
        rows = from_south if r < 8 else from_north
        p = r % 8
        tile = chunk[r, 32:40, :]
        parts = (rows[p : p + 1, :128], rows[p : p + 1, 128:], rows[8 + p : 9 + p, :128], rows[8 + p : 9 + p, 128:])
        for i, part in enumerate(parts):
            tile = jnp.where(row_id == i, jnp.broadcast_to(part, (8, 128)), tile)
        out[r, 32:40, :] = tile


def tails(chunk, from_south, from_north):
    return call(
        tails_kernel,
        vds(G, 40, 128),
        [VM, VM, VM],
        VM,
        input_output_aliases={0: 0},
        name="tails",
    )(chunk, from_south, from_north)


def cmul(a, b, c, s):
    return a * c - b * s, a * s + b * c


def four(z):
    (ar, ai), (br, bi), (cr, ci), (dr, di) = z
    t0r, t0i, t1r, t1i = ar + cr, ai + ci, ar - cr, ai - ci
    t2r, t2i, t3r, t3i = br + dr, bi + di, br - dr, bi - di
    return (
        (t0r + t2r, t0i + t2i),
        (t1r - t3i, t1i + t3r),
        (t0r - t2r, t0i - t2i),
        (t1r + t3i, t1i - t3r),
    )


def sixteen(z):
    inner = [four([z[4 * g1 + g0] for g1 in range(4)]) for g0 in range(4)]
    out = [None] * 16
    for r0 in range(4):
        column = []
        for g0 in range(4):
            angle = 2 * math.pi * g0 * r0 / 16
            a, b = inner[g0][r0]
            column.append((a, b) if g0 * r0 == 0 else cmul(a, b, math.cos(angle), math.sin(angle)))
        for r1, value in enumerate(four(column)):
            out[4 * r1 + r0] = value
    return out


def inverse_kernel(recv, twc, tws, inv_high, inv_low, send_hbm, left_high, left_low, mid, send, sems):
    row_id = iota((8, 128), 0)
    lane_id = iota((8, 128), 1)

    def put(r, top, part, value):
        high, low = halves(value)
        left_high[16 * r + 8 * top : 16 * r + 8 * top + 8, 128 * part : 128 * part + 128] = high
        left_low[16 * r + 8 * top : 16 * r + 8 * top + 8, 128 * part : 128 * part + 128] = low

    for h in range(2):
        z = [(recv[g, 16 * h : 16 * h + 8, :], recv[g, 16 * h + 8 : 16 * h + 16, :]) for g in range(G)]
        for r, (a, b) in enumerate(sixteen(z)):
            a, b = cmul(a, b, twc[r, h : h + 1, :], tws[r, h : h + 1, :])
            put(r, 0, h, a)
            put(r, 0, 2 + h, b)
    z = []
    for g in range(G):
        tile = jnp.where(row_id < 4, recv[g, 32:40, :], 0.0)
        z.append((tile, roll(tile, -2, 0)))
    for r, (a, b) in enumerate(sixteen(z)):
        a, b = cmul(a, b, twc[r], tws[r])
        for part, value in ((0, a), (2, b)):
            put(r, 1, part, jnp.where(row_id == 0, value, 0.0))
            put(r, 1, part + 1, jnp.where(row_id == 0, roll(value, -1, 0), 0.0))

    mid[...] = (
        mm(left_high[...], inv_high[...]) + mm(left_low[...], inv_high[...]) + mm(left_high[...], inv_low[...])
    )

    first, second, single = [], [], []
    for r in range(G):
        first.append(mid[16 * r : 16 * r + 8, 0:128])
        second.append(mid[16 * r : 16 * r + 8, 128:256])
        low = mid[16 * r + 8 : 16 * r + 16, 0:128]
        high = mid[16 * r + 8 : 16 * r + 16, 128:256]
        single.append(jnp.where(row_id == 0, low, roll(high, 1, 0)))
    for i in range(8):
        a, b = first[i], second[i]
        c, d = first[i + 8], second[i + 8]
        first[i], second[i], first[i + 8], second[i + 8] = a, c, b, d
        a, c = single[i], single[i + 8]
        single[i] = jnp.where(row_id == 0, a, roll(c, 1, 0))
        single[i + 8] = jnp.where(row_id == 0, roll(a, -1, 0), c)
    for bit in (4, 2, 1):
        upper = (lane_id // (16 * bit)) % 2 == 1
        for tiles in (first, second, single):
            for i in range(G):
                if i & bit:
                    continue
                a, b = tiles[i], tiles[i | bit]
                tiles[i] = jnp.where(upper, roll(b, 16 * bit, 1), a)
                tiles[i | bit] = jnp.where(upper, b, roll(a, -16 * bit, 1))

    left = [roll(second[d], 1, 1) for d in range(G)]
    right = [roll(first[d], 1, 1) for d in range(G)]
    side = [roll(single[d], 5, 1) for d in range(G)]
    stores = []
    for d in range(G):
        before, after = (d - 1) % G, (d + 1) % G
        own = jnp.where(lane_id == 0, left[before], jnp.where(lane_id == 1, right[after], 0.0))
        rim = own + roll(roll(own, -1, 0), 2, 1)
        base = jnp.where(row_id == 2, roll(single[d], 2, 0), 0.0)
        base = jnp.where(row_id == 6, roll(single[d], 5, 0), base)
        base = jnp.where((row_id == 3) & (lane_id == 4), roll(side[before], 2, 0), base)
        base = jnp.where((row_id == 3) & (lane_id == 5), roll(side[after], 3, 0), base)
        for g in range(4):
            tile = jnp.where(row_id < 2, roll(first[d], -2 * g, 0), base)
            tile = jnp.where((row_id == 4) | (row_id == 5), roll(second[d], 4 - 2 * g, 0), tile)
            tile = jnp.where((row_id == 3) & (lane_id < 4), roll(rim, 3 - 2 * g, 0), tile)
            send[g, d] = tile
        if d % 4 == 3:
            ds = slice(d - 3, d + 1)
            stores += fetch(((send.at[:, ds], send_hbm.at[:, ds]),), sems, d // 4)
    for store in stores:
        store.wait()


def inverse(recv, twc, tws, high, low):
    return call(
        inverse_kernel,
        hds(4, G, 8, 128),
        [VM] * 5,
        HB,
        scratch_shapes=[
            pltpu.VMEM((256, 512), BF16),
            pltpu.VMEM((256, 512), BF16),
            pltpu.VMEM((256, 256), F32),
            pltpu.VMEM((4, G, 8, 128), F32),
            pltpu.SemaphoreType.DMA((4,)),
        ],
        name="inverse",
    )(recv, twc, tws, high, low).reshape(64, 8, 128)


EARLY = ("ym", "yt", "edge", "ref", "rm", "cm")


def still_levels(
    levels, runs, me, rate, salinity, zlow, zhigh, edge_cols, from_south, from_north, base, parts, parts_hbm, out_sems
):
    west_t = edge_cols[(me[0] + G - 1) % G, 32:40, :].T
    east_t = edge_cols[(me[0] + 1) % G, 32:40, :].T
    last_row = iota((8, FINE), 0) == 7
    first_row = iota((8, FINE), 0) == 0
    last_lane = iota((8, 128), 1) == 127
    first_lane = iota((8, 128), 1) == 0

    def outer(rows, l):
        line = jnp.concatenate([rows[16 + 8 * j + l : 17 + 8 * j + l, :] for j in range(4)], 1)
        return jnp.broadcast_to(line, (8, FINE))

    stores = []
    for yb in range(8):
        ys = slice(8 * yb, 8 * yb + 8)
        for l in levels:
            c = salinity[l, ys, :]
            upper = salinity[l + 1, ys, :] if l < 7 else zhigh[ys, :]
            lower = salinity[l - 1, ys, :] if l > 0 else zlow[ys, :]
            if yb < 7:
                north = salinity[l, 8 * yb + 1 : 8 * yb + 9, :]
            else:
                north = jnp.where(last_row, outer(from_north, l), roll(c, -1, 0))
            if yb > 0:
                south = salinity[l, 8 * yb - 1 : 8 * yb + 7, :]
            else:
                south = jnp.where(first_row, outer(from_south, l), roll(c, 1, 0))
            at = (l % 2) * 64 + 8 * yb
            ecol = jnp.broadcast_to(east_t[at : at + 8, 4 + l // 2 : 5 + l // 2], (8, 128))
            wcol = jnp.broadcast_to(west_t[at : at + 8, 4 + l // 2 : 5 + l // 2], (8, 128))
            e = roll(c, -1, 1)
            w = roll(c, 1, 1)
            e = jnp.concatenate([e[:, :-128], jnp.where(last_lane, ecol, e[:, -128:])], 1)
            w = jnp.concatenate([jnp.where(first_lane, wcol, w[:, :128]), w[:, 128:]], 1)
            k = rate[l] * 0.1
            base[l, ys, :] = c + k * (((e + w) + (north + south)) + (upper + lower) - 6.0 * c)
            parts[0, l, ys, :] = (e - w) * 0.05
            parts[1, l, ys, :] = (north - south) * 0.05
            parts[2, l, ys, :] = (upper - lower) * 0.05
        for at in runs:
            stores.append(pltpu.make_async_copy(parts.at[:, at, ys, :], parts_hbm.at[:, at, ys, :], out_sems.at[len(stores)]))
            stores[-1].start()
    return stores


def inner_kernel(me, rate_hbm, sal_hbm, edge_cols, from_south, from_north, inner_hbm, outer_hbm, *rest):
    count = len(EARLY)
    hbm, (base, parts_hbm, high_hbm, low_hbm), rest = rest[:count], rest[count : count + 4], rest[count + 4 :]
    kept, rest = rest[:count], rest[count:]
    rate, salinity, parts, high, low, inner, outer, sems, const_sems, out_sems, table_sems = rest
    copies = fetch(
        ((rate_hbm, rate), (sal_hbm, salinity), (inner_hbm, inner), (outer_hbm, outer)), sems
    )
    consts = fetch(tuple(zip(hbm, kept)), const_sems)
    turns = (iota((16, 128), 0) * me[0]) % G
    angle = turns.astype(F32) * (2.0 * math.pi / G)
    cos = jnp.concatenate([jnp.cos(angle)] * 2, 1)
    sin = -jnp.concatenate([jnp.sin(angle)] * 2, 1)
    for copy in copies:
        copy.wait()
    stores = still_levels(
        range(1, 7), (slice(1, 7),), me, rate, salinity, None, None, edge_cols, from_south, from_north, base, parts, parts_hbm, out_sems
    )
    real, imag = cmul(inner[:, :256], inner[:, 256:], cos, sin)
    for t in range(G):
        rows = slice(16 * t, 16 * t + 16)
        value = cmul(real, imag, outer[t : t + 1, :256], outer[t : t + 1, 256:])
        for at in range(2):
            high[rows, 256 * at : 256 * at + 256], low[rows, 256 * at : 256 * at + 256] = halves(value[at])
    for copy in stores + consts + fetch(((high, high_hbm), (low, low_hbm)), table_sems):
        copy.wait()


def inner_levels(me, rate, salinity, recv1, from_south, from_north):
    consts = [jnp.asarray(tables()[name]) for name in EARLY]
    out = call(
        inner_kernel,
        [vds(8, 64, FINE), hds(3, 8, 64, FINE)]
        + [hds(256, 512, dtype=BF16)] * 2
        + [vds(*x.shape, dtype=x.dtype) for x in consts],
        [SM, HB, HB, VM, VM, VM, HB, HB] + [HB] * len(consts),
        [VM, HB, HB, HB] + [VM] * len(consts),
        scratch_shapes=[
            pltpu.SMEM((8,), F32),
            pltpu.VMEM((8, 64, FINE), F32),
            pltpu.VMEM((3, 8, 64, FINE), F32),
            pltpu.VMEM((256, 512), BF16),
            pltpu.VMEM((256, 512), BF16),
            pltpu.VMEM((G, 512), F32),
            pltpu.VMEM((G, 512), F32),
            pltpu.SemaphoreType.DMA((4,)),
            pltpu.SemaphoreType.DMA((len(consts),)),
            pltpu.SemaphoreType.DMA((8,)),
            pltpu.SemaphoreType.DMA((2,)),
        ],
        limit=24,
        name="inner_levels",
    )(me, rate, salinity, recv1, from_south, from_north, *map(jnp.asarray, tables()["fwd"]), *consts)
    return out[0], out[1], out[2:4], out[4:]


def outer_kernel(
    me, rate_hbm, sal_hbm, zlow_hbm, zhigh_hbm, edge_cols, from_south, from_north, base_in, parts_in, base, parts_hbm, *rest
):
    rate, salinity, zlow, zhigh, parts, sems, out_sems = rest
    copies = fetch(
        (
            (rate_hbm, rate),
            (sal_hbm.at[0:2], salinity.at[0:2]),
            (sal_hbm.at[6:8], salinity.at[6:8]),
            (zlow_hbm, zlow),
            (zhigh_hbm, zhigh),
        ),
        sems,
    )
    for copy in copies:
        copy.wait()
    stores = still_levels(
        (0, 7), (slice(0, 1), slice(7, 8)), me, rate, salinity, zlow, zhigh, edge_cols, from_south, from_north, base, parts, parts_hbm, out_sems
    )
    for store in stores:
        store.wait()


def outer_levels(me, rate, salinity, zlow, zhigh, recv1, from_south, from_north, base, parts):
    return call(
        outer_kernel,
        [vds(8, 64, FINE), hds(3, 8, 64, FINE)],
        [SM, HB, HB, HB, HB, VM, VM, VM, VM, HB],
        [VM, HB],
        input_output_aliases={8: 0, 9: 1},
        scratch_shapes=[
            pltpu.SMEM((8,), F32),
            pltpu.VMEM((8, 64, FINE), F32),
            pltpu.VMEM((64, FINE), F32),
            pltpu.VMEM((64, FINE), F32),
            pltpu.VMEM((3, 8, 64, FINE), F32),
            pltpu.SemaphoreType.DMA((5,)),
            pltpu.SemaphoreType.DMA((16,)),
        ],
        limit=24,
        name="outer_levels",
    )(me, rate, salinity, zlow, zhigh, recv1, from_south, from_north, base, parts)


def fine_kernel(
    grp_ref,
    base,
    parts_hbm,
    recv,
    ym,
    yt,
    edge,
    ref,
    rm,
    cm,
    out,
    spread,
    y_high,
    y_low,
    side_high,
    side_low,
    vel,
    total,
    parts,
    in_sems,
):
    rows = [slice(8 * yb, 8 * yb + 8) for yb in range(8)]
    loads = fetch([(parts_hbm.at[:, :, ys, :], parts.at[:, :, ys, :]) for ys in rows], in_sems)
    grp = grp_ref[0]
    row_id = iota((8, 128), 0)
    lane_id = iota((8, 128), 1)

    def lines(f, q):
        main = [recv[pl.ds(f * 128 + i, 16, stride=8), :] for i in (q, 4 + q, 3)]
        south = recv[pl.ds(pl.multiple_of((f * 16 + 2 * grp + q) * 8, 8), 8), :]
        north = recv[pl.ds(pl.multiple_of((f * 16 + 8 + 2 * grp + q) * 8, 8), 8), :]
        parts = []
        for x, row in zip(main, (2, 6, 3)):
            s, n = roll(south, -row, 0), roll(north, 1 - row, 0)
            if row == 3:
                x, s, n = roll(x, -2 * q, 1), roll(s, -4, 1), roll(n, -4, 1)
            tile = jnp.where(row_id == 0, s, jnp.where(row_id == 1, n, 0.0))
            parts.append(jnp.concatenate([x, tile, jnp.zeros((8, 128), F32)], 0))
        return jnp.concatenate(parts, 1)

    def along_y(table, f, q):
        high, low = halves(lines(f, q))
        return mm(table[...], jnp.concatenate([high, low], 0))

    for f in range(4):
        for q in range(2):
            at = slice(64 * (2 * f + q), 64 * (2 * f + q) + 64) if f < 3 else slice(384 + 16 * q, 400 + 16 * q)
            high, low = halves(along_y(ym if f < 3 else yt, f, q))
            y_high[at, :], side_high[at, :] = high[:, :256], high[:, 256:]
            y_low[at, :], side_low[at, :] = low[:, :256], low[:, 256:]
    vel[...] = mm(y_high[...], ref[...]) + mm(y_low[...], ref[...])
    side = mm(side_high[...], edge[...]) + mm(side_low[...], edge[...])
    vel[:, :128] += side[:, :128]
    vel[:, FINE - 128 :] += side[:, 128:]

    for yb in range(8):
        ys = rows[yb]
        loads[yb].wait()
        for q in range(2):
            vx, vy, vz = (vel[64 * (2 * f + q) + 8 * yb : 64 * (2 * f + q) + 8 * yb + 8, :] for f in range(3))
            acc = None
            for l in range(4 * q, 4 * q + 4):
                new = base[l, ys, :] - (vx * parts[0, l, ys, :] + vy * parts[1, l, ys, :] + vz * parts[2, l, ys, :])
                out[l, ys, :] = new
                acc = new if acc is None else acc + new
            total[64 * q + 8 * yb : 64 * q + 8 * yb + 8, :] = acc
    high, low = halves(total[...])
    high, low = halves(vel[384:416, :] - mm(rm[...], jnp.concatenate([high, low], 0)))
    means = [mm(high[:, at], cm[...]) + mm(low[:, at], cm[...]) for at in (slice(0, 512), slice(512, FINE))]
    mean = jnp.concatenate(means, 1)
    for a in range(G):
        spread[a] = mean


def fine(grp, base, parts, recv2, consts):
    return call(
        fine_kernel,
        (vds(8, 64, FINE), vds(G, 32, 256)),
        [SM, VM, HB, VM] + [VM] * len(consts),
        [VM, VM],
        input_output_aliases={1: 0},
        scratch_shapes=[
            pltpu.VMEM((416, 256), BF16),
            pltpu.VMEM((416, 256), BF16),
            pltpu.VMEM((416, 128), BF16),
            pltpu.VMEM((416, 128), BF16),
            pltpu.VMEM((416, FINE), F32),
            pltpu.VMEM((128, FINE), F32),
            pltpu.VMEM((3, 8, 64, FINE), F32),
            pltpu.SemaphoreType.DMA((8,)),
        ],
        limit=20,
        name="fine",
    )(grp, base, parts, recv2.reshape(512, 128), *consts)


def forward_kernel(recv, table_high, table_low, out, left_high, left_low, mid):
    turns = (iota((G, 128), 0) * iota((G, 128), 1)) % G
    angle = turns.astype(F32) * (2.0 * math.pi / G)
    comb_cos = jnp.concatenate([jnp.cos(angle)] * 2, 1)
    comb_sin = jnp.concatenate([jnp.sin(angle)] * 2, 1)
    for a in range(G):
        high, low = halves(recv[a])
        left_high[32 * a : 32 * a + 32, :] = high
        left_low[32 * a : 32 * a + 32, :] = low
    mid[...] = (
        mm(left_high[...], table_high[...]) + mm(left_low[...], table_high[...]) + mm(left_high[...], table_low[...])
    )
    real = imag = jnp.zeros((32, 256), F32)
    for a in range(G):
        c, s = comb_cos[a : a + 1, :], comb_sin[a : a + 1, :]
        x, y = mid[32 * a : 32 * a + 32, :256], mid[32 * a : 32 * a + 32, 256:]
        real = real + (x * c + y * s)
        imag = imag + (y * c - x * s)
    for g in range(4):
        out[g, 0:32, :] = real
        out[g, 32:64, :] = imag


def forward(recv, high, low):
    return call(
        forward_kernel,
        sds(4, 64, 256),
        [VM, VM, VM],
        VM,
        scratch_shapes=[
            pltpu.VMEM((512, 256), BF16),
            pltpu.VMEM((512, 256), BF16),
            pltpu.VMEM((512, 512), F32),
        ],
        name="forward",
    )(recv, high, low)


def finish_kernel(me, viscosity, gain, recv, modes, out):
    index = me[0] * W + iota((8, W), 1)
    number = jnp.where(index < NV // 2, index, index - NV).astype(F32)
    wave = (2.0 * math.pi / NV) * number
    damping = jnp.exp(-viscosity[0] * wave * wave)[0:1, :]
    for c in range(2):
        for g in range(4):
            at = slice(128 * c + 32 * g, 128 * c + 32 * g + 32)
            out[at, :] = damping * modes[at, :] + gain[0] * recv[g, 32 * c : 32 * c + 32, :]


def finish(me, viscosity, gain, recv, modes):
    return call(finish_kernel, sds(256, W), [SM, SM, SM, VM, VM], VM, name="finish")(
        me, viscosity, gain, recv, modes
    )


def shifted(array, axis, step):
    count = lax.axis_size(axis)
    return lax.ppermute(array, axis, [(i, (i + step) % count) for i in range(count)])


def per_device(coarse_modes, salinity, viscosity, forcing_gain, diffusivity):
    me = lax.axis_index(GX).astype(jnp.int32).reshape(1)
    grp = lax.axis_index("grp").astype(jnp.int32).reshape(1)
    modes = coarse_modes.reshape(256, 256)
    up, down = outer_lines(modes, salinity)
    from_south = shifted(up, "gy", 1)
    from_north = shifted(down, "gy", -1)
    chunk, low_face, high_face = pack(me, modes, salinity)
    chunk = tails(chunk, from_south, from_north)
    recv1 = lax.all_to_all(chunk, GX, 0, 0, tiled=True)
    send2 = inverse(recv1, *[jnp.asarray(x) for x in (*tables()["tw"], *tables()["inv"])])
    send2, low_face, high_face, recv1 = lax.optimization_barrier((send2, low_face, high_face, recv1))
    recv2 = lax.all_to_all(send2, GRP_GX, 0, 0, tiled=True)
    zlow = shifted(high_face, "grp", 1)
    zhigh = shifted(low_face, "grp", -1)
    base, parts, weights, consts = inner_levels(me, diffusivity, salinity, recv1, from_south, from_north)
    base, parts = outer_levels(me, diffusivity, salinity, zlow, zhigh, recv1, from_south, from_north, base, parts)
    salinity_next, spread = fine(grp, base, parts, recv2, consts)
    recv3 = lax.all_to_all(spread, GX, 0, 0, tiled=True)
    recv4 = lax.all_to_all(forward(recv3, *weights), "grp", 0, 0, tiled=True)
    coarse_next = finish(me, viscosity, forcing_gain, recv4, modes)
    return (salinity_next, coarse_next.reshape(coarse_modes.shape))


def solution(mesh):
    finer = Mesh(
        mesh.devices.reshape(mesh.shape["grp"], 2, 8, mesh.shape["gy"]),
        ("grp", "gx_0", "gx_1", "gy"),
    )
    in_specs = (P("grp", None, None, "gy", GX), P("grp", "gy", GX), P("grp"), P("grp"), P("grp"))
    out_specs = (P("grp", "gy", GX), P("grp", None, None, "gy", GX))
    return jax.shard_map(
        per_device, mesh=finer, in_specs=in_specs, out_specs=out_specs, check_vma=False
    )
```

```python
import functools
import math

import jax
import jax.numpy as jnp
import numpy as np
from jax import lax
from jax.experimental import pallas as pl
from jax.experimental.pallas import tpu as pltpu
from jax.sharding import Mesh
from jax.sharding import PartitionSpec as P

GX = ("gx_0", "gx_1")
GRP_GX = ("grp", "gx_0", "gx_1")
F32 = jnp.float32
BF16 = jnp.bfloat16
G = 16
NV = 4096
W = 256
FINE = 1024


def split_table(table):
    table = np.asarray(table, np.float64)
    high = table.astype(np.float32).astype(jnp.bfloat16)
    low = (table - high.astype(np.float64)).astype(np.float32).astype(jnp.bfloat16)
    return high, low


@functools.cache
def tables():
    out = {}
    k = np.arange(W)
    angle = 2 * np.pi * (np.outer(k, k) % W) / W
    norm = NV ** -0.5
    out["inv"] = split_table(np.concatenate([np.cos(angle), -np.sin(angle)], 0) * norm)
    r = np.arange(G)
    angle = 2 * np.pi * np.outer(r, k) / NV
    twc = np.zeros((G, 8, 128), np.float32)
    tws = np.zeros((G, 8, 128), np.float32)
    twc[:, :2] = np.cos(angle).reshape(G, 2, 128)
    tws[:, :2] = np.sin(angle).reshape(G, 2, 128)
    out["tw"] = (twc, tws)
    lanes = 16 * (k % 16) + k // 16
    order = np.argsort(lanes)
    assert np.array_equal(order, 16 * (k % 16) + k // 16)
    full = np.zeros((W + 2, FINE))
    for n in range(FINE):
        c, s = divmod(n, 4)
        o = (s + 0.5) / 4 - 0.5
        full[c + 1, n] += 1 - abs(o)
        full[c + 1 + (1 if o > 0 else -1), n] += abs(o)
    out["ref"] = full[1:-1][order].astype(jnp.bfloat16)
    edge = np.zeros((128, 256))
    edge[0, :128] = full[0, :128]
    edge[1, 128:] = full[-1, -128:]
    out["edge"] = edge.astype(jnp.bfloat16)
    ym = np.zeros((64, 32))
    yt = np.zeros((16, 32))
    place = lambda c: 16 if c < 0 else 17 if c > 15 else c
    for n in range(64):
        c, s = divmod(n, 4)
        o = (s + 0.5) / 4 - 0.5
        ym[n, c] += 1 - abs(o)
        ym[n, place(c + (1 if o > 0 else -1))] += abs(o)
    for c in range(16):
        yt[c, c] += 0.75
        yt[c, place(c - 1)] += 0.125
        yt[c, place(c + 1)] += 0.125
    out["ym"] = np.concatenate([ym, ym], 1).astype(jnp.bfloat16)
    out["yt"] = np.concatenate([yt, yt], 1).astype(jnp.bfloat16)
    cm = np.zeros((512, 128))
    cm[np.arange(512), np.arange(512) // 4] = 1.0 / 4
    out["cm"] = cm.astype(jnp.bfloat16)
    rm = np.zeros((32, 128))
    rm[np.arange(128) // 4, np.arange(128)] = 1.0 / 16
    out["rm"] = np.concatenate([rm, rm], 1).astype(jnp.bfloat16)
    g = np.arange(G)
    fine_angle = 2 * np.pi * np.outer(g, k) / NV
    coarse_angle = 2 * np.pi * (np.outer(g, k) % W) / W
    out["fwd"] = tuple(
        x.astype(np.float32)
        for x in (
            np.concatenate([np.cos(fine_angle), -np.sin(fine_angle)], 1) * norm,
            np.concatenate([np.cos(coarse_angle), -np.sin(coarse_angle)], 1),
        )
    )
    return out


def halves(x):
    high = x.astype(BF16)
    low = (x - high.astype(F32)).astype(BF16)
    return high, low


def mm(a, b):
    return jnp.dot(a, b, preferred_element_type=F32)


VM = pl.BlockSpec(memory_space=pltpu.VMEM)
SM = pl.BlockSpec(memory_space=pltpu.SMEM)
HB = pl.BlockSpec(memory_space=pltpu.HBM)


def call(kernel, out_shape, in_specs, out_specs, limit=12, **kw):
    inner = pl.pallas_call(
        kernel,
        out_shape=out_shape,
        in_specs=in_specs,
        out_specs=out_specs,
        compiler_params=pltpu.CompilerParams(vmem_limit_bytes=limit << 20),
        **kw,
    )

    def placed(*args):
        return inner(
            *[x if spec is not HB else pltpu.with_memory_space_constraint(x, pltpu.HBM) for x, spec in zip(args, in_specs)]
        )

    return placed


def fetch(pairs, sems, first=0):
    copies = [pltpu.make_async_copy(src, dst, sems.at[first + i]) for i, (src, dst) in enumerate(pairs)]
    for copy in copies:
        copy.start()
    return copies


def sds(*shape, dtype=F32):
    return jax.ShapeDtypeStruct(shape, dtype)


def vds(*shape, dtype=F32):
    return pltpu.VMEM(shape, dtype)


def hds(*shape, dtype=F32):
    return pltpu.HBM(shape, dtype)


def iota(shape, dim):
    return lax.broadcasted_iota(jnp.int32, shape, dim)


def roll(x, shift, axis):
    return pltpu.roll(x, shift % x.shape[axis], axis)


def lines_kernel(modes, sal, up, down, ends, south, north, sems):
    copies = fetch(
        (
            (modes.at[:, 0:8, :], ends.at[0]),
            (modes.at[:, 8:16, :], ends.at[1]),
            (sal.at[:, 0:8, :], south),
            (sal.at[:, 56:64, :], north),
        ),
        sems,
    )
    for copy in copies:
        copy.wait()
    for dst, rows, end, row in ((up, north, 1, 7), (down, south, 0, 0)):
        dst[0:16, :] = ends[end, :, row, :]
        face = rows[:, row, :]
        for j in range(4):
            dst[16 + 8 * j : 24 + 8 * j, :] = face[:, 256 * j : 256 * j + 256]


def outer_lines(modes, salinity):
    return call(
        lines_kernel,
        (vds(48, 256), vds(48, 256)),
        [HB, HB],
        [VM, VM],
        scratch_shapes=[
            pltpu.VMEM((2, 16, 8, 256), F32),
            pltpu.VMEM((8, 8, FINE), F32),
            pltpu.VMEM((8, 8, FINE), F32),
            pltpu.SemaphoreType.DMA((4,)),
        ],
        name="outer_lines",
    )(modes.reshape(16, 16, 256), salinity)


def pack_kernel(me, modes, sal, chunk, tail, low_face, high_face, modes_a, modes_b, west, east, faces, lines, sems, out_sems):
    copies = fetch(
        (
            (modes.at[:, 0:128], modes_a),
            (modes.at[:, 128:256], modes_b),
            (sal.at[0], faces.at[0]),
            (sal.at[7], faces.at[1]),
            (sal.at[:, :, 0:128], west),
            (sal.at[:, :, FINE - 128 :], east),
        ),
        sems,
    )
    for copy in copies[:2]:
        copy.wait()
    zero = jnp.zeros((8, 128), F32)
    for r in range(G):
        lines[r, 0:16, :] = modes_a[pl.ds(r, 16, stride=16), :]
        lines[r, 16:32, :] = modes_b[pl.ds(r, 16, stride=16), :]
        tail[r] = zero
    stores = [pltpu.make_async_copy(lines, chunk.at[:, 0:32, :], out_sems.at[0])]
    stores[0].start()
    for i, face in enumerate((low_face, high_face)):
        copies[2 + i].wait()
        stores.append(pltpu.make_async_copy(faces.at[i], face, out_sems.at[1 + i]))
        stores[-1].start()
    row_id = iota((8, 128), 0)

    def column(block, lane):
        tile = zero
        for i in range(4):
            both = jnp.concatenate([block[2 * i], block[2 * i + 1]], 0).T
            line = jnp.broadcast_to(both[lane : lane + 1, :], (8, 128))
            tile = jnp.where(row_id == 4 + i, line, tile)
        return tile

    for copy in copies[4:]:
        copy.wait()
    tail[(me[0] + 1) % G] = column(east, 127)
    tail[(me[0] + G - 1) % G] = column(west, 0)
    for store in stores:
        store.wait()


def pack(me, modes, salinity):
    return call(
        pack_kernel,
        (hds(G, 40, 128), vds(G, 8, 128), hds(64, FINE), hds(64, FINE)),
        [SM, HB, HB],
        [HB, VM, HB, HB],
        scratch_shapes=[
            pltpu.VMEM((256, 128), F32),
            pltpu.VMEM((256, 128), F32),
            pltpu.VMEM((8, 64, 128), F32),
            pltpu.VMEM((8, 64, 128), F32),
            pltpu.VMEM((2, 64, FINE), F32),
            pltpu.VMEM((G, 32, 128), F32),
            pltpu.SemaphoreType.DMA((6,)),
            pltpu.SemaphoreType.DMA((3,)),
        ],
        name="pack",
    )(me, modes, salinity)


def tails_kernel(chunk, tail, from_south, from_north, out, tiles, sem):
    row_id = iota((8, 128), 0)
    for r in range(G):
        rows = from_south if r < 8 else from_north
        p = r % 8
        tile = tail[r]
        parts = (rows[p : p + 1, :128], rows[p : p + 1, 128:], rows[8 + p : 9 + p, :128], rows[8 + p : 9 + p, 128:])
        for i, part in enumerate(parts):
            tile = jnp.where(row_id == i, jnp.broadcast_to(part, (8, 128)), tile)
        tiles[r] = tile
    store = pltpu.make_async_copy(tiles, out.at[:, 32:40, :], sem)
    store.start()
    store.wait()


def tails(chunk, tail, from_south, from_north):
    return call(
        tails_kernel,
        hds(G, 40, 128),
        [HB, VM, VM, VM],
        HB,
        input_output_aliases={0: 0},
        scratch_shapes=[pltpu.VMEM((G, 8, 128), F32), pltpu.SemaphoreType.DMA],
        name="tails",
    )(chunk, tail, from_south, from_north)


def cmul(a, b, c, s):
    return a * c - b * s, a * s + b * c


def four(z):
    (ar, ai), (br, bi), (cr, ci), (dr, di) = z
    t0r, t0i, t1r, t1i = ar + cr, ai + ci, ar - cr, ai - ci
    t2r, t2i, t3r, t3i = br + dr, bi + di, br - dr, bi - di
    return (
        (t0r + t2r, t0i + t2i),
        (t1r - t3i, t1i + t3r),
        (t0r - t2r, t0i - t2i),
        (t1r + t3i, t1i - t3r),
    )


def sixteen(z):
    inner = [four([z[4 * g1 + g0] for g1 in range(4)]) for g0 in range(4)]
    out = [None] * 16
    for r0 in range(4):
        column = []
        for g0 in range(4):
            angle = 2 * math.pi * g0 * r0 / 16
            a, b = inner[g0][r0]
            column.append((a, b) if g0 * r0 == 0 else cmul(a, b, math.cos(angle), math.sin(angle)))
        for r1, value in enumerate(four(column)):
            out[4 * r1 + r0] = value
    return out


def inverse_kernel(recv, twc, tws, inv_high, inv_low, send_hbm, left_high, left_low, mid, send, sems):
    row_id = iota((8, 128), 0)
    lane_id = iota((8, 128), 1)

    def put(r, top, part, value):
        high, low = halves(value)
        left_high[16 * r + 8 * top : 16 * r + 8 * top + 8, 128 * part : 128 * part + 128] = high
        left_low[16 * r + 8 * top : 16 * r + 8 * top + 8, 128 * part : 128 * part + 128] = low

    for h in range(2):
        z = [(recv[g, 16 * h : 16 * h + 8, :], recv[g, 16 * h + 8 : 16 * h + 16, :]) for g in range(G)]
        for r, (a, b) in enumerate(sixteen(z)):
            a, b = cmul(a, b, twc[r, h : h + 1, :], tws[r, h : h + 1, :])
            put(r, 0, h, a)
            put(r, 0, 2 + h, b)
    z = []
    for g in range(G):
        tile = jnp.where(row_id < 4, recv[g, 32:40, :], 0.0)
        z.append((tile, roll(tile, -2, 0)))
    for r, (a, b) in enumerate(sixteen(z)):
        a, b = cmul(a, b, twc[r], tws[r])
        for part, value in ((0, a), (2, b)):
            put(r, 1, part, jnp.where(row_id == 0, value, 0.0))
            put(r, 1, part + 1, jnp.where(row_id == 0, roll(value, -1, 0), 0.0))

    mid[...] = (
        mm(left_high[...], inv_high[...]) + mm(left_low[...], inv_high[...]) + mm(left_high[...], inv_low[...])
    )

    first, second, single = [], [], []
    for r in range(G):
        first.append(mid[16 * r : 16 * r + 8, 0:128])
        second.append(mid[16 * r : 16 * r + 8, 128:256])
        low = mid[16 * r + 8 : 16 * r + 16, 0:128]
        high = mid[16 * r + 8 : 16 * r + 16, 128:256]
        single.append(jnp.where(row_id == 0, low, roll(high, 1, 0)))
    for i in range(8):
        a, b = first[i], second[i]
        c, d = first[i + 8], second[i + 8]
        first[i], second[i], first[i + 8], second[i + 8] = a, c, b, d
        a, c = single[i], single[i + 8]
        single[i] = jnp.where(row_id == 0, a, roll(c, 1, 0))
        single[i + 8] = jnp.where(row_id == 0, roll(a, -1, 0), c)
    for bit in (4, 2, 1):
        upper = (lane_id // (16 * bit)) % 2 == 1
        for tiles in (first, second, single):
            for i in range(G):
                if i & bit:
                    continue
                a, b = tiles[i], tiles[i | bit]
                tiles[i] = jnp.where(upper, roll(b, 16 * bit, 1), a)
                tiles[i | bit] = jnp.where(upper, b, roll(a, -16 * bit, 1))

    left = [roll(second[d], 1, 1) for d in range(G)]
    right = [roll(first[d], 1, 1) for d in range(G)]
    side = [roll(single[d], 5, 1) for d in range(G)]
    stores = []
    for d in range(G):
        before, after = (d - 1) % G, (d + 1) % G
        own = jnp.where(lane_id == 0, left[before], jnp.where(lane_id == 1, right[after], 0.0))
        rim = own + roll(roll(own, -1, 0), 2, 1)
        base = jnp.where(row_id == 2, roll(single[d], 2, 0), 0.0)
        base = jnp.where(row_id == 6, roll(single[d], 5, 0), base)
        base = jnp.where((row_id == 3) & (lane_id == 4), roll(side[before], 2, 0), base)
        base = jnp.where((row_id == 3) & (lane_id == 5), roll(side[after], 3, 0), base)
        for g in range(4):
            tile = jnp.where(row_id < 2, roll(first[d], -2 * g, 0), base)
            tile = jnp.where((row_id == 4) | (row_id == 5), roll(second[d], 4 - 2 * g, 0), tile)
            tile = jnp.where((row_id == 3) & (lane_id < 4), roll(rim, 3 - 2 * g, 0), tile)
            send[g, d] = tile
        if d % 4 == 3:
            ds = slice(d - 3, d + 1)
            stores += fetch(((send.at[:, ds], send_hbm.at[:, ds]),), sems, d // 4)
    for store in stores:
        store.wait()


def inverse(recv, twc, tws, high, low):
    return call(
        inverse_kernel,
        hds(4, G, 8, 128),
        [VM] * 5,
        HB,
        scratch_shapes=[
            pltpu.VMEM((256, 512), BF16),
            pltpu.VMEM((256, 512), BF16),
            pltpu.VMEM((256, 256), F32),
            pltpu.VMEM((4, G, 8, 128), F32),
            pltpu.SemaphoreType.DMA((4,)),
        ],
        name="inverse",
    )(recv, twc, tws, high, low).reshape(64, 8, 128)


EARLY = ("ym", "yt", "edge", "ref", "rm", "cm")


def still_kernel(me, rate_hbm, sal_hbm, zlow_hbm, zhigh_hbm, edge_cols, from_south, from_north, *rest):
    count = len(EARLY)
    hbm, (base, parts_hbm), kept, rest = rest[:count], rest[count : count + 2], rest[count + 2 : 2 * count + 2], rest[2 * count + 2 :]
    rate, salinity, zlow, zhigh, parts, sems, const_sems, out_sems = rest
    copies = fetch(((rate_hbm, rate), (sal_hbm, salinity), (zlow_hbm, zlow), (zhigh_hbm, zhigh)), sems)
    stores = fetch(tuple(zip(hbm, kept)), const_sems)
    west_t = edge_cols[(me[0] + G - 1) % G, 32:40, :].T
    east_t = edge_cols[(me[0] + 1) % G, 32:40, :].T
    last_row = iota((8, FINE), 0) == 7
    first_row = iota((8, FINE), 0) == 0
    last_lane = iota((8, 128), 1) == 127
    first_lane = iota((8, 128), 1) == 0

    def outer(rows, l):
        line = jnp.concatenate([rows[16 + 8 * j + l : 17 + 8 * j + l, :] for j in range(4)], 1)
        return jnp.broadcast_to(line, (8, FINE))

    for copy in copies:
        copy.wait()
    for yb in range(8):
        ys = slice(8 * yb, 8 * yb + 8)
        for l in range(8):
            c = salinity[l, ys, :]
            upper = salinity[l + 1, ys, :] if l < 7 else zhigh[ys, :]
            lower = salinity[l - 1, ys, :] if l > 0 else zlow[ys, :]
            if yb < 7:
                north = salinity[l, 8 * yb + 1 : 8 * yb + 9, :]
            else:
                north = jnp.where(last_row, outer(from_north, l), roll(c, -1, 0))
            if yb > 0:
                south = salinity[l, 8 * yb - 1 : 8 * yb + 7, :]
            else:
                south = jnp.where(first_row, outer(from_south, l), roll(c, 1, 0))
            at = (l % 2) * 64 + 8 * yb
            ecol = jnp.broadcast_to(east_t[at : at + 8, 4 + l // 2 : 5 + l // 2], (8, 128))
            wcol = jnp.broadcast_to(west_t[at : at + 8, 4 + l // 2 : 5 + l // 2], (8, 128))
            e = roll(c, -1, 1)
            w = roll(c, 1, 1)
            e = jnp.concatenate([e[:, :-128], jnp.where(last_lane, ecol, e[:, -128:])], 1)
            w = jnp.concatenate([jnp.where(first_lane, wcol, w[:, :128]), w[:, 128:]], 1)
            k = rate[l] * 0.1
            base[l, ys, :] = c + k * (((e + w) + (north + south)) + (upper + lower) - 6.0 * c)
            parts[0, l, ys, :] = (e - w) * 0.05
            parts[1, l, ys, :] = (north - south) * 0.05
            parts[2, l, ys, :] = (upper - lower) * 0.05
        stores.append(pltpu.make_async_copy(parts.at[:, :, ys, :], parts_hbm.at[:, :, ys, :], out_sems.at[yb]))
        stores[-1].start()
    for store in stores:
        store.wait()


def still(me, rate, salinity, zlow, zhigh, recv1, from_south, from_north):
    consts = [jnp.asarray(tables()[name]) for name in EARLY]
    return call(
        still_kernel,
        [vds(8, 64, FINE), hds(3, 8, 64, FINE)] + [vds(*x.shape, dtype=x.dtype) for x in consts],
        [SM, HB, HB, HB, HB, VM, VM, VM] + [HB] * len(consts),
        [VM, HB] + [VM] * len(consts),
        scratch_shapes=[
            pltpu.SMEM((8,), F32),
            pltpu.VMEM((8, 64, FINE), F32),
            pltpu.VMEM((64, FINE), F32),
            pltpu.VMEM((64, FINE), F32),
            pltpu.VMEM((3, 8, 64, FINE), F32),
            pltpu.SemaphoreType.DMA((4,)),
            pltpu.SemaphoreType.DMA((len(consts),)),
            pltpu.SemaphoreType.DMA((8,)),
        ],
        limit=24,
        name="still",
    )(me, rate, salinity, zlow, zhigh, recv1, from_south, from_north, *consts)


def fine_kernel(
    grp_ref,
    base,
    parts_hbm,
    recv,
    ym,
    yt,
    edge,
    ref,
    rm,
    cm,
    out,
    spread,
    y_high,
    y_low,
    side_high,
    side_low,
    vel,
    total,
    parts,
    in_sems,
):
    rows = [slice(8 * yb, 8 * yb + 8) for yb in range(8)]
    loads = fetch([(parts_hbm.at[:, :, ys, :], parts.at[:, :, ys, :]) for ys in rows], in_sems)
    grp = grp_ref[0]
    row_id = iota((8, 128), 0)
    lane_id = iota((8, 128), 1)

    def lines(f, q):
        main = [recv[pl.ds(f * 128 + i, 16, stride=8), :] for i in (q, 4 + q, 3)]
        south = recv[pl.ds(pl.multiple_of((f * 16 + 2 * grp + q) * 8, 8), 8), :]
        north = recv[pl.ds(pl.multiple_of((f * 16 + 8 + 2 * grp + q) * 8, 8), 8), :]
        parts = []
        for x, row in zip(main, (2, 6, 3)):
            s, n = roll(south, -row, 0), roll(north, 1 - row, 0)
            if row == 3:
                x, s, n = roll(x, -2 * q, 1), roll(s, -4, 1), roll(n, -4, 1)
            tile = jnp.where(row_id == 0, s, jnp.where(row_id == 1, n, 0.0))
            parts.append(jnp.concatenate([x, tile, jnp.zeros((8, 128), F32)], 0))
        return jnp.concatenate(parts, 1)

    def along_y(table, f, q):
        high, low = halves(lines(f, q))
        return mm(table[...], jnp.concatenate([high, low], 0))

    for f in range(4):
        for q in range(2):
            at = slice(64 * (2 * f + q), 64 * (2 * f + q) + 64) if f < 3 else slice(384 + 16 * q, 400 + 16 * q)
            high, low = halves(along_y(ym if f < 3 else yt, f, q))
            y_high[at, :], side_high[at, :] = high[:, :256], high[:, 256:]
            y_low[at, :], side_low[at, :] = low[:, :256], low[:, 256:]
    vel[...] = mm(y_high[...], ref[...]) + mm(y_low[...], ref[...])
    side = mm(side_high[...], edge[...]) + mm(side_low[...], edge[...])
    vel[:, :128] += side[:, :128]
    vel[:, FINE - 128 :] += side[:, 128:]

    for yb in range(8):
        ys = rows[yb]
        loads[yb].wait()
        for q in range(2):
            vx, vy, vz = (vel[64 * (2 * f + q) + 8 * yb : 64 * (2 * f + q) + 8 * yb + 8, :] for f in range(3))
            acc = None
            for l in range(4 * q, 4 * q + 4):
                new = base[l, ys, :] - (vx * parts[0, l, ys, :] + vy * parts[1, l, ys, :] + vz * parts[2, l, ys, :])
                out[l, ys, :] = new
                acc = new if acc is None else acc + new
            total[64 * q + 8 * yb : 64 * q + 8 * yb + 8, :] = acc
    high, low = halves(total[...])
    high, low = halves(vel[384:416, :] - mm(rm[...], jnp.concatenate([high, low], 0)))
    means = [mm(high[:, at], cm[...]) + mm(low[:, at], cm[...]) for at in (slice(0, 512), slice(512, FINE))]
    mean = jnp.concatenate(means, 1)
    for a in range(G):
        spread[a] = mean


def fine(grp, base, parts, recv2, consts):
    return call(
        fine_kernel,
        (vds(8, 64, FINE), vds(G, 32, 256)),
        [SM, VM, HB, VM] + [VM] * len(consts),
        [VM, VM],
        input_output_aliases={1: 0},
        scratch_shapes=[
            pltpu.VMEM((416, 256), BF16),
            pltpu.VMEM((416, 256), BF16),
            pltpu.VMEM((416, 128), BF16),
            pltpu.VMEM((416, 128), BF16),
            pltpu.VMEM((416, FINE), F32),
            pltpu.VMEM((128, FINE), F32),
            pltpu.VMEM((3, 8, 64, FINE), F32),
            pltpu.SemaphoreType.DMA((8,)),
        ],
        limit=20,
        name="fine",
    )(grp, base, parts, recv2.reshape(512, 128), *consts)


def stage_kernel(me, inner_hbm, outer_hbm, *rest):
    count = (len(rest) - 8) // 2
    hbm, dst, rest = rest[:count], rest[count : 2 * count], rest[2 * count :]
    high_hbm, low_hbm, high, low, inner, outer, sems, out_sems = rest
    copies = fetch(((inner_hbm, inner), (outer_hbm, outer)) + tuple(zip(hbm, dst)), sems)
    turns = (iota((16, 128), 0) * me[0]) % G
    angle = turns.astype(F32) * (2.0 * math.pi / G)
    cos = jnp.concatenate([jnp.cos(angle)] * 2, 1)
    sin = -jnp.concatenate([jnp.sin(angle)] * 2, 1)
    copies[0].wait()
    copies[1].wait()
    real, imag = cmul(inner[:, :256], inner[:, 256:], cos, sin)
    for t in range(G):
        rows = slice(16 * t, 16 * t + 16)
        value = cmul(real, imag, outer[t : t + 1, :256], outer[t : t + 1, 256:])
        for at in range(2):
            high[rows, 256 * at : 256 * at + 256], low[rows, 256 * at : 256 * at + 256] = halves(value[at])
    for copy in copies[2:] + fetch(((high, high_hbm), (low, low_hbm)), out_sems):
        copy.wait()


def stage(me):
    t = tables()
    consts = [jnp.asarray(x) for x in (*t["tw"], *t["inv"])]
    out = call(
        stage_kernel,
        [vds(*x.shape, dtype=x.dtype) for x in consts] + [hds(256, 512, dtype=BF16)] * 2,
        [SM, HB, HB] + [HB] * len(consts),
        [VM] * len(consts) + [HB] * 2,
        scratch_shapes=[
            pltpu.VMEM((256, 512), BF16),
            pltpu.VMEM((256, 512), BF16),
            pltpu.VMEM((G, 512), F32),
            pltpu.VMEM((G, 512), F32),
            pltpu.SemaphoreType.DMA((len(consts) + 2,)),
            pltpu.SemaphoreType.DMA((2,)),
        ],
        name="stage",
    )(me, *map(jnp.asarray, t["fwd"]), *consts)
    return out[0:4], out[4:6]


def forward_kernel(recv, table_high, table_low, out, left_high, left_low, mid):
    turns = (iota((G, 128), 0) * iota((G, 128), 1)) % G
    angle = turns.astype(F32) * (2.0 * math.pi / G)
    comb_cos = jnp.concatenate([jnp.cos(angle)] * 2, 1)
    comb_sin = jnp.concatenate([jnp.sin(angle)] * 2, 1)
    for a in range(G):
        high, low = halves(recv[a])
        left_high[32 * a : 32 * a + 32, :] = high
        left_low[32 * a : 32 * a + 32, :] = low
    mid[...] = (
        mm(left_high[...], table_high[...]) + mm(left_low[...], table_high[...]) + mm(left_high[...], table_low[...])
    )
    real = imag = jnp.zeros((32, 256), F32)
    for a in range(G):
        c, s = comb_cos[a : a + 1, :], comb_sin[a : a + 1, :]
        x, y = mid[32 * a : 32 * a + 32, :256], mid[32 * a : 32 * a + 32, 256:]
        real = real + (x * c + y * s)
        imag = imag + (y * c - x * s)
    for g in range(4):
        out[g, 0:32, :] = real
        out[g, 32:64, :] = imag


def forward(recv, high, low):
    return call(
        forward_kernel,
        sds(4, 64, 256),
        [VM, VM, VM],
        VM,
        scratch_shapes=[
            pltpu.VMEM((512, 256), BF16),
            pltpu.VMEM((512, 256), BF16),
            pltpu.VMEM((512, 512), F32),
        ],
        name="forward",
    )(recv, high, low)


def finish_kernel(me, viscosity, gain, recv, modes, out):
    index = me[0] * W + iota((8, W), 1)
    number = jnp.where(index < NV // 2, index, index - NV).astype(F32)
    wave = (2.0 * math.pi / NV) * number
    damping = jnp.exp(-viscosity[0] * wave * wave)[0:1, :]
    for c in range(2):
        for g in range(4):
            at = slice(128 * c + 32 * g, 128 * c + 32 * g + 32)
            out[at, :] = damping * modes[at, :] + gain[0] * recv[g, 32 * c : 32 * c + 32, :]


def finish(me, viscosity, gain, recv, modes):
    return call(finish_kernel, sds(256, W), [SM, SM, SM, VM, VM], VM, name="finish")(
        me, viscosity, gain, recv, modes
    )


def shifted(array, axis, step):
    count = lax.axis_size(axis)
    return lax.ppermute(array, axis, [(i, (i + step) % count) for i in range(count)])


def per_device(coarse_modes, salinity, viscosity, forcing_gain, diffusivity):
    me = lax.axis_index(GX).astype(jnp.int32).reshape(1)
    grp = lax.axis_index("grp").astype(jnp.int32).reshape(1)
    modes = coarse_modes.reshape(256, 256)
    up, down = outer_lines(modes, salinity)
    from_south = shifted(up, "gy", 1)
    from_north = shifted(down, "gy", -1)
    chunk, tail, low_face, high_face = pack(me, modes, salinity)
    chunk = tails(chunk, tail, from_south, from_north)
    recv1 = lax.all_to_all(chunk, GX, 0, 0, tiled=True)
    inv, weights = stage(me)
    zlow = shifted(high_face, "grp", 1)
    zhigh = shifted(low_face, "grp", -1)
    recv1, zlow, zhigh = lax.optimization_barrier((recv1, zlow, zhigh))
    send2 = inverse(recv1, *inv)
    recv2 = lax.all_to_all(send2, GRP_GX, 0, 0, tiled=True)
    base, parts, *consts = still(me, diffusivity, salinity, zlow, zhigh, recv1, from_south, from_north)
    salinity_next, spread = fine(grp, base, parts, recv2, consts)
    recv3 = lax.all_to_all(spread, GX, 0, 0, tiled=True)
    recv4 = lax.all_to_all(forward(recv3, *weights), "grp", 0, 0, tiled=True)
    coarse_next = finish(me, viscosity, forcing_gain, recv4, modes)
    return (salinity_next, coarse_next.reshape(coarse_modes.shape))


def solution(mesh):
    finer = Mesh(
        mesh.devices.reshape(mesh.shape["grp"], 2, 8, mesh.shape["gy"]),
        ("grp", "gx_0", "gx_1", "gy"),
    )
    in_specs = (P("grp", None, None, "gy", GX), P("grp", "gy", GX), P("grp"), P("grp"), P("grp"))
    out_specs = (P("grp", "gy", GX), P("grp", None, None, "gy", GX))
    return jax.shard_map(
        per_device, mesh=finer, in_specs=in_specs, out_specs=out_specs, check_vma=False
    )
```

```python
import functools
import math

import jax
import jax.numpy as jnp
import numpy as np
from jax import lax
from jax.experimental import pallas as pl
from jax.experimental.pallas import tpu as pltpu
from jax.sharding import Mesh
from jax.sharding import PartitionSpec as P

GX = ("gx_0", "gx_1")
GRP_GX = ("grp", "gx_0", "gx_1")
F32 = jnp.float32
BF16 = jnp.bfloat16
G = 16
NV = 4096
W = 256
FINE = 1024


def split_table(table):
    table = np.asarray(table, np.float64)
    high = table.astype(np.float32).astype(jnp.bfloat16)
    low = (table - high.astype(np.float64)).astype(np.float32).astype(jnp.bfloat16)
    return high, low


@functools.cache
def tables():
    out = {}
    k = np.arange(W)
    angle = 2 * np.pi * (np.outer(k, k) % W) / W
    norm = NV ** -0.5
    out["inv"] = split_table(np.concatenate([np.cos(angle), -np.sin(angle)], 0) * norm)
    r = np.arange(G)
    angle = 2 * np.pi * np.outer(r, k) / NV
    twc = np.zeros((G, 8, 128), np.float32)
    tws = np.zeros((G, 8, 128), np.float32)
    twc[:, :2] = np.cos(angle).reshape(G, 2, 128)
    tws[:, :2] = np.sin(angle).reshape(G, 2, 128)
    out["tw"] = (twc, tws)
    lanes = 16 * (k % 16) + k // 16
    order = np.argsort(lanes)
    assert np.array_equal(order, 16 * (k % 16) + k // 16)
    full = np.zeros((W + 2, FINE))
    for n in range(FINE):
        c, s = divmod(n, 4)
        o = (s + 0.5) / 4 - 0.5
        full[c + 1, n] += 1 - abs(o)
        full[c + 1 + (1 if o > 0 else -1), n] += abs(o)
    out["ref"] = full[1:-1][order].astype(jnp.bfloat16)
    edge = np.zeros((128, 256))
    edge[0, :128] = full[0, :128]
    edge[1, 128:] = full[-1, -128:]
    out["edge"] = edge.astype(jnp.bfloat16)
    ym = np.zeros((64, 32))
    yt = np.zeros((16, 32))
    place = lambda c: 16 if c < 0 else 17 if c > 15 else c
    for n in range(64):
        c, s = divmod(n, 4)
        o = (s + 0.5) / 4 - 0.5
        ym[n, c] += 1 - abs(o)
        ym[n, place(c + (1 if o > 0 else -1))] += abs(o)
    for c in range(16):
        yt[c, c] += 0.75
        yt[c, place(c - 1)] += 0.125
        yt[c, place(c + 1)] += 0.125
    out["ym"] = np.concatenate([ym, ym], 1).astype(jnp.bfloat16)
    out["yt"] = np.concatenate([yt, yt], 1).astype(jnp.bfloat16)
    cm = np.zeros((512, 128))
    cm[np.arange(512), np.arange(512) // 4] = 1.0 / 4
    out["cm"] = cm.astype(jnp.bfloat16)
    rm = np.zeros((32, 128))
    rm[np.arange(128) // 4, np.arange(128)] = 1.0 / 16
    out["rm"] = np.concatenate([rm, rm], 1).astype(jnp.bfloat16)
    g = np.arange(G)
    fine_angle = 2 * np.pi * np.outer(g, k) / NV
    coarse_angle = 2 * np.pi * (np.outer(g, k) % W) / W
    out["fwd"] = tuple(
        x.astype(np.float32)
        for x in (
            np.concatenate([np.cos(fine_angle), -np.sin(fine_angle)], 1) * norm,
            np.concatenate([np.cos(coarse_angle), -np.sin(coarse_angle)], 1),
        )
    )
    return out


def halves(x):
    high = x.astype(BF16)
    low = (x - high.astype(F32)).astype(BF16)
    return high, low


def mm(a, b):
    return jnp.dot(a, b, preferred_element_type=F32)


VM = pl.BlockSpec(memory_space=pltpu.VMEM)
SM = pl.BlockSpec(memory_space=pltpu.SMEM)
HB = pl.BlockSpec(memory_space=pltpu.HBM)


def call(kernel, out_shape, in_specs, out_specs, limit=12, **kw):
    inner = pl.pallas_call(
        kernel,
        out_shape=out_shape,
        in_specs=in_specs,
        out_specs=out_specs,
        compiler_params=pltpu.CompilerParams(vmem_limit_bytes=limit << 20),
        **kw,
    )

    def placed(*args):
        return inner(
            *[x if spec is not HB else pltpu.with_memory_space_constraint(x, pltpu.HBM) for x, spec in zip(args, in_specs)]
        )

    return placed


def fetch(pairs, sems, first=0):
    copies = [pltpu.make_async_copy(src, dst, sems.at[first + i]) for i, (src, dst) in enumerate(pairs)]
    for copy in copies:
        copy.start()
    return copies


def sds(*shape, dtype=F32):
    return jax.ShapeDtypeStruct(shape, dtype)


def vds(*shape, dtype=F32):
    return pltpu.VMEM(shape, dtype)


def hds(*shape, dtype=F32):
    return pltpu.HBM(shape, dtype)


def iota(shape, dim):
    return lax.broadcasted_iota(jnp.int32, shape, dim)


def roll(x, shift, axis):
    return pltpu.roll(x, shift % x.shape[axis], axis)


def lines_kernel(modes, sal, up, down, low_face, high_face, ends, south, north, sems):
    copies = fetch(
        (
            (modes.at[:, 0:8, :], ends.at[0]),
            (modes.at[:, 8:16, :], ends.at[1]),
            (sal.at[:, 0:8, :], south),
            (sal.at[:, 56:64, :], north),
            (sal.at[0], low_face),
            (sal.at[7], high_face),
        ),
        sems,
    )
    for copy in copies:
        copy.wait()
    for dst, rows, end, row in ((up, north, 1, 7), (down, south, 0, 0)):
        dst[0:16, :] = ends[end, :, row, :]
        face = rows[:, row, :]
        for j in range(4):
            dst[16 + 8 * j : 24 + 8 * j, :] = face[:, 256 * j : 256 * j + 256]


def outer_lines(modes, salinity):
    return call(
        lines_kernel,
        (vds(48, 256), vds(48, 256), vds(64, FINE), vds(64, FINE)),
        [HB, HB],
        [VM] * 4,
        scratch_shapes=[
            pltpu.VMEM((2, 16, 8, 256), F32),
            pltpu.VMEM((8, 8, FINE), F32),
            pltpu.VMEM((8, 8, FINE), F32),
            pltpu.SemaphoreType.DMA((6,)),
        ],
        name="outer_lines",
    )(modes.reshape(16, 16, 256), salinity)


def pack_kernel(me, modes, sal, chunk, modes_a, modes_b, west, east, sems):
    copies = fetch(
        (
            (modes.at[:, 0:128], modes_a),
            (modes.at[:, 128:256], modes_b),
            (sal.at[:, :, 0:128], west),
            (sal.at[:, :, FINE - 128 :], east),
        ),
        sems,
    )
    for copy in copies[:2]:
        copy.wait()
    zero = jnp.zeros((8, 128), F32)
    for r in range(G):
        chunk[r, 0:16, :] = modes_a[pl.ds(r, 16, stride=16), :]
        chunk[r, 16:32, :] = modes_b[pl.ds(r, 16, stride=16), :]
        chunk[r, 32:40, :] = zero
    row_id = iota((8, 128), 0)

    def column(block, lane):
        tile = zero
        for i in range(4):
            both = jnp.concatenate([block[2 * i], block[2 * i + 1]], 0).T
            line = jnp.broadcast_to(both[lane : lane + 1, :], (8, 128))
            tile = jnp.where(row_id == 4 + i, line, tile)
        return tile

    for copy in copies[2:]:
        copy.wait()
    chunk[(me[0] + 1) % G, 32:40, :] = column(east, 127)
    chunk[(me[0] + G - 1) % G, 32:40, :] = column(west, 0)


def pack(me, modes, salinity):
    return call(
        pack_kernel,
        vds(G, 40, 128),
        [SM, HB, HB],
        VM,
        scratch_shapes=[
            pltpu.VMEM((256, 128), F32),
            pltpu.VMEM((256, 128), F32),
            pltpu.VMEM((8, 64, 128), F32),
            pltpu.VMEM((8, 64, 128), F32),
            pltpu.SemaphoreType.DMA((4,)),
        ],
        name="pack",
    )(me, modes, salinity)


def tails_kernel(chunk, from_south, from_north, out):
    row_id = iota((8, 128), 0)
    for r in range(G):
        rows = from_south if r < 8 else from_north
        p = r % 8
        tile = chunk[r, 32:40, :]
        parts = (rows[p : p + 1, :128], rows[p : p + 1, 128:], rows[8 + p : 9 + p, :128], rows[8 + p : 9 + p, 128:])
        for i, part in enumerate(parts):
            tile = jnp.where(row_id == i, jnp.broadcast_to(part, (8, 128)), tile)
        out[r, 32:40, :] = tile


def tails(chunk, from_south, from_north):
    return call(
        tails_kernel,
        vds(G, 40, 128),
        [VM, VM, VM],
        VM,
        input_output_aliases={0: 0},
        name="tails",
    )(chunk, from_south, from_north)


def cmul(a, b, c, s):
    return a * c - b * s, a * s + b * c


def four(z):
    (ar, ai), (br, bi), (cr, ci), (dr, di) = z
    t0r, t0i, t1r, t1i = ar + cr, ai + ci, ar - cr, ai - ci
    t2r, t2i, t3r, t3i = br + dr, bi + di, br - dr, bi - di
    return (
        (t0r + t2r, t0i + t2i),
        (t1r - t3i, t1i + t3r),
        (t0r - t2r, t0i - t2i),
        (t1r + t3i, t1i - t3r),
    )


def sixteen(z):
    inner = [four([z[4 * g1 + g0] for g1 in range(4)]) for g0 in range(4)]
    out = [None] * 16
    for r0 in range(4):
        column = []
        for g0 in range(4):
            angle = 2 * math.pi * g0 * r0 / 16
            a, b = inner[g0][r0]
            column.append((a, b) if g0 * r0 == 0 else cmul(a, b, math.cos(angle), math.sin(angle)))
        for r1, value in enumerate(four(column)):
            out[4 * r1 + r0] = value
    return out


def inverse_kernel(recv, twc, tws, inv_high, inv_low, send_hbm, left_high, left_low, mid, send, sems):
    row_id = iota((8, 128), 0)
    lane_id = iota((8, 128), 1)

    def put(r, top, part, value):
        high, low = halves(value)
        left_high[16 * r + 8 * top : 16 * r + 8 * top + 8, 128 * part : 128 * part + 128] = high
        left_low[16 * r + 8 * top : 16 * r + 8 * top + 8, 128 * part : 128 * part + 128] = low

    for h in range(2):
        z = [(recv[g, 16 * h : 16 * h + 8, :], recv[g, 16 * h + 8 : 16 * h + 16, :]) for g in range(G)]
        for r, (a, b) in enumerate(sixteen(z)):
            a, b = cmul(a, b, twc[r, h : h + 1, :], tws[r, h : h + 1, :])
            put(r, 0, h, a)
            put(r, 0, 2 + h, b)
    z = []
    for g in range(G):
        tile = jnp.where(row_id < 4, recv[g, 32:40, :], 0.0)
        z.append((tile, roll(tile, -2, 0)))
    for r, (a, b) in enumerate(sixteen(z)):
        a, b = cmul(a, b, twc[r], tws[r])
        for part, value in ((0, a), (2, b)):
            put(r, 1, part, jnp.where(row_id == 0, value, 0.0))
            put(r, 1, part + 1, jnp.where(row_id == 0, roll(value, -1, 0), 0.0))

    mid[...] = (
        mm(left_high[...], inv_high[...]) + mm(left_low[...], inv_high[...]) + mm(left_high[...], inv_low[...])
    )

    first, second, single = [], [], []
    for r in range(G):
        first.append(mid[16 * r : 16 * r + 8, 0:128])
        second.append(mid[16 * r : 16 * r + 8, 128:256])
        low = mid[16 * r + 8 : 16 * r + 16, 0:128]
        high = mid[16 * r + 8 : 16 * r + 16, 128:256]
        single.append(jnp.where(row_id == 0, low, roll(high, 1, 0)))
    for i in range(8):
        a, b = first[i], second[i]
        c, d = first[i + 8], second[i + 8]
        first[i], second[i], first[i + 8], second[i + 8] = a, c, b, d
        a, c = single[i], single[i + 8]
        single[i] = jnp.where(row_id == 0, a, roll(c, 1, 0))
        single[i + 8] = jnp.where(row_id == 0, roll(a, -1, 0), c)
    for bit in (4, 2, 1):
        upper = (lane_id // (16 * bit)) % 2 == 1
        for tiles in (first, second, single):
            for i in range(G):
                if i & bit:
                    continue
                a, b = tiles[i], tiles[i | bit]
                tiles[i] = jnp.where(upper, roll(b, 16 * bit, 1), a)
                tiles[i | bit] = jnp.where(upper, b, roll(a, -16 * bit, 1))

    left = [roll(second[d], 1, 1) for d in range(G)]
    right = [roll(first[d], 1, 1) for d in range(G)]
    side = [roll(single[d], 5, 1) for d in range(G)]
    stores = []
    for d in range(G):
        before, after = (d - 1) % G, (d + 1) % G
        own = jnp.where(lane_id == 0, left[before], jnp.where(lane_id == 1, right[after], 0.0))
        rim = own + roll(roll(own, -1, 0), 2, 1)
        base = jnp.where(row_id == 2, roll(single[d], 2, 0), 0.0)
        base = jnp.where(row_id == 6, roll(single[d], 5, 0), base)
        base = jnp.where((row_id == 3) & (lane_id == 4), roll(side[before], 2, 0), base)
        base = jnp.where((row_id == 3) & (lane_id == 5), roll(side[after], 3, 0), base)
        for g in range(4):
            tile = jnp.where(row_id < 2, roll(first[d], -2 * g, 0), base)
            tile = jnp.where((row_id == 4) | (row_id == 5), roll(second[d], 4 - 2 * g, 0), tile)
            tile = jnp.where((row_id == 3) & (lane_id < 4), roll(rim, 3 - 2 * g, 0), tile)
            send[g, d] = tile
        if d % 4 == 3:
            ds = slice(d - 3, d + 1)
            stores += fetch(((send.at[:, ds], send_hbm.at[:, ds]),), sems, d // 4)
    for store in stores:
        store.wait()


def inverse(recv, twc, tws, high, low):
    return call(
        inverse_kernel,
        hds(4, G, 8, 128),
        [VM] * 5,
        HB,
        scratch_shapes=[
            pltpu.VMEM((256, 512), BF16),
            pltpu.VMEM((256, 512), BF16),
            pltpu.VMEM((256, 256), F32),
            pltpu.VMEM((4, G, 8, 128), F32),
            pltpu.SemaphoreType.DMA((4,)),
        ],
        name="inverse",
    )(recv, twc, tws, high, low).reshape(64, 8, 128)


EARLY = ("ym", "yt", "edge", "ref", "rm", "cm")


def still_kernel(me, rate_hbm, sal_hbm, zlow_hbm, zhigh_hbm, edge_cols, from_south, from_north, *rest):
    count = len(EARLY)
    hbm, (base, parts_hbm), kept, rest = rest[:count], rest[count : count + 2], rest[count + 2 : 2 * count + 2], rest[2 * count + 2 :]
    rate, salinity, zlow, zhigh, parts, sems, const_sems, out_sems = rest
    copies = fetch(((rate_hbm, rate), (sal_hbm, salinity), (zlow_hbm, zlow), (zhigh_hbm, zhigh)), sems)
    stores = fetch(tuple(zip(hbm, kept)), const_sems)
    west_t = edge_cols[(me[0] + G - 1) % G, 32:40, :].T
    east_t = edge_cols[(me[0] + 1) % G, 32:40, :].T
    last_row = iota((8, FINE), 0) == 7
    first_row = iota((8, FINE), 0) == 0
    last_lane = iota((8, 128), 1) == 127
    first_lane = iota((8, 128), 1) == 0

    def outer(rows, l):
        line = jnp.concatenate([rows[16 + 8 * j + l : 17 + 8 * j + l, :] for j in range(4)], 1)
        return jnp.broadcast_to(line, (8, FINE))

    for copy in copies:
        copy.wait()
    for yb in range(8):
        ys = slice(8 * yb, 8 * yb + 8)
        for l in range(8):
            c = salinity[l, ys, :]
            upper = salinity[l + 1, ys, :] if l < 7 else zhigh[ys, :]
            lower = salinity[l - 1, ys, :] if l > 0 else zlow[ys, :]
            if yb < 7:
                north = salinity[l, 8 * yb + 1 : 8 * yb + 9, :]
            else:
                north = jnp.where(last_row, outer(from_north, l), roll(c, -1, 0))
            if yb > 0:
                south = salinity[l, 8 * yb - 1 : 8 * yb + 7, :]
            else:
                south = jnp.where(first_row, outer(from_south, l), roll(c, 1, 0))
            at = (l % 2) * 64 + 8 * yb
            ecol = jnp.broadcast_to(east_t[at : at + 8, 4 + l // 2 : 5 + l // 2], (8, 128))
            wcol = jnp.broadcast_to(west_t[at : at + 8, 4 + l // 2 : 5 + l // 2], (8, 128))
            e = roll(c, -1, 1)
            w = roll(c, 1, 1)
            e = jnp.concatenate([e[:, :-128], jnp.where(last_lane, ecol, e[:, -128:])], 1)
            w = jnp.concatenate([jnp.where(first_lane, wcol, w[:, :128]), w[:, 128:]], 1)
            k = rate[l] * 0.1
            base[l, ys, :] = c + k * (((e + w) + (north + south)) + (upper + lower) - 6.0 * c)
            parts[0, l, ys, :] = (e - w) * 0.05
            parts[1, l, ys, :] = (north - south) * 0.05
            parts[2, l, ys, :] = (upper - lower) * 0.05
        stores.append(pltpu.make_async_copy(parts.at[:, :, ys, :], parts_hbm.at[:, :, ys, :], out_sems.at[yb]))
        stores[-1].start()
    for store in stores:
        store.wait()


def still(me, rate, salinity, zlow, zhigh, recv1, from_south, from_north):
    consts = [jnp.asarray(tables()[name]) for name in EARLY]
    return call(
        still_kernel,
        [vds(8, 64, FINE), hds(3, 8, 64, FINE)] + [vds(*x.shape, dtype=x.dtype) for x in consts],
        [SM, HB, HB, HB, HB, VM, VM, VM] + [HB] * len(consts),
        [VM, HB] + [VM] * len(consts),
        scratch_shapes=[
            pltpu.SMEM((8,), F32),
            pltpu.VMEM((8, 64, FINE), F32),
            pltpu.VMEM((64, FINE), F32),
            pltpu.VMEM((64, FINE), F32),
            pltpu.VMEM((3, 8, 64, FINE), F32),
            pltpu.SemaphoreType.DMA((4,)),
            pltpu.SemaphoreType.DMA((len(consts),)),
            pltpu.SemaphoreType.DMA((8,)),
        ],
        limit=24,
        name="still",
    )(me, rate, salinity, zlow, zhigh, recv1, from_south, from_north, *consts)


def fine_kernel(
    grp_ref,
    base,
    parts_hbm,
    recv,
    ym,
    yt,
    edge,
    ref,
    rm,
    cm,
    out,
    spread,
    y_high,
    y_low,
    side_high,
    side_low,
    vel,
    total,
    parts,
    in_sems,
):
    rows = [slice(8 * yb, 8 * yb + 8) for yb in range(8)]
    loads = fetch([(parts_hbm.at[:, :, ys, :], parts.at[:, :, ys, :]) for ys in rows], in_sems)
    grp = grp_ref[0]
    row_id = iota((8, 128), 0)
    lane_id = iota((8, 128), 1)

    def lines(f, q):
        main = [recv[pl.ds(f * 128 + i, 16, stride=8), :] for i in (q, 4 + q, 3)]
        south = recv[pl.ds(pl.multiple_of((f * 16 + 2 * grp + q) * 8, 8), 8), :]
        north = recv[pl.ds(pl.multiple_of((f * 16 + 8 + 2 * grp + q) * 8, 8), 8), :]
        parts = []
        for x, row in zip(main, (2, 6, 3)):
            s, n = roll(south, -row, 0), roll(north, 1 - row, 0)
            if row == 3:
                x, s, n = roll(x, -2 * q, 1), roll(s, -4, 1), roll(n, -4, 1)
            tile = jnp.where(row_id == 0, s, jnp.where(row_id == 1, n, 0.0))
            parts.append(jnp.concatenate([x, tile, jnp.zeros((8, 128), F32)], 0))
        return jnp.concatenate(parts, 1)

    def along_y(table, f, q):
        high, low = halves(lines(f, q))
        return mm(table[...], jnp.concatenate([high, low], 0))

    for f in range(4):
        for q in range(2):
            at = slice(64 * (2 * f + q), 64 * (2 * f + q) + 64) if f < 3 else slice(384 + 16 * q, 400 + 16 * q)
            high, low = halves(along_y(ym if f < 3 else yt, f, q))
            y_high[at, :], side_high[at, :] = high[:, :256], high[:, 256:]
            y_low[at, :], side_low[at, :] = low[:, :256], low[:, 256:]
    vel[...] = mm(y_high[...], ref[...]) + mm(y_low[...], ref[...])
    side = mm(side_high[...], edge[...]) + mm(side_low[...], edge[...])
    vel[:, :128] += side[:, :128]
    vel[:, FINE - 128 :] += side[:, 128:]

    for yb in range(8):
        ys = rows[yb]
        loads[yb].wait()
        for q in range(2):
            vx, vy, vz = (vel[64 * (2 * f + q) + 8 * yb : 64 * (2 * f + q) + 8 * yb + 8, :] for f in range(3))
            acc = None
            for l in range(4 * q, 4 * q + 4):
                new = base[l, ys, :] - (vx * parts[0, l, ys, :] + vy * parts[1, l, ys, :] + vz * parts[2, l, ys, :])
                out[l, ys, :] = new
                acc = new if acc is None else acc + new
            total[64 * q + 8 * yb : 64 * q + 8 * yb + 8, :] = acc
    high, low = halves(total[...])
    high, low = halves(vel[384:416, :] - mm(rm[...], jnp.concatenate([high, low], 0)))
    means = [mm(high[:, at], cm[...]) + mm(low[:, at], cm[...]) for at in (slice(0, 512), slice(512, FINE))]
    mean = jnp.concatenate(means, 1)
    for a in range(G):
        spread[a] = mean


def fine(grp, base, parts, recv2, consts):
    return call(
        fine_kernel,
        (vds(8, 64, FINE), vds(G, 32, 256)),
        [SM, VM, HB, VM] + [VM] * len(consts),
        [VM, VM],
        input_output_aliases={1: 0},
        scratch_shapes=[
            pltpu.VMEM((416, 256), BF16),
            pltpu.VMEM((416, 256), BF16),
            pltpu.VMEM((416, 128), BF16),
            pltpu.VMEM((416, 128), BF16),
            pltpu.VMEM((416, FINE), F32),
            pltpu.VMEM((128, FINE), F32),
            pltpu.VMEM((3, 8, 64, FINE), F32),
            pltpu.SemaphoreType.DMA((8,)),
        ],
        limit=20,
        name="fine",
    )(grp, base, parts, recv2.reshape(512, 128), *consts)


def stage_kernel(me, inner_hbm, outer_hbm, *rest):
    count = (len(rest) - 8) // 2
    hbm, dst, rest = rest[:count], rest[count : 2 * count], rest[2 * count :]
    high_hbm, low_hbm, high, low, inner, outer, sems, out_sems = rest
    copies = fetch(((inner_hbm, inner), (outer_hbm, outer)) + tuple(zip(hbm, dst)), sems)
    turns = (iota((16, 128), 0) * me[0]) % G
    angle = turns.astype(F32) * (2.0 * math.pi / G)
    cos = jnp.concatenate([jnp.cos(angle)] * 2, 1)
    sin = -jnp.concatenate([jnp.sin(angle)] * 2, 1)
    copies[0].wait()
    copies[1].wait()
    real, imag = cmul(inner[:, :256], inner[:, 256:], cos, sin)
    for t in range(G):
        rows = slice(16 * t, 16 * t + 16)
        value = cmul(real, imag, outer[t : t + 1, :256], outer[t : t + 1, 256:])
        for at in range(2):
            high[rows, 256 * at : 256 * at + 256], low[rows, 256 * at : 256 * at + 256] = halves(value[at])
    for copy in copies[2:] + fetch(((high, high_hbm), (low, low_hbm)), out_sems):
        copy.wait()


def stage(me):
    t = tables()
    consts = [jnp.asarray(x) for x in (*t["tw"], *t["inv"])]
    out = call(
        stage_kernel,
        [vds(*x.shape, dtype=x.dtype) for x in consts] + [hds(256, 512, dtype=BF16)] * 2,
        [SM, HB, HB] + [HB] * len(consts),
        [VM] * len(consts) + [HB] * 2,
        scratch_shapes=[
            pltpu.VMEM((256, 512), BF16),
            pltpu.VMEM((256, 512), BF16),
            pltpu.VMEM((G, 512), F32),
            pltpu.VMEM((G, 512), F32),
            pltpu.SemaphoreType.DMA((len(consts) + 2,)),
            pltpu.SemaphoreType.DMA((2,)),
        ],
        name="stage",
    )(me, *map(jnp.asarray, t["fwd"]), *consts)
    return out[0:4], out[4:6]


def forward_kernel(recv, table_high, table_low, out, left_high, left_low, mid):
    turns = (iota((G, 128), 0) * iota((G, 128), 1)) % G
    angle = turns.astype(F32) * (2.0 * math.pi / G)
    comb_cos = jnp.concatenate([jnp.cos(angle)] * 2, 1)
    comb_sin = jnp.concatenate([jnp.sin(angle)] * 2, 1)
    for a in range(G):
        high, low = halves(recv[a])
        left_high[32 * a : 32 * a + 32, :] = high
        left_low[32 * a : 32 * a + 32, :] = low
    mid[...] = (
        mm(left_high[...], table_high[...]) + mm(left_low[...], table_high[...]) + mm(left_high[...], table_low[...])
    )
    real = imag = jnp.zeros((32, 256), F32)
    for a in range(G):
        c, s = comb_cos[a : a + 1, :], comb_sin[a : a + 1, :]
        x, y = mid[32 * a : 32 * a + 32, :256], mid[32 * a : 32 * a + 32, 256:]
        real = real + (x * c + y * s)
        imag = imag + (y * c - x * s)
    for g in range(4):
        out[g, 0:32, :] = real
        out[g, 32:64, :] = imag


def forward(recv, high, low):
    return call(
        forward_kernel,
        sds(4, 64, 256),
        [VM, VM, VM],
        VM,
        scratch_shapes=[
            pltpu.VMEM((512, 256), BF16),
            pltpu.VMEM((512, 256), BF16),
            pltpu.VMEM((512, 512), F32),
        ],
        name="forward",
    )(recv, high, low)


def finish_kernel(me, viscosity, gain, recv, modes, out):
    index = me[0] * W + iota((8, W), 1)
    number = jnp.where(index < NV // 2, index, index - NV).astype(F32)
    wave = (2.0 * math.pi / NV) * number
    damping = jnp.exp(-viscosity[0] * wave * wave)[0:1, :]
    for c in range(2):
        for g in range(4):
            at = slice(128 * c + 32 * g, 128 * c + 32 * g + 32)
            out[at, :] = damping * modes[at, :] + gain[0] * recv[g, 32 * c : 32 * c + 32, :]


def finish(me, viscosity, gain, recv, modes):
    return call(finish_kernel, sds(256, W), [SM, SM, SM, VM, VM], VM, name="finish")(
        me, viscosity, gain, recv, modes
    )


def shifted(array, axis, step):
    count = lax.axis_size(axis)
    return lax.ppermute(array, axis, [(i, (i + step) % count) for i in range(count)])


def per_device(coarse_modes, salinity, viscosity, forcing_gain, diffusivity):
    me = lax.axis_index(GX).astype(jnp.int32).reshape(1)
    grp = lax.axis_index("grp").astype(jnp.int32).reshape(1)
    modes = coarse_modes.reshape(256, 256)
    up, down, low_face, high_face = outer_lines(modes, salinity)
    from_south = shifted(up, "gy", 1)
    from_north = shifted(down, "gy", -1)
    zlow = shifted(high_face, "grp", 1)
    zhigh = shifted(low_face, "grp", -1)
    chunk, inv, weights = pack(me, modes, salinity), *stage(me)
    chunk, from_south, from_north, zlow, zhigh, inv, weights = lax.optimization_barrier(
        (chunk, from_south, from_north, zlow, zhigh, inv, weights)
    )
    chunk = tails(chunk, from_south, from_north)
    recv1 = lax.all_to_all(chunk, GX, 0, 0, tiled=True)
    send2 = inverse(recv1, *inv)
    recv2 = lax.all_to_all(send2, GRP_GX, 0, 0, tiled=True)
    base, parts, *consts = still(me, diffusivity, salinity, zlow, zhigh, recv1, from_south, from_north)
    salinity_next, spread = fine(grp, base, parts, recv2, consts)
    recv3 = lax.all_to_all(spread, GX, 0, 0, tiled=True)
    recv4 = lax.all_to_all(forward(recv3, *weights), "grp", 0, 0, tiled=True)
    coarse_next = finish(me, viscosity, forcing_gain, recv4, modes)
    return (salinity_next, coarse_next.reshape(coarse_modes.shape))


def solution(mesh):
    finer = Mesh(
        mesh.devices.reshape(mesh.shape["grp"], 2, 8, mesh.shape["gy"]),
        ("grp", "gx_0", "gx_1", "gy"),
    )
    in_specs = (P("grp", None, None, "gy", GX), P("grp", "gy", GX), P("grp"), P("grp"), P("grp"))
    out_specs = (P("grp", "gy", GX), P("grp", None, None, "gy", GX))
    return jax.shard_map(
        per_device, mesh=finer, in_specs=in_specs, out_specs=out_specs, check_vma=False
    )
```

```python
import functools
import math

import jax
import jax.numpy as jnp
import numpy as np
from jax import lax
from jax.experimental import pallas as pl
from jax.experimental.pallas import tpu as pltpu
from jax.sharding import Mesh
from jax.sharding import PartitionSpec as P

GX = ("gx_0", "gx_1")
GRP_GX = ("grp", "gx_0", "gx_1")
F32 = jnp.float32
BF16 = jnp.bfloat16
G = 16
NV = 4096
W = 256
FINE = 1024


def split_table(table):
    table = np.asarray(table, np.float64)
    high = table.astype(np.float32).astype(jnp.bfloat16)
    low = (table - high.astype(np.float64)).astype(np.float32).astype(jnp.bfloat16)
    return high, low


@functools.cache
def tables():
    out = {}
    k = np.arange(W)
    angle = 2 * np.pi * (np.outer(k, k) % W) / W
    norm = NV ** -0.5
    out["inv"] = split_table(np.concatenate([np.cos(angle), -np.sin(angle)], 0) * norm)
    r = np.arange(G)
    angle = 2 * np.pi * np.outer(r, k) / NV
    twc = np.zeros((G, 8, 128), np.float32)
    tws = np.zeros((G, 8, 128), np.float32)
    twc[:, :2] = np.cos(angle).reshape(G, 2, 128)
    tws[:, :2] = np.sin(angle).reshape(G, 2, 128)
    out["tw"] = (twc, tws)
    lanes = 16 * (k % 16) + k // 16
    order = np.argsort(lanes)
    assert np.array_equal(order, 16 * (k % 16) + k // 16)
    full = np.zeros((W + 2, FINE))
    for n in range(FINE):
        c, s = divmod(n, 4)
        o = (s + 0.5) / 4 - 0.5
        full[c + 1, n] += 1 - abs(o)
        full[c + 1 + (1 if o > 0 else -1), n] += abs(o)
    out["ref"] = full[1:-1][order].astype(jnp.bfloat16)
    edge = np.zeros((128, 256))
    edge[0, :128] = full[0, :128]
    edge[1, 128:] = full[-1, -128:]
    out["edge"] = edge.astype(jnp.bfloat16)
    ym = np.zeros((64, 32))
    yt = np.zeros((16, 32))
    place = lambda c: 16 if c < 0 else 17 if c > 15 else c
    for n in range(64):
        c, s = divmod(n, 4)
        o = (s + 0.5) / 4 - 0.5
        ym[n, c] += 1 - abs(o)
        ym[n, place(c + (1 if o > 0 else -1))] += abs(o)
    for c in range(16):
        yt[c, c] += 0.75
        yt[c, place(c - 1)] += 0.125
        yt[c, place(c + 1)] += 0.125
    out["ym"] = np.concatenate([ym, ym], 1).astype(jnp.bfloat16)
    out["yt"] = np.concatenate([yt, yt], 1).astype(jnp.bfloat16)
    cm = np.zeros((512, 128))
    cm[np.arange(512), np.arange(512) // 4] = 1.0 / 4
    out["cm"] = cm.astype(jnp.bfloat16)
    rm = np.zeros((32, 128))
    rm[np.arange(128) // 4, np.arange(128)] = 1.0 / 16
    out["rm"] = np.concatenate([rm, rm], 1).astype(jnp.bfloat16)
    g = np.arange(G)
    fine_angle = 2 * np.pi * np.outer(g, k) / NV
    coarse_angle = 2 * np.pi * (np.outer(g, k) % W) / W
    out["fwd"] = tuple(
        x.astype(np.float32)
        for x in (
            np.concatenate([np.cos(fine_angle), -np.sin(fine_angle)], 1) * norm,
            np.concatenate([np.cos(coarse_angle), -np.sin(coarse_angle)], 1),
        )
    )
    return out


def halves(x):
    high = x.astype(BF16)
    low = (x - high.astype(F32)).astype(BF16)
    return high, low


def mm(a, b):
    return jnp.dot(a, b, preferred_element_type=F32)


VM = pl.BlockSpec(memory_space=pltpu.VMEM)
SM = pl.BlockSpec(memory_space=pltpu.SMEM)
HB = pl.BlockSpec(memory_space=pltpu.HBM)


def call(kernel, out_shape, in_specs, out_specs, limit=12, **kw):
    inner = pl.pallas_call(
        kernel,
        out_shape=out_shape,
        in_specs=in_specs,
        out_specs=out_specs,
        compiler_params=pltpu.CompilerParams(vmem_limit_bytes=limit << 20),
        **kw,
    )

    def placed(*args):
        return inner(
            *[x if spec is not HB else pltpu.with_memory_space_constraint(x, pltpu.HBM) for x, spec in zip(args, in_specs)]
        )

    return placed


def fetch(pairs, sems, first=0):
    copies = [pltpu.make_async_copy(src, dst, sems.at[first + i]) for i, (src, dst) in enumerate(pairs)]
    for copy in copies:
        copy.start()
    return copies


def sds(*shape, dtype=F32):
    return jax.ShapeDtypeStruct(shape, dtype)


def vds(*shape, dtype=F32):
    return pltpu.VMEM(shape, dtype)


def hds(*shape, dtype=F32):
    return pltpu.HBM(shape, dtype)


def iota(shape, dim):
    return lax.broadcasted_iota(jnp.int32, shape, dim)


def roll(x, shift, axis):
    return pltpu.roll(x, shift % x.shape[axis], axis)


def lines_kernel(modes, sal, up, down, low_face, high_face, ends, south, north, sems):
    copies = fetch(
        (
            (modes.at[:, 0:8, :], ends.at[0]),
            (modes.at[:, 8:16, :], ends.at[1]),
            (sal.at[:, 0:8, :], south),
            (sal.at[:, 56:64, :], north),
            (sal.at[0], low_face),
            (sal.at[7], high_face),
        ),
        sems,
    )
    for copy in copies[:4]:
        copy.wait()
    for dst, rows, end, row in ((up, north, 1, 7), (down, south, 0, 0)):
        dst[0:16, :] = ends[end, :, row, :]
        face = rows[:, row, :]
        for j in range(4):
            dst[16 + 8 * j : 24 + 8 * j, :] = face[:, 256 * j : 256 * j + 256]
    for copy in copies[4:]:
        copy.wait()


def outer_lines(modes, salinity):
    return call(
        lines_kernel,
        (vds(48, 256), vds(48, 256), vds(64, FINE), vds(64, FINE)),
        [HB, HB],
        [VM] * 4,
        scratch_shapes=[
            pltpu.VMEM((2, 16, 8, 256), F32),
            pltpu.VMEM((8, 8, FINE), F32),
            pltpu.VMEM((8, 8, FINE), F32),
            pltpu.SemaphoreType.DMA((6,)),
        ],
        name="outer_lines",
    )(modes.reshape(16, 16, 256), salinity)


def pack_kernel(me, modes, sal, chunk, modes_a, modes_b, west, east, sems):
    copies = fetch(
        (
            (modes.at[:, 0:128], modes_a),
            (modes.at[:, 128:256], modes_b),
            (sal.at[:, :, 0:128], west),
            (sal.at[:, :, FINE - 128 :], east),
        ),
        sems,
    )
    for copy in copies[:2]:
        copy.wait()
    zero = jnp.zeros((8, 128), F32)
    for r in range(G):
        chunk[r, 0:16, :] = modes_a[pl.ds(r, 16, stride=16), :]
        chunk[r, 16:32, :] = modes_b[pl.ds(r, 16, stride=16), :]
        chunk[r, 32:40, :] = zero
    row_id = iota((8, 128), 0)

    def column(block, lane):
        tile = zero
        for i in range(4):
            both = jnp.concatenate([block[2 * i], block[2 * i + 1]], 0).T
            line = jnp.broadcast_to(both[lane : lane + 1, :], (8, 128))
            tile = jnp.where(row_id == 4 + i, line, tile)
        return tile

    for copy in copies[2:]:
        copy.wait()
    chunk[(me[0] + 1) % G, 32:40, :] = column(east, 127)
    chunk[(me[0] + G - 1) % G, 32:40, :] = column(west, 0)


def pack(me, modes, salinity):
    return call(
        pack_kernel,
        vds(G, 40, 128),
        [SM, HB, HB],
        VM,
        scratch_shapes=[
            pltpu.VMEM((256, 128), F32),
            pltpu.VMEM((256, 128), F32),
            pltpu.VMEM((8, 64, 128), F32),
            pltpu.VMEM((8, 64, 128), F32),
            pltpu.SemaphoreType.DMA((4,)),
        ],
        name="pack",
    )(me, modes, salinity)


def tails_kernel(chunk, from_south, from_north, out):
    row_id = iota((8, 128), 0)
    for r in range(G):
        rows = from_south if r < 8 else from_north
        p = r % 8
        tile = chunk[r, 32:40, :]
        parts = (rows[p : p + 1, :128], rows[p : p + 1, 128:], rows[8 + p : 9 + p, :128], rows[8 + p : 9 + p, 128:])
        for i, part in enumerate(parts):
            tile = jnp.where(row_id == i, jnp.broadcast_to(part, (8, 128)), tile)
        out[r, 32:40, :] = tile


def tails(chunk, from_south, from_north):
    return call(
        tails_kernel,
        vds(G, 40, 128),
        [VM, VM, VM],
        VM,
        input_output_aliases={0: 0},
        name="tails",
    )(chunk, from_south, from_north)


def cmul(a, b, c, s):
    return a * c - b * s, a * s + b * c


def four(z):
    (ar, ai), (br, bi), (cr, ci), (dr, di) = z
    t0r, t0i, t1r, t1i = ar + cr, ai + ci, ar - cr, ai - ci
    t2r, t2i, t3r, t3i = br + dr, bi + di, br - dr, bi - di
    return (
        (t0r + t2r, t0i + t2i),
        (t1r - t3i, t1i + t3r),
        (t0r - t2r, t0i - t2i),
        (t1r + t3i, t1i - t3r),
    )


def sixteen(z):
    inner = [four([z[4 * g1 + g0] for g1 in range(4)]) for g0 in range(4)]
    out = [None] * 16
    for r0 in range(4):
        column = []
        for g0 in range(4):
            angle = 2 * math.pi * g0 * r0 / 16
            a, b = inner[g0][r0]
            column.append((a, b) if g0 * r0 == 0 else cmul(a, b, math.cos(angle), math.sin(angle)))
        for r1, value in enumerate(four(column)):
            out[4 * r1 + r0] = value
    return out


def inverse_kernel(recv, twc, tws, inv_high, inv_low, send_hbm, left_high, left_low, mid, send, sems):
    row_id = iota((8, 128), 0)
    lane_id = iota((8, 128), 1)

    def put(r, top, part, value):
        high, low = halves(value)
        left_high[16 * r + 8 * top : 16 * r + 8 * top + 8, 128 * part : 128 * part + 128] = high
        left_low[16 * r + 8 * top : 16 * r + 8 * top + 8, 128 * part : 128 * part + 128] = low

    for h in range(2):
        z = [(recv[g, 16 * h : 16 * h + 8, :], recv[g, 16 * h + 8 : 16 * h + 16, :]) for g in range(G)]
        for r, (a, b) in enumerate(sixteen(z)):
            a, b = cmul(a, b, twc[r, h : h + 1, :], tws[r, h : h + 1, :])
            put(r, 0, h, a)
            put(r, 0, 2 + h, b)
    z = []
    for g in range(G):
        tile = jnp.where(row_id < 4, recv[g, 32:40, :], 0.0)
        z.append((tile, roll(tile, -2, 0)))
    for r, (a, b) in enumerate(sixteen(z)):
        a, b = cmul(a, b, twc[r], tws[r])
        for part, value in ((0, a), (2, b)):
            put(r, 1, part, jnp.where(row_id == 0, value, 0.0))
            put(r, 1, part + 1, jnp.where(row_id == 0, roll(value, -1, 0), 0.0))

    mid[...] = (
        mm(left_high[...], inv_high[...]) + mm(left_low[...], inv_high[...]) + mm(left_high[...], inv_low[...])
    )

    first, second, single = [], [], []
    for r in range(G):
        first.append(mid[16 * r : 16 * r + 8, 0:128])
        second.append(mid[16 * r : 16 * r + 8, 128:256])
        low = mid[16 * r + 8 : 16 * r + 16, 0:128]
        high = mid[16 * r + 8 : 16 * r + 16, 128:256]
        single.append(jnp.where(row_id == 0, low, roll(high, 1, 0)))
    for i in range(8):
        a, b = first[i], second[i]
        c, d = first[i + 8], second[i + 8]
        first[i], second[i], first[i + 8], second[i + 8] = a, c, b, d
        a, c = single[i], single[i + 8]
        single[i] = jnp.where(row_id == 0, a, roll(c, 1, 0))
        single[i + 8] = jnp.where(row_id == 0, roll(a, -1, 0), c)
    for bit in (4, 2, 1):
        upper = (lane_id // (16 * bit)) % 2 == 1
        for tiles in (first, second, single):
            for i in range(G):
                if i & bit:
                    continue
                a, b = tiles[i], tiles[i | bit]
                tiles[i] = jnp.where(upper, roll(b, 16 * bit, 1), a)
                tiles[i | bit] = jnp.where(upper, b, roll(a, -16 * bit, 1))

    left = [roll(second[d], 1, 1) for d in range(G)]
    right = [roll(first[d], 1, 1) for d in range(G)]
    side = [roll(single[d], 5, 1) for d in range(G)]
    stores = []
    for d in range(G):
        before, after = (d - 1) % G, (d + 1) % G
        own = jnp.where(lane_id == 0, left[before], jnp.where(lane_id == 1, right[after], 0.0))
        rim = own + roll(roll(own, -1, 0), 2, 1)
        base = jnp.where(row_id == 2, roll(single[d], 2, 0), 0.0)
        base = jnp.where(row_id == 6, roll(single[d], 5, 0), base)
        base = jnp.where((row_id == 3) & (lane_id == 4), roll(side[before], 2, 0), base)
        base = jnp.where((row_id == 3) & (lane_id == 5), roll(side[after], 3, 0), base)
        for g in range(4):
            tile = jnp.where(row_id < 2, roll(first[d], -2 * g, 0), base)
            tile = jnp.where((row_id == 4) | (row_id == 5), roll(second[d], 4 - 2 * g, 0), tile)
            tile = jnp.where((row_id == 3) & (lane_id < 4), roll(rim, 3 - 2 * g, 0), tile)
            send[g, d] = tile
        if d % 4 == 3:
            ds = slice(d - 3, d + 1)
            stores += fetch(((send.at[:, ds], send_hbm.at[:, ds]),), sems, d // 4)
    for store in stores:
        store.wait()


def inverse(recv, twc, tws, high, low):
    return call(
        inverse_kernel,
        hds(4, G, 8, 128),
        [VM] * 5,
        HB,
        scratch_shapes=[
            pltpu.VMEM((256, 512), BF16),
            pltpu.VMEM((256, 512), BF16),
            pltpu.VMEM((256, 256), F32),
            pltpu.VMEM((4, G, 8, 128), F32),
            pltpu.SemaphoreType.DMA((4,)),
        ],
        name="inverse",
    )(recv, twc, tws, high, low).reshape(64, 8, 128)


EARLY = ("ym", "yt", "edge", "ref", "rm", "cm")


def still_kernel(me, rate_hbm, sal_hbm, zlow_hbm, zhigh_hbm, edge_cols, from_south, from_north, *rest):
    (inner_hbm, outer_hbm), rest = rest[:2], rest[2:]
    count = len(EARLY)
    hbm, (base, parts_hbm, high_hbm, low_hbm), rest = rest[:count], rest[count : count + 4], rest[count + 4 :]
    kept, (high, low, inner, outer, table_sems), rest = rest[:count], rest[count : count + 5], rest[count + 5 :]
    rate, salinity, zlow, zhigh, parts, sems, const_sems, out_sems = rest
    copies = fetch(((rate_hbm, rate), (sal_hbm, salinity), (zlow_hbm, zlow), (zhigh_hbm, zhigh)), sems)
    stores = fetch(tuple(zip(hbm, kept)), const_sems)
    bases = fetch(((inner_hbm, inner), (outer_hbm, outer)), table_sems)
    turns = (iota((16, 128), 0) * me[0]) % G
    angle = turns.astype(F32) * (2.0 * math.pi / G)
    cos = jnp.concatenate([jnp.cos(angle)] * 2, 1)
    sin = -jnp.concatenate([jnp.sin(angle)] * 2, 1)
    for copy in bases:
        copy.wait()
    real, imag = cmul(inner[:, :256], inner[:, 256:], cos, sin)
    for t in range(G):
        rows = slice(16 * t, 16 * t + 16)
        value = cmul(real, imag, outer[t : t + 1, :256], outer[t : t + 1, 256:])
        for at in range(2):
            high[rows, 256 * at : 256 * at + 256], low[rows, 256 * at : 256 * at + 256] = halves(value[at])
    stores += fetch(((high, high_hbm), (low, low_hbm)), table_sems, 2)
    west_t = edge_cols[(me[0] + G - 1) % G, 32:40, :].T
    east_t = edge_cols[(me[0] + 1) % G, 32:40, :].T
    last_row = iota((8, FINE), 0) == 7
    first_row = iota((8, FINE), 0) == 0
    last_lane = iota((8, 128), 1) == 127
    first_lane = iota((8, 128), 1) == 0

    def outer(rows, l):
        line = jnp.concatenate([rows[16 + 8 * j + l : 17 + 8 * j + l, :] for j in range(4)], 1)
        return jnp.broadcast_to(line, (8, FINE))

    for copy in copies:
        copy.wait()
    for yb in range(8):
        ys = slice(8 * yb, 8 * yb + 8)
        for l in range(8):
            c = salinity[l, ys, :]
            upper = salinity[l + 1, ys, :] if l < 7 else zhigh[ys, :]
            lower = salinity[l - 1, ys, :] if l > 0 else zlow[ys, :]
            if yb < 7:
                north = salinity[l, 8 * yb + 1 : 8 * yb + 9, :]
            else:
                north = jnp.where(last_row, outer(from_north, l), roll(c, -1, 0))
            if yb > 0:
                south = salinity[l, 8 * yb - 1 : 8 * yb + 7, :]
            else:
                south = jnp.where(first_row, outer(from_south, l), roll(c, 1, 0))
            at = (l % 2) * 64 + 8 * yb
            ecol = jnp.broadcast_to(east_t[at : at + 8, 4 + l // 2 : 5 + l // 2], (8, 128))
            wcol = jnp.broadcast_to(west_t[at : at + 8, 4 + l // 2 : 5 + l // 2], (8, 128))
            e = roll(c, -1, 1)
            w = roll(c, 1, 1)
            e = jnp.concatenate([e[:, :-128], jnp.where(last_lane, ecol, e[:, -128:])], 1)
            w = jnp.concatenate([jnp.where(first_lane, wcol, w[:, :128]), w[:, 128:]], 1)
            k = rate[l] * 0.1
            base[l, ys, :] = c + k * (((e + w) + (north + south)) + (upper + lower) - 6.0 * c)
            parts[0, l, ys, :] = (e - w) * 0.05
            parts[1, l, ys, :] = (north - south) * 0.05
            parts[2, l, ys, :] = (upper - lower) * 0.05
        stores.append(pltpu.make_async_copy(parts.at[:, :, ys, :], parts_hbm.at[:, :, ys, :], out_sems.at[yb]))
        stores[-1].start()
    for store in stores:
        store.wait()


def still(me, rate, salinity, zlow, zhigh, recv1, from_south, from_north):
    consts = [jnp.asarray(tables()[name]) for name in EARLY]
    return call(
        still_kernel,
        [vds(8, 64, FINE), hds(3, 8, 64, FINE)]
        + [hds(256, 512, dtype=BF16)] * 2
        + [vds(*x.shape, dtype=x.dtype) for x in consts],
        [SM, HB, HB, HB, HB, VM, VM, VM] + [HB] * (2 + len(consts)),
        [VM, HB, HB, HB] + [VM] * len(consts),
        scratch_shapes=[
            pltpu.VMEM((256, 512), BF16),
            pltpu.VMEM((256, 512), BF16),
            pltpu.VMEM((G, 512), F32),
            pltpu.VMEM((G, 512), F32),
            pltpu.SemaphoreType.DMA((4,)),
            pltpu.SMEM((8,), F32),
            pltpu.VMEM((8, 64, FINE), F32),
            pltpu.VMEM((64, FINE), F32),
            pltpu.VMEM((64, FINE), F32),
            pltpu.VMEM((3, 8, 64, FINE), F32),
            pltpu.SemaphoreType.DMA((4,)),
            pltpu.SemaphoreType.DMA((len(consts),)),
            pltpu.SemaphoreType.DMA((8,)),
        ],
        limit=24,
        name="still",
    )(me, rate, salinity, zlow, zhigh, recv1, from_south, from_north, *map(jnp.asarray, tables()["fwd"]), *consts)


def fine_kernel(
    grp_ref,
    base,
    parts_hbm,
    recv,
    ym,
    yt,
    edge,
    ref,
    rm,
    cm,
    out,
    spread,
    y_high,
    y_low,
    side_high,
    side_low,
    vel,
    total,
    parts,
    in_sems,
):
    rows = [slice(8 * yb, 8 * yb + 8) for yb in range(8)]
    loads = fetch([(parts_hbm.at[:, :, ys, :], parts.at[:, :, ys, :]) for ys in rows], in_sems)
    grp = grp_ref[0]
    row_id = iota((8, 128), 0)
    lane_id = iota((8, 128), 1)

    def lines(f, q):
        main = [recv[pl.ds(f * 128 + i, 16, stride=8), :] for i in (q, 4 + q, 3)]
        south = recv[pl.ds(pl.multiple_of((f * 16 + 2 * grp + q) * 8, 8), 8), :]
        north = recv[pl.ds(pl.multiple_of((f * 16 + 8 + 2 * grp + q) * 8, 8), 8), :]
        parts = []
        for x, row in zip(main, (2, 6, 3)):
            s, n = roll(south, -row, 0), roll(north, 1 - row, 0)
            if row == 3:
                x, s, n = roll(x, -2 * q, 1), roll(s, -4, 1), roll(n, -4, 1)
            tile = jnp.where(row_id == 0, s, jnp.where(row_id == 1, n, 0.0))
            parts.append(jnp.concatenate([x, tile, jnp.zeros((8, 128), F32)], 0))
        return jnp.concatenate(parts, 1)

    def along_y(table, f, q):
        high, low = halves(lines(f, q))
        return mm(table[...], jnp.concatenate([high, low], 0))

    for f in range(4):
        for q in range(2):
            at = slice(64 * (2 * f + q), 64 * (2 * f + q) + 64) if f < 3 else slice(384 + 16 * q, 400 + 16 * q)
            high, low = halves(along_y(ym if f < 3 else yt, f, q))
            y_high[at, :], side_high[at, :] = high[:, :256], high[:, 256:]
            y_low[at, :], side_low[at, :] = low[:, :256], low[:, 256:]
    vel[...] = mm(y_high[...], ref[...]) + mm(y_low[...], ref[...])
    side = mm(side_high[...], edge[...]) + mm(side_low[...], edge[...])
    vel[:, :128] += side[:, :128]
    vel[:, FINE - 128 :] += side[:, 128:]

    for yb in range(8):
        ys = rows[yb]
        loads[yb].wait()
        for q in range(2):
            vx, vy, vz = (vel[64 * (2 * f + q) + 8 * yb : 64 * (2 * f + q) + 8 * yb + 8, :] for f in range(3))
            acc = None
            for l in range(4 * q, 4 * q + 4):
                new = base[l, ys, :] - (vx * parts[0, l, ys, :] + vy * parts[1, l, ys, :] + vz * parts[2, l, ys, :])
                out[l, ys, :] = new
                acc = new if acc is None else acc + new
            total[64 * q + 8 * yb : 64 * q + 8 * yb + 8, :] = acc
    high, low = halves(total[...])
    high, low = halves(vel[384:416, :] - mm(rm[...], jnp.concatenate([high, low], 0)))
    means = [mm(high[:, at], cm[...]) + mm(low[:, at], cm[...]) for at in (slice(0, 512), slice(512, FINE))]
    mean = jnp.concatenate(means, 1)
    for a in range(G):
        spread[a] = mean


def fine(grp, base, parts, recv2, consts):
    return call(
        fine_kernel,
        (vds(8, 64, FINE), vds(G, 32, 256)),
        [SM, VM, HB, VM] + [VM] * len(consts),
        [VM, VM],
        input_output_aliases={1: 0},
        scratch_shapes=[
            pltpu.VMEM((416, 256), BF16),
            pltpu.VMEM((416, 256), BF16),
            pltpu.VMEM((416, 128), BF16),
            pltpu.VMEM((416, 128), BF16),
            pltpu.VMEM((416, FINE), F32),
            pltpu.VMEM((128, FINE), F32),
            pltpu.VMEM((3, 8, 64, FINE), F32),
            pltpu.SemaphoreType.DMA((8,)),
        ],
        limit=20,
        name="fine",
    )(grp, base, parts, recv2.reshape(512, 128), *consts)


def stage_kernel(*refs):
    sems = refs[-1]
    count = len(refs) // 2
    for copy in fetch(tuple(zip(refs[:count], refs[count:-1])), sems):
        copy.wait()


def stage():
    t = tables()
    consts = [jnp.asarray(x) for x in (*t["tw"], *t["inv"])]
    return call(
        stage_kernel,
        [vds(*x.shape, dtype=x.dtype) for x in consts],
        [HB] * len(consts),
        [VM] * len(consts),
        scratch_shapes=[pltpu.SemaphoreType.DMA((len(consts),))],
        name="stage",
    )(*consts)


def forward_kernel(recv, table_high, table_low, out, left_high, left_low, mid):
    turns = (iota((G, 128), 0) * iota((G, 128), 1)) % G
    angle = turns.astype(F32) * (2.0 * math.pi / G)
    comb_cos = jnp.concatenate([jnp.cos(angle)] * 2, 1)
    comb_sin = jnp.concatenate([jnp.sin(angle)] * 2, 1)
    for a in range(G):
        high, low = halves(recv[a])
        left_high[32 * a : 32 * a + 32, :] = high
        left_low[32 * a : 32 * a + 32, :] = low
    mid[...] = (
        mm(left_high[...], table_high[...]) + mm(left_low[...], table_high[...]) + mm(left_high[...], table_low[...])
    )
    real = imag = jnp.zeros((32, 256), F32)
    for a in range(G):
        c, s = comb_cos[a : a + 1, :], comb_sin[a : a + 1, :]
        x, y = mid[32 * a : 32 * a + 32, :256], mid[32 * a : 32 * a + 32, 256:]
        real = real + (x * c + y * s)
        imag = imag + (y * c - x * s)
    for g in range(4):
        out[g, 0:32, :] = real
        out[g, 32:64, :] = imag


def forward(recv, high, low):
    return call(
        forward_kernel,
        sds(4, 64, 256),
        [VM, VM, VM],
        VM,
        scratch_shapes=[
            pltpu.VMEM((512, 256), BF16),
            pltpu.VMEM((512, 256), BF16),
            pltpu.VMEM((512, 512), F32),
        ],
        name="forward",
    )(recv, high, low)


def finish_kernel(me, viscosity, gain, recv, modes, out_hbm, out, sems):
    index = me[0] * W + iota((8, W), 1)
    number = jnp.where(index < NV // 2, index, index - NV).astype(F32)
    wave = (2.0 * math.pi / NV) * number
    damping = jnp.exp(-viscosity[0] * wave * wave)[0:1, :]
    stores = []
    for c in range(2):
        for g in range(4):
            at = slice(128 * c + 32 * g, 128 * c + 32 * g + 32)
            out[at, :] = damping * modes[at, :] + gain[0] * recv[g, 32 * c : 32 * c + 32, :]
        half = slice(128 * c, 128 * c + 128)
        stores += fetch(((out.at[half], out_hbm.at[half]),), sems, c)
    for store in stores:
        store.wait()


def finish(me, viscosity, gain, recv, modes):
    return call(
        finish_kernel,
        hds(256, W),
        [SM, SM, SM, VM, VM],
        HB,
        scratch_shapes=[pltpu.VMEM((256, W), F32), pltpu.SemaphoreType.DMA((2,))],
        name="finish",
    )(me, viscosity, gain, recv, modes)


def shifted(array, axis, step):
    count = lax.axis_size(axis)
    return lax.ppermute(array, axis, [(i, (i + step) % count) for i in range(count)])


def per_device(coarse_modes, salinity, viscosity, forcing_gain, diffusivity):
    me = lax.axis_index(GX).astype(jnp.int32).reshape(1)
    grp = lax.axis_index("grp").astype(jnp.int32).reshape(1)
    modes = coarse_modes.reshape(256, 256)
    up, down, low_face, high_face = outer_lines(modes, salinity)
    from_south = shifted(up, "gy", 1)
    from_north = shifted(down, "gy", -1)
    zlow = shifted(high_face, "grp", 1)
    zhigh = shifted(low_face, "grp", -1)
    chunk, inv = pack(me, modes, salinity), stage()
    chunk, from_south, from_north, zlow, zhigh, inv = lax.optimization_barrier(
        (chunk, from_south, from_north, zlow, zhigh, inv)
    )
    chunk = tails(chunk, from_south, from_north)
    recv1 = lax.all_to_all(chunk, GX, 0, 0, tiled=True)
    send2 = inverse(recv1, *inv)
    recv2 = lax.all_to_all(send2, GRP_GX, 0, 0, tiled=True)
    base, parts, *rest = still(me, diffusivity, salinity, zlow, zhigh, recv1, from_south, from_north)
    weights, consts = rest[:2], rest[2:]
    salinity_next, spread = fine(grp, base, parts, recv2, consts)
    recv3 = lax.all_to_all(spread, GX, 0, 0, tiled=True)
    recv4 = lax.all_to_all(forward(recv3, *weights), "grp", 0, 0, tiled=True)
    coarse_next = finish(me, viscosity, forcing_gain, recv4, modes)
    return (salinity_next, coarse_next.reshape(coarse_modes.shape))


def solution(mesh):
    finer = Mesh(
        mesh.devices.reshape(mesh.shape["grp"], 2, 8, mesh.shape["gy"]),
        ("grp", "gx_0", "gx_1", "gy"),
    )
    in_specs = (P("grp", None, None, "gy", GX), P("grp", "gy", GX), P("grp"), P("grp"), P("grp"))
    out_specs = (P("grp", "gy", GX), P("grp", None, None, "gy", GX))
    return jax.shard_map(
        per_device, mesh=finer, in_specs=in_specs, out_specs=out_specs, check_vma=False
    )
```

```python
import functools
import math

import jax
import jax.numpy as jnp
import numpy as np
from jax import lax
from jax.experimental import pallas as pl
from jax.experimental.pallas import tpu as pltpu
from jax.sharding import Mesh
from jax.sharding import PartitionSpec as P

GX = ("gx_0", "gx_1")
GRP_GX = ("grp", "gx_0", "gx_1")
F32 = jnp.float32
BF16 = jnp.bfloat16
G = 16
NV = 4096
W = 256
FINE = 1024


def split_table(table):
    table = np.asarray(table, np.float64)
    high = table.astype(np.float32).astype(jnp.bfloat16)
    low = (table - high.astype(np.float64)).astype(np.float32).astype(jnp.bfloat16)
    return high, low


@functools.cache
def tables():
    out = {}
    k = np.arange(W)
    angle = 2 * np.pi * (np.outer(k, k) % W) / W
    norm = NV ** -0.5
    out["inv"] = split_table(np.concatenate([np.cos(angle), -np.sin(angle)], 0) * norm)
    r = np.arange(G)
    angle = 2 * np.pi * np.outer(r, k) / NV
    twc = np.zeros((G, 8, 128), np.float32)
    tws = np.zeros((G, 8, 128), np.float32)
    twc[:, :2] = np.cos(angle).reshape(G, 2, 128)
    tws[:, :2] = np.sin(angle).reshape(G, 2, 128)
    out["tw"] = (twc, tws)
    lanes = 16 * (k % 16) + k // 16
    order = np.argsort(lanes)
    assert np.array_equal(order, 16 * (k % 16) + k // 16)
    full = np.zeros((W + 2, FINE))
    for n in range(FINE):
        c, s = divmod(n, 4)
        o = (s + 0.5) / 4 - 0.5
        full[c + 1, n] += 1 - abs(o)
        full[c + 1 + (1 if o > 0 else -1), n] += abs(o)
    out["ref"] = full[1:-1][order].astype(jnp.bfloat16)
    edge = np.zeros((128, 256))
    edge[0, :128] = full[0, :128]
    edge[1, 128:] = full[-1, -128:]
    out["edge"] = edge.astype(jnp.bfloat16)
    ym = np.zeros((64, 32))
    yt = np.zeros((16, 32))
    place = lambda c: 16 if c < 0 else 17 if c > 15 else c
    for n in range(64):
        c, s = divmod(n, 4)
        o = (s + 0.5) / 4 - 0.5
        ym[n, c] += 1 - abs(o)
        ym[n, place(c + (1 if o > 0 else -1))] += abs(o)
    for c in range(16):
        yt[c, c] += 0.75
        yt[c, place(c - 1)] += 0.125
        yt[c, place(c + 1)] += 0.125
    out["ym"] = np.concatenate([ym, ym], 1).astype(jnp.bfloat16)
    out["yt"] = np.concatenate([yt, yt], 1).astype(jnp.bfloat16)
    cm = np.zeros((512, 128))
    cm[np.arange(512), np.arange(512) // 4] = 1.0 / 4
    out["cm"] = cm.astype(jnp.bfloat16)
    rm = np.zeros((32, 128))
    rm[np.arange(128) // 4, np.arange(128)] = 1.0 / 16
    out["rm"] = np.concatenate([rm, rm], 1).astype(jnp.bfloat16)
    g = np.arange(G)
    fine_angle = 2 * np.pi * np.outer(g, k) / NV
    coarse_angle = 2 * np.pi * (np.outer(g, k) % W) / W
    out["fwd"] = tuple(
        x.astype(np.float32)
        for x in (
            np.concatenate([np.cos(fine_angle), -np.sin(fine_angle)], 1) * norm,
            np.concatenate([np.cos(coarse_angle), -np.sin(coarse_angle)], 1),
        )
    )
    return out


def halves(x):
    high = x.astype(BF16)
    low = (x - high.astype(F32)).astype(BF16)
    return high, low


def mm(a, b):
    return jnp.dot(a, b, preferred_element_type=F32)


VM = pl.BlockSpec(memory_space=pltpu.VMEM)
SM = pl.BlockSpec(memory_space=pltpu.SMEM)
HB = pl.BlockSpec(memory_space=pltpu.HBM)


def call(kernel, out_shape, in_specs, out_specs, limit=12, **kw):
    inner = pl.pallas_call(
        kernel,
        out_shape=out_shape,
        in_specs=in_specs,
        out_specs=out_specs,
        compiler_params=pltpu.CompilerParams(vmem_limit_bytes=limit << 20),
        **kw,
    )

    def placed(*args):
        return inner(
            *[x if spec is not HB else pltpu.with_memory_space_constraint(x, pltpu.HBM) for x, spec in zip(args, in_specs)]
        )

    return placed


def fetch(pairs, sems, first=0):
    copies = [pltpu.make_async_copy(src, dst, sems.at[first + i]) for i, (src, dst) in enumerate(pairs)]
    for copy in copies:
        copy.start()
    return copies


def sds(*shape, dtype=F32):
    return jax.ShapeDtypeStruct(shape, dtype)


def vds(*shape, dtype=F32):
    return pltpu.VMEM(shape, dtype)


def hds(*shape, dtype=F32):
    return pltpu.HBM(shape, dtype)


def iota(shape, dim):
    return lax.broadcasted_iota(jnp.int32, shape, dim)


def roll(x, shift, axis):
    return pltpu.roll(x, shift % x.shape[axis], axis)


def lines_kernel(modes, sal, up, down, low_face, high_face, ends, south, north, sems):
    copies = fetch(
        (
            (modes.at[:, 0:8, :], ends.at[0]),
            (modes.at[:, 8:16, :], ends.at[1]),
            (sal.at[:, 0:8, :], south),
            (sal.at[:, 56:64, :], north),
            (sal.at[0], low_face),
            (sal.at[7], high_face),
        ),
        sems,
    )
    for copy in copies:
        copy.wait()
    for dst, rows, end, row in ((up, north, 1, 7), (down, south, 0, 0)):
        dst[0:16, :] = ends[end, :, row, :]
        face = rows[:, row, :]
        for j in range(4):
            dst[16 + 8 * j : 24 + 8 * j, :] = face[:, 256 * j : 256 * j + 256]


def outer_lines(modes, salinity):
    return call(
        lines_kernel,
        (vds(48, 256), vds(48, 256), vds(64, FINE), vds(64, FINE)),
        [HB, HB],
        [VM] * 4,
        scratch_shapes=[
            pltpu.VMEM((2, 16, 8, 256), F32),
            pltpu.VMEM((8, 8, FINE), F32),
            pltpu.VMEM((8, 8, FINE), F32),
            pltpu.SemaphoreType.DMA((6,)),
        ],
        name="outer_lines",
    )(modes.reshape(16, 16, 256), salinity)


def pack_kernel(me, modes, sal, chunk, modes_a, modes_b, west, east, sems):
    copies = fetch(
        (
            (modes.at[:, 0:128], modes_a),
            (modes.at[:, 128:256], modes_b),
            (sal.at[:, :, 0:128], west),
            (sal.at[:, :, FINE - 128 :], east),
        ),
        sems,
    )
    for copy in copies[:2]:
        copy.wait()
    zero = jnp.zeros((8, 128), F32)
    for r in range(G):
        chunk[r, 0:16, :] = modes_a[pl.ds(r, 16, stride=16), :]
        chunk[r, 16:32, :] = modes_b[pl.ds(r, 16, stride=16), :]
        chunk[r, 32:40, :] = zero
    row_id = iota((8, 128), 0)

    def column(block, lane):
        tile = zero
        for i in range(4):
            both = jnp.concatenate([block[2 * i], block[2 * i + 1]], 0).T
            line = jnp.broadcast_to(both[lane : lane + 1, :], (8, 128))
            tile = jnp.where(row_id == 4 + i, line, tile)
        return tile

    for copy in copies[2:]:
        copy.wait()
    chunk[(me[0] + 1) % G, 32:40, :] = column(east, 127)
    chunk[(me[0] + G - 1) % G, 32:40, :] = column(west, 0)


def pack(me, modes, salinity):
    return call(
        pack_kernel,
        vds(G, 40, 128),
        [SM, HB, HB],
        VM,
        scratch_shapes=[
            pltpu.VMEM((256, 128), F32),
            pltpu.VMEM((256, 128), F32),
            pltpu.VMEM((8, 64, 128), F32),
            pltpu.VMEM((8, 64, 128), F32),
            pltpu.SemaphoreType.DMA((4,)),
        ],
        name="pack",
    )(me, modes, salinity)


def tails_kernel(chunk, from_south, from_north, out):
    row_id = iota((8, 128), 0)
    for r in range(G):
        rows = from_south if r < 8 else from_north
        p = r % 8
        tile = chunk[r, 32:40, :]
        parts = (rows[p : p + 1, :128], rows[p : p + 1, 128:], rows[8 + p : 9 + p, :128], rows[8 + p : 9 + p, 128:])
        for i, part in enumerate(parts):
            tile = jnp.where(row_id == i, jnp.broadcast_to(part, (8, 128)), tile)
        out[r, 32:40, :] = tile


def tails(chunk, from_south, from_north):
    return call(
        tails_kernel,
        vds(G, 40, 128),
        [VM, VM, VM],
        VM,
        input_output_aliases={0: 0},
        name="tails",
    )(chunk, from_south, from_north)


def cmul(a, b, c, s):
    return a * c - b * s, a * s + b * c


def four(z):
    (ar, ai), (br, bi), (cr, ci), (dr, di) = z
    t0r, t0i, t1r, t1i = ar + cr, ai + ci, ar - cr, ai - ci
    t2r, t2i, t3r, t3i = br + dr, bi + di, br - dr, bi - di
    return (
        (t0r + t2r, t0i + t2i),
        (t1r - t3i, t1i + t3r),
        (t0r - t2r, t0i - t2i),
        (t1r + t3i, t1i - t3r),
    )


def sixteen(z):
    inner = [four([z[4 * g1 + g0] for g1 in range(4)]) for g0 in range(4)]
    out = [None] * 16
    for r0 in range(4):
        column = []
        for g0 in range(4):
            angle = 2 * math.pi * g0 * r0 / 16
            a, b = inner[g0][r0]
            column.append((a, b) if g0 * r0 == 0 else cmul(a, b, math.cos(angle), math.sin(angle)))
        for r1, value in enumerate(four(column)):
            out[4 * r1 + r0] = value
    return out


def inverse_kernel(recv, twc, tws, inv_high, inv_low, send_hbm, left_high, left_low, mid, send, sems):
    row_id = iota((8, 128), 0)
    lane_id = iota((8, 128), 1)

    def put(row, part, upper, lower):
        high, low = halves(jnp.concatenate([upper, lower], 0))
        left_high[row : row + 16, 128 * part : 128 * part + 128] = high
        left_low[row : row + 16, 128 * part : 128 * part + 128] = low

    for h in range(2):
        z = [(recv[g, 16 * h : 16 * h + 8, :], recv[g, 16 * h + 8 : 16 * h + 16, :]) for g in range(G)]
        turned = [cmul(a, b, twc[r, h : h + 1, :], tws[r, h : h + 1, :]) for r, (a, b) in enumerate(sixteen(z))]
        for r in range(0, G, 2):
            for i in range(2):
                put(8 * r, 2 * i + h, turned[r][i], turned[r + 1][i])
    z = []
    for g in range(G):
        tile = jnp.where(row_id < 4, recv[g, 32:40, :], 0.0)
        z.append((tile, roll(tile, -2, 0)))
    rows = [[jnp.zeros((8, 128), F32)] * 2 for _ in range(4)]
    for r, pair in enumerate(sixteen(z)):
        pair = cmul(*pair, twc[r], tws[r])
        for part in range(4):
            value = roll(pair[part // 2], r % 8 - part % 2, 0)
            rows[part][r // 8] = jnp.where(row_id == r % 8, value, rows[part][r // 8])
    for part in range(4):
        put(128, part, *rows[part])

    mid[...] = (
        mm(left_high[...], inv_high[...]) + mm(left_low[...], inv_high[...]) + mm(left_high[...], inv_low[...])
    )

    first, second, single = [], [], []
    for r in range(G):
        first.append(mid[8 * r : 8 * r + 8, 0:128])
        second.append(mid[8 * r : 8 * r + 8, 128:256])
        at = slice(128 + r // 8 * 8, 136 + r // 8 * 8)
        low, high = roll(mid[at, 0:128], -(r % 8), 0), roll(mid[at, 128:256], 1 - r % 8, 0)
        single.append(jnp.where(row_id == 0, low, high))
    for i in range(8):
        a, b = first[i], second[i]
        c, d = first[i + 8], second[i + 8]
        first[i], second[i], first[i + 8], second[i + 8] = a, c, b, d
        a, c = single[i], single[i + 8]
        single[i] = jnp.where(row_id == 0, a, roll(c, 1, 0))
        single[i + 8] = jnp.where(row_id == 0, roll(a, -1, 0), c)
    for bit in (4, 2, 1):
        upper = (lane_id // (16 * bit)) % 2 == 1
        for tiles in (first, second, single):
            for i in range(G):
                if i & bit:
                    continue
                a, b = tiles[i], tiles[i | bit]
                tiles[i] = jnp.where(upper, roll(b, 16 * bit, 1), a)
                tiles[i | bit] = jnp.where(upper, b, roll(a, -16 * bit, 1))

    left = [roll(second[d], 1, 1) for d in range(G)]
    right = [roll(first[d], 1, 1) for d in range(G)]
    side = [roll(single[d], 5, 1) for d in range(G)]
    stores = []
    for d in range(G):
        before, after = (d - 1) % G, (d + 1) % G
        own = jnp.where(lane_id == 0, left[before], jnp.where(lane_id == 1, right[after], 0.0))
        rim = own + roll(roll(own, -1, 0), 2, 1)
        base = jnp.where(row_id == 2, roll(single[d], 2, 0), 0.0)
        base = jnp.where(row_id == 6, roll(single[d], 5, 0), base)
        base = jnp.where((row_id == 3) & (lane_id == 4), roll(side[before], 2, 0), base)
        base = jnp.where((row_id == 3) & (lane_id == 5), roll(side[after], 3, 0), base)
        for g in range(4):
            tile = jnp.where(row_id < 2, roll(first[d], -2 * g, 0), base)
            tile = jnp.where((row_id == 4) | (row_id == 5), roll(second[d], 4 - 2 * g, 0), tile)
            tile = jnp.where((row_id == 3) & (lane_id < 4), roll(rim, 3 - 2 * g, 0), tile)
            send[g, d] = tile
        if d % 4 == 3:
            ds = slice(d - 3, d + 1)
            stores += fetch(((send.at[:, ds], send_hbm.at[:, ds]),), sems, d // 4)
    for store in stores:
        store.wait()


def inverse(recv, twc, tws, high, low):
    return call(
        inverse_kernel,
        hds(4, G, 8, 128),
        [VM] * 5,
        HB,
        scratch_shapes=[
            pltpu.VMEM((144, 512), BF16),
            pltpu.VMEM((144, 512), BF16),
            pltpu.VMEM((144, 256), F32),
            pltpu.VMEM((4, G, 8, 128), F32),
            pltpu.SemaphoreType.DMA((4,)),
        ],
        name="inverse",
    )(recv, twc, tws, high, low).reshape(64, 8, 128)


EARLY = ("ym", "yt", "edge", "ref", "rm", "cm")


def still_kernel(me, rate_hbm, sal_hbm, zlow_hbm, zhigh_hbm, edge_cols, from_south, from_north, *rest):
    count = len(EARLY)
    hbm, (base, parts_hbm), kept, rest = rest[:count], rest[count : count + 2], rest[count + 2 : 2 * count + 2], rest[2 * count + 2 :]
    rate, salinity, zlow, zhigh, parts, sems, const_sems, out_sems = rest
    copies = fetch(((rate_hbm, rate), (sal_hbm, salinity), (zlow_hbm, zlow), (zhigh_hbm, zhigh)), sems)
    stores = fetch(tuple(zip(hbm, kept)), const_sems)
    west_t = edge_cols[(me[0] + G - 1) % G, 32:40, :].T
    east_t = edge_cols[(me[0] + 1) % G, 32:40, :].T
    last_row = iota((8, FINE), 0) == 7
    first_row = iota((8, FINE), 0) == 0
    last_lane = iota((8, 128), 1) == 127
    first_lane = iota((8, 128), 1) == 0

    def outer(rows, l):
        line = jnp.concatenate([rows[16 + 8 * j + l : 17 + 8 * j + l, :] for j in range(4)], 1)
        return jnp.broadcast_to(line, (8, FINE))

    for copy in copies:
        copy.wait()
    for yb in range(8):
        ys = slice(8 * yb, 8 * yb + 8)
        for l in range(8):
            c = salinity[l, ys, :]
            upper = salinity[l + 1, ys, :] if l < 7 else zhigh[ys, :]
            lower = salinity[l - 1, ys, :] if l > 0 else zlow[ys, :]
            if yb < 7:
                north = salinity[l, 8 * yb + 1 : 8 * yb + 9, :]
            else:
                north = jnp.where(last_row, outer(from_north, l), roll(c, -1, 0))
            if yb > 0:
                south = salinity[l, 8 * yb - 1 : 8 * yb + 7, :]
            else:
                south = jnp.where(first_row, outer(from_south, l), roll(c, 1, 0))
            at = (l % 2) * 64 + 8 * yb
            ecol = jnp.broadcast_to(east_t[at : at + 8, 4 + l // 2 : 5 + l // 2], (8, 128))
            wcol = jnp.broadcast_to(west_t[at : at + 8, 4 + l // 2 : 5 + l // 2], (8, 128))
            e = roll(c, -1, 1)
            w = roll(c, 1, 1)
            e = jnp.concatenate([e[:, :-128], jnp.where(last_lane, ecol, e[:, -128:])], 1)
            w = jnp.concatenate([jnp.where(first_lane, wcol, w[:, :128]), w[:, 128:]], 1)
            k = rate[l] * 0.1
            base[l, ys, :] = c + k * (((e + w) + (north + south)) + (upper + lower) - 6.0 * c)
            parts[0, l, ys, :] = (e - w) * 0.05
            parts[1, l, ys, :] = (north - south) * 0.05
            parts[2, l, ys, :] = (upper - lower) * 0.05
        stores.append(pltpu.make_async_copy(parts.at[:, :, ys, :], parts_hbm.at[:, :, ys, :], out_sems.at[yb]))
        stores[-1].start()
    for store in stores:
        store.wait()


def still(me, rate, salinity, zlow, zhigh, recv1, from_south, from_north):
    consts = [jnp.asarray(tables()[name]) for name in EARLY]
    return call(
        still_kernel,
        [vds(8, 64, FINE), hds(3, 8, 64, FINE)] + [vds(*x.shape, dtype=x.dtype) for x in consts],
        [SM, HB, HB, HB, HB, VM, VM, VM] + [HB] * len(consts),
        [VM, HB] + [VM] * len(consts),
        scratch_shapes=[
            pltpu.SMEM((8,), F32),
            pltpu.VMEM((8, 64, FINE), F32),
            pltpu.VMEM((64, FINE), F32),
            pltpu.VMEM((64, FINE), F32),
            pltpu.VMEM((3, 8, 64, FINE), F32),
            pltpu.SemaphoreType.DMA((4,)),
            pltpu.SemaphoreType.DMA((len(consts),)),
            pltpu.SemaphoreType.DMA((8,)),
        ],
        limit=24,
        name="still",
    )(me, rate, salinity, zlow, zhigh, recv1, from_south, from_north, *consts)


def fine_kernel(
    grp_ref,
    base,
    parts_hbm,
    recv,
    ym,
    yt,
    edge,
    ref,
    rm,
    cm,
    out,
    spread,
    y_high,
    y_low,
    side_high,
    side_low,
    vel,
    total,
    parts,
    in_sems,
):
    rows = [slice(8 * yb, 8 * yb + 8) for yb in range(8)]
    loads = fetch([(parts_hbm.at[:, :, ys, :], parts.at[:, :, ys, :]) for ys in rows], in_sems)
    grp = grp_ref[0]
    row_id = iota((8, 128), 0)
    lane_id = iota((8, 128), 1)

    def lines(f, q):
        main = [recv[pl.ds(f * 128 + i, 16, stride=8), :] for i in (q, 4 + q, 3)]
        south = recv[pl.ds(pl.multiple_of((f * 16 + 2 * grp + q) * 8, 8), 8), :]
        north = recv[pl.ds(pl.multiple_of((f * 16 + 8 + 2 * grp + q) * 8, 8), 8), :]
        parts = []
        for x, row in zip(main, (2, 6, 3)):
            s, n = roll(south, -row, 0), roll(north, 1 - row, 0)
            if row == 3:
                x, s, n = roll(x, -2 * q, 1), roll(s, -4, 1), roll(n, -4, 1)
            tile = jnp.where(row_id == 0, s, jnp.where(row_id == 1, n, 0.0))
            parts.append(jnp.concatenate([x, tile, jnp.zeros((8, 128), F32)], 0))
        return jnp.concatenate(parts, 1)

    def along_y(table, f, q):
        high, low = halves(lines(f, q))
        return mm(table[...], jnp.concatenate([high, low], 0))

    for f in range(4):
        for q in range(2):
            at = slice(64 * (2 * f + q), 64 * (2 * f + q) + 64) if f < 3 else slice(384 + 16 * q, 400 + 16 * q)
            high, low = halves(along_y(ym if f < 3 else yt, f, q))
            y_high[at, :], side_high[at, :] = high[:, :256], high[:, 256:]
            y_low[at, :], side_low[at, :] = low[:, :256], low[:, 256:]
    vel[...] = mm(y_high[...], ref[...]) + mm(y_low[...], ref[...])
    side = mm(side_high[...], edge[...]) + mm(side_low[...], edge[...])
    vel[:, :128] += side[:, :128]
    vel[:, FINE - 128 :] += side[:, 128:]

    for yb in range(8):
        ys = rows[yb]
        loads[yb].wait()
        for q in range(2):
            vx, vy, vz = (vel[64 * (2 * f + q) + 8 * yb : 64 * (2 * f + q) + 8 * yb + 8, :] for f in range(3))
            acc = None
            for l in range(4 * q, 4 * q + 4):
                new = base[l, ys, :] - (vx * parts[0, l, ys, :] + vy * parts[1, l, ys, :] + vz * parts[2, l, ys, :])
                out[l, ys, :] = new
                acc = new if acc is None else acc + new
            total[64 * q + 8 * yb : 64 * q + 8 * yb + 8, :] = acc
    high, low = halves(total[...])
    high, low = halves(vel[384:416, :] - mm(rm[...], jnp.concatenate([high, low], 0)))
    means = [mm(high[:, at], cm[...]) + mm(low[:, at], cm[...]) for at in (slice(0, 512), slice(512, FINE))]
    mean = jnp.concatenate(means, 1)
    for a in range(G):
        spread[a] = mean


def fine(grp, base, parts, recv2, consts):
    return call(
        fine_kernel,
        (vds(8, 64, FINE), vds(G, 32, 256)),
        [SM, VM, HB, VM] + [VM] * len(consts),
        [VM, VM],
        input_output_aliases={1: 0},
        scratch_shapes=[
            pltpu.VMEM((416, 256), BF16),
            pltpu.VMEM((416, 256), BF16),
            pltpu.VMEM((416, 128), BF16),
            pltpu.VMEM((416, 128), BF16),
            pltpu.VMEM((416, FINE), F32),
            pltpu.VMEM((128, FINE), F32),
            pltpu.VMEM((3, 8, 64, FINE), F32),
            pltpu.SemaphoreType.DMA((8,)),
        ],
        limit=20,
        name="fine",
    )(grp, base, parts, recv2.reshape(512, 128), *consts)


def stage_kernel(me, inner_hbm, outer_hbm, *rest):
    count = (len(rest) - 8) // 2
    hbm, dst, rest = rest[:count], rest[count : 2 * count], rest[2 * count :]
    high_hbm, low_hbm, high, low, inner, outer, sems, out_sems = rest
    copies = fetch(((inner_hbm, inner), (outer_hbm, outer)) + tuple(zip(hbm, dst)), sems)
    turns = (iota((16, 128), 0) * me[0]) % G
    angle = turns.astype(F32) * (2.0 * math.pi / G)
    cos = jnp.concatenate([jnp.cos(angle)] * 2, 1)
    sin = -jnp.concatenate([jnp.sin(angle)] * 2, 1)
    copies[0].wait()
    copies[1].wait()
    real, imag = cmul(inner[:, :256], inner[:, 256:], cos, sin)
    for t in range(G):
        rows = slice(16 * t, 16 * t + 16)
        value = cmul(real, imag, outer[t : t + 1, :256], outer[t : t + 1, 256:])
        for at in range(2):
            high[rows, 256 * at : 256 * at + 256], low[rows, 256 * at : 256 * at + 256] = halves(value[at])
    for copy in copies[2:] + fetch(((high, high_hbm), (low, low_hbm)), out_sems):
        copy.wait()


def stage(me):
    t = tables()
    consts = [jnp.asarray(x) for x in (*t["tw"], *t["inv"])]
    out = call(
        stage_kernel,
        [vds(*x.shape, dtype=x.dtype) for x in consts] + [hds(256, 512, dtype=BF16)] * 2,
        [SM, HB, HB] + [HB] * len(consts),
        [VM] * len(consts) + [HB] * 2,
        scratch_shapes=[
            pltpu.VMEM((256, 512), BF16),
            pltpu.VMEM((256, 512), BF16),
            pltpu.VMEM((G, 512), F32),
            pltpu.VMEM((G, 512), F32),
            pltpu.SemaphoreType.DMA((len(consts) + 2,)),
            pltpu.SemaphoreType.DMA((2,)),
        ],
        name="stage",
    )(me, *map(jnp.asarray, t["fwd"]), *consts)
    return out[0:4], out[4:6]


def forward_kernel(recv, table_high, table_low, out, left_high, left_low, mid):
    turns = (iota((G, 128), 0) * iota((G, 128), 1)) % G
    angle = turns.astype(F32) * (2.0 * math.pi / G)
    comb_cos = jnp.concatenate([jnp.cos(angle)] * 2, 1)
    comb_sin = jnp.concatenate([jnp.sin(angle)] * 2, 1)
    for a in range(G):
        high, low = halves(recv[a])
        left_high[32 * a : 32 * a + 32, :] = high
        left_low[32 * a : 32 * a + 32, :] = low
    mid[...] = (
        mm(left_high[...], table_high[...]) + mm(left_low[...], table_high[...]) + mm(left_high[...], table_low[...])
    )
    real = imag = jnp.zeros((32, 256), F32)
    for a in range(G):
        c, s = comb_cos[a : a + 1, :], comb_sin[a : a + 1, :]
        x, y = mid[32 * a : 32 * a + 32, :256], mid[32 * a : 32 * a + 32, 256:]
        real = real + (x * c + y * s)
        imag = imag + (y * c - x * s)
    for g in range(4):
        out[g, 0:32, :] = real
        out[g, 32:64, :] = imag


def forward(recv, high, low):
    return call(
        forward_kernel,
        sds(4, 64, 256),
        [VM, VM, VM],
        VM,
        scratch_shapes=[
            pltpu.VMEM((512, 256), BF16),
            pltpu.VMEM((512, 256), BF16),
            pltpu.VMEM((512, 512), F32),
        ],
        name="forward",
    )(recv, high, low)


def finish_kernel(me, viscosity, gain, recv, modes, out):
    index = me[0] * W + iota((8, W), 1)
    number = jnp.where(index < NV // 2, index, index - NV).astype(F32)
    wave = (2.0 * math.pi / NV) * number
    damping = jnp.exp(-viscosity[0] * wave * wave)[0:1, :]
    for c in range(2):
        for g in range(4):
            at = slice(128 * c + 32 * g, 128 * c + 32 * g + 32)
            out[at, :] = damping * modes[at, :] + gain[0] * recv[g, 32 * c : 32 * c + 32, :]


def finish(me, viscosity, gain, recv, modes):
    return call(finish_kernel, sds(256, W), [SM, SM, SM, VM, VM], VM, name="finish")(
        me, viscosity, gain, recv, modes
    )


def shifted(array, axis, step):
    count = lax.axis_size(axis)
    return lax.ppermute(array, axis, [(i, (i + step) % count) for i in range(count)])


def per_device(coarse_modes, salinity, viscosity, forcing_gain, diffusivity):
    me = lax.axis_index(GX).astype(jnp.int32).reshape(1)
    grp = lax.axis_index("grp").astype(jnp.int32).reshape(1)
    modes = coarse_modes.reshape(256, 256)
    up, down, low_face, high_face = outer_lines(modes, salinity)
    from_south = shifted(up, "gy", 1)
    from_north = shifted(down, "gy", -1)
    zlow = shifted(high_face, "grp", 1)
    zhigh = shifted(low_face, "grp", -1)
    chunk, inv, weights = pack(me, modes, salinity), *stage(me)
    chunk, from_south, from_north, zlow, zhigh, inv, weights = lax.optimization_barrier(
        (chunk, from_south, from_north, zlow, zhigh, inv, weights)
    )
    chunk = tails(chunk, from_south, from_north)
    recv1 = lax.all_to_all(chunk, GX, 0, 0, tiled=True)
    send2 = inverse(recv1, *inv)
    recv2 = lax.all_to_all(send2, GRP_GX, 0, 0, tiled=True)
    base, parts, *consts = still(me, diffusivity, salinity, zlow, zhigh, recv1, from_south, from_north)
    salinity_next, spread = fine(grp, base, parts, recv2, consts)
    recv3 = lax.all_to_all(spread, GX, 0, 0, tiled=True)
    recv4 = lax.all_to_all(forward(recv3, *weights), "grp", 0, 0, tiled=True)
    coarse_next = finish(me, viscosity, forcing_gain, recv4, modes)
    return (salinity_next, coarse_next.reshape(coarse_modes.shape))


def solution(mesh):
    finer = Mesh(
        mesh.devices.reshape(mesh.shape["grp"], 2, 8, mesh.shape["gy"]),
        ("grp", "gx_0", "gx_1", "gy"),
    )
    in_specs = (P("grp", None, None, "gy", GX), P("grp", "gy", GX), P("grp"), P("grp"), P("grp"))
    out_specs = (P("grp", "gy", GX), P("grp", None, None, "gy", GX))
    return jax.shard_map(
        per_device, mesh=finer, in_specs=in_specs, out_specs=out_specs, check_vma=False
    )
```
